256 devices in a mesh: dp: 8 (over y, z_lo), fsdp: 32 (over x, z_hi, core).
Axes of the slice: x: 4, y: 4, z: 8 (z_hi: 4, z_lo: 2; z = z_hi * 2 + z_lo), core: 2. Of those that a mesh axis runs over, the one named last changes fastest.
Arguments:
- queries: bfloat16 [49152, 2560], P(('dp', 'fsdp')), may hold values from -8 to 8
- keys: bfloat16 [49152, 2560], P(('dp', 'fsdp')), may hold values from -8 to 8
- values: bfloat16 [49152, 2560], P(('dp', 'fsdp')), may hold values from -6 to 6
- lengths: int32 [32, 8, 4], P('fsdp'), may hold values from 0 to 192, as said below
- normalized_weight: bfloat16 [2560, 5120], P(None, 'fsdp'), may hold values from -1 to 1
- block_scale_codes: int32 [40, 5120], P(None, 'fsdp'), may hold values from 0 to 255
- scale_group_factor: float32 [5, 5120], P(None, 'fsdp'), may hold values from 0.01 to 0.03
- scale_group_offset: float32 [5, 5120], P(None, 'fsdp'), may hold values from 0.005 to 0.015
- adapter_down_weight: bfloat16 [64, 2560], P(None, 'fsdp'), may hold values from -0.125 to 0.125
- adapter_up_weight: bfloat16 [64, 5120], P(None, 'fsdp'), may hold values from -0.75 to 0.75
- cotangent: bfloat16 [49152, 5120], P(('dp', 'fsdp')), may hold values from -24 to 24
Outputs:
- projection_output: bfloat16 [49152, 5120], P(('dp', 'fsdp'))
- attention_gradient: bfloat16 [49152, 2560], P(('dp', 'fsdp'))
- down_grad: float32 [64, 2560], P(None, 'fsdp')
- adapter_up_gradient: float32 [64, 5120], P(None, 'fsdp')
The draws below stay inside these ranges and needn't reach their ends.
Inputs may be any that keep to these rules, and one draw needn't show every extreme that they name: The 4 lengths of each block sum to 192; zero lengths, if any, come last; some block is a single document of 192 tokens.
All inputs are finite; a program needn't handle non-finite values.
Results may differ from the reference program's by a relative error of at most 0.0059.
Values may be sent and summed in bfloat16 or wider, within the bound.
No kernel may reach another device: no remote copies, remote signals or barrier semaphores. Data moves between devices by JAX's collectives and lax.ppermute only.
A program may use at most 192 MiB of HBM per device.

```python
import math
import jax
import jax.numpy as jnp
from jax import lax

MODEL_WIDTH = 5120
HEADS = 20
HEAD_SIZE = 128
ADAPTER_RANK = 64
QBLOCK = 64
SCALE_GROUP = 8
DOCS = 4
TOK_DEV = 192
HEAD_FEATURES = 2560
TOKENS = 49152
N_DP = 8
N_FSDP = 32


def draw_queries(key, part):
    noise = jax.random.normal(jax.random.fold_in(key, 11), (TOKENS, HEADS, HEAD_SIZE), jnp.float32)
    result = jnp.clip(noise, -6.0, 6.0)
    return result.reshape(TOKENS, HEAD_FEATURES).astype(jnp.bfloat16)


def draw_keys(key, part):
    noise = jax.random.normal(jax.random.fold_in(key, 12), (TOKENS, HEADS, HEAD_SIZE), jnp.float32)
    result = jnp.clip(noise, -6.0, 6.0)
    return result.reshape(TOKENS, HEAD_FEATURES).astype(jnp.bfloat16)


def draw_lengths(key, part):
    blocks = N_FSDP * N_DP
    doc_count = jax.random.randint(jax.random.fold_in(key, 21), (blocks,), 1, DOCS + 1)
    single = jax.random.randint(jax.random.fold_in(key, 22), (), 0, blocks)
    doc_count = jnp.where(jnp.arange(blocks) == single, 1, doc_count)
    scores = jax.random.randint(jax.random.fold_in(key, 23), (blocks, TOK_DEV - 1), 0, 2 ** 20) * TOK_DEV + jnp.arange(1, TOK_DEV, dtype=jnp.int32)[None, :]
    order = jnp.argsort(scores, axis=-1)
    picks = order[:, :DOCS - 1].astype(jnp.int32) + 1
    usable = jnp.arange(DOCS - 1, dtype=jnp.int32)[None, :] < doc_count[:, None] - 1
    cuts = jnp.sort(jnp.where(usable, picks, TOK_DEV), axis=-1)
    edges = jnp.concatenate([jnp.zeros((blocks, 1), jnp.int32), cuts.astype(jnp.int32), jnp.full((blocks, 1), TOK_DEV, jnp.int32)], axis=1)
    doc_lengths = edges[:, 1:] - edges[:, :-1]
    return doc_lengths.reshape(N_FSDP, N_DP, DOCS).astype(jnp.int32)


def set_ends(values, stream_key, least, largest):
    dims = values.shape
    place = [jax.random.randint(jax.random.fold_in(stream_key, axis), (), 0, dims[axis]) for axis in range(len(dims))]
    values = values.at[tuple(place)].set(least)
    longest = dims.index(max(dims))
    place[longest] = (place[longest] + 1) % dims[longest]
    return values.at[tuple(place)].set(largest)


def strengthened(entries, key, source, target, shards_of, factor):
    owner, partner = [(jnp.arange(entries.shape[dim]) // (entries.shape[dim] // shards_of)).reshape([-1 if axis == dim else 1 for axis in range(entries.ndim)]) for dim in (source, target)]
    chosen = jax.random.permutation(key, shards_of)[partner]
    strong = (owner == chosen) | (owner == (partner + shards_of // 2) % shards_of)
    return jnp.where(strong, factor * entries, entries)


def shard_levels(key, shape, split, smallest, largest):
    level = 1.0
    for dim, blocks in split:
        heights = jax.random.uniform(jax.random.fold_in(jax.random.fold_in(key, 6), dim), (blocks,), jnp.float32, smallest / len(split), largest / len(split))
        level = level * jnp.repeat(jnp.exp(heights), shape[dim] // blocks).reshape((-1,) + (1,) * (len(shape) - 1 - dim))
    return level


def scatter_about(own_key, shape, deviation, bound, split=(), kind=jnp.bfloat16):
    level = shard_levels(own_key, shape, split, -0.22, 0.18) if split else 1.0
    drawn = jax.random.normal(own_key, shape, jnp.float32) * deviation * level
    return jnp.minimum(jnp.maximum(drawn, -bound), bound).astype(kind)


def bell_draw_with(rng, extent, width, most, cuts, heavy, kind=jnp.bfloat16):
    array = width * jax.random.normal(rng, extent, jnp.float32)
    if cuts:
        array = array * shard_levels(rng, extent, cuts, -0.22, 0.18)
    return jnp.clip(strengthened(array, jax.random.fold_in(rng, 3), *heavy), -most, most).astype(kind)


def setup_inputs(seed: int = 0) -> dict:
    key_list = jax.random.split(jax.random.key(seed), 12)
    return {
        "queries": draw_queries(jax.random.fold_in(key_list[11], 71), 0),
        "keys": draw_keys(jax.random.fold_in(key_list[11], 71), 0),
        "values": scatter_about(key_list[2], (TOKENS, HEAD_FEATURES), 1.0, 6.0, ((0, 256),)),
        "lengths": draw_lengths(jax.random.fold_in(key_list[11], 71), 0),
        "normalized_weight": jnp.clip(jax.random.uniform(key_list[4], (HEAD_FEATURES, MODEL_WIDTH), jnp.float32, -1.0, 1.0) * shard_levels(key_list[4], (HEAD_FEATURES, MODEL_WIDTH), ((1, 32),), -0.4, 0.0), -1.0, 1.0).astype(jnp.bfloat16),
        "block_scale_codes": set_ends(jax.random.randint(key_list[5], (HEAD_FEATURES // QBLOCK, MODEL_WIDTH), 0, 256), jax.random.fold_in(key_list[5], 1), 0, 255).astype(jnp.int32),
        "scale_group_factor": jnp.clip(jnp.exp(math.log(0.03) - 1.0986123 * jax.random.uniform(key_list[6], (HEAD_FEATURES // (QBLOCK * SCALE_GROUP), MODEL_WIDTH), jnp.float32) ** shard_levels(key_list[6], (HEAD_FEATURES // (QBLOCK * SCALE_GROUP), MODEL_WIDTH), ((1, 32),), -0.2, 0.2)), 0.01, 0.03),
        "scale_group_offset": jnp.clip(jnp.exp(math.log(0.015) - 1.0986123 * jax.random.uniform(key_list[7], (HEAD_FEATURES // (QBLOCK * SCALE_GROUP), MODEL_WIDTH), jnp.float32) ** shard_levels(key_list[7], (HEAD_FEATURES // (QBLOCK * SCALE_GROUP), MODEL_WIDTH), ((1, 32),), -0.2, 0.2)), 0.005, 0.015),
        "adapter_down_weight": scatter_about(key_list[8], (ADAPTER_RANK, HEAD_FEATURES), HEAD_FEATURES ** -0.5, 0.125, ((1, 32),)),
        "adapter_up_weight": scatter_about(key_list[9], (ADAPTER_RANK, MODEL_WIDTH), ADAPTER_RANK ** -0.5, 0.75, ((1, 32),)),
        "cotangent": bell_draw_with(key_list[10], (TOKENS, MODEL_WIDTH), 1.0, 24.0, ((0, 256),), (0, 1, 256, 6.0)),
    }


adapter_scale = 0.25


def dequantize(normalized_weight, block_scale_codes, scale_group_factor, scale_group_offset):
    spread_scale = jnp.repeat(scale_group_factor, SCALE_GROUP, axis=0)
    spread_offset = jnp.repeat(scale_group_offset, SCALE_GROUP, axis=0)
    absmax = spread_scale * (block_scale_codes.astype(jnp.float32) + 1.0) / 256.0 + spread_offset
    return (normalized_weight.astype(jnp.float32) * jnp.repeat(absmax, QBLOCK, axis=0)).astype(jnp.bfloat16)


def attend_block(operands):
    queries, keys, values, doc_lengths = operands
    doc_ends = jnp.cumsum(doc_lengths)
    places = jnp.arange(TOK_DEV, dtype=jnp.int32)
    segment = jnp.sum((doc_ends[None, :] <= places[:, None]).astype(jnp.int32), axis=1)
    allowed = (segment[:, None] == segment[None, :]) & (places[None, :] <= places[:, None])
    query_heads = queries.reshape(TOK_DEV, HEADS, HEAD_SIZE).astype(jnp.float32)
    key_heads = keys.reshape(TOK_DEV, HEADS, HEAD_SIZE).astype(jnp.float32)
    value_heads = values.reshape(TOK_DEV, HEADS, HEAD_SIZE).astype(jnp.float32)
    scores = jnp.einsum("qhe,khe->hqk", query_heads, key_heads) * (HEAD_SIZE ** -0.5)
    scores = jnp.where(allowed[None], scores, -jnp.inf)
    row_max = jnp.max(scores, axis=-1, keepdims=True)
    weights = jnp.exp(scores - row_max)
    total = jnp.sum(weights, axis=-1)
    rounded = lax.optimization_barrier(weights.astype(jnp.bfloat16)).astype(jnp.float32)
    mixed = jnp.einsum("hqk,khe->qhe", rounded, value_heads) / jnp.transpose(total)[:, :, None]
    return mixed.astype(jnp.bfloat16).reshape(TOK_DEV, HEAD_FEATURES)


def reference(queries, keys, values, lengths, normalized_weight, block_scale_codes, scale_group_factor, scale_group_offset, adapter_down_weight, adapter_up_weight, cotangent):
    blocks = N_DP * N_FSDP
    block_lengths = jnp.transpose(lengths, (1, 0, 2)).reshape(blocks, DOCS)
    attention_output = lax.map(attend_block, (queries.reshape(blocks, TOK_DEV, HEAD_FEATURES), keys.reshape(blocks, TOK_DEV, HEAD_FEATURES), values.reshape(blocks, TOK_DEV, HEAD_FEATURES), block_lengths))
    attention_output = attention_output.reshape(TOKENS, HEAD_FEATURES)
    frozen_output = dequantize(normalized_weight, block_scale_codes, scale_group_factor, scale_group_offset)
    reduced_activation = jnp.dot(attention_output, adapter_down_weight.T, preferred_element_type=jnp.float32).astype(jnp.bfloat16)
    projection_output = (jnp.dot(attention_output, frozen_output, preferred_element_type=jnp.float32) + adapter_scale * jnp.dot(reduced_activation, adapter_up_weight, preferred_element_type=jnp.float32)).astype(jnp.bfloat16)
    reduced_gradient = (adapter_scale * jnp.dot(cotangent, adapter_up_weight.T, preferred_element_type=jnp.float32)).astype(jnp.bfloat16)
    attention_gradient = (jnp.dot(cotangent, frozen_output.T, preferred_element_type=jnp.float32) + jnp.dot(reduced_gradient, adapter_down_weight, preferred_element_type=jnp.float32)).astype(jnp.bfloat16)
    down_grad = jnp.dot(reduced_gradient.T, attention_output, preferred_element_type=jnp.float32)
    adapter_up_gradient = adapter_scale * jnp.dot(reduced_activation.T, cotangent, preferred_element_type=jnp.float32)
    return projection_output, attention_gradient, down_grad, adapter_up_gradient
```

```python
import jax
import jax.numpy as jnp
import numpy as np
from jax import lax
from jax.experimental import pallas as pl
from jax.experimental.pallas import tpu as pltpu
from jax.sharding import Mesh
from jax.sharding import PartitionSpec as P

HEAD = 128
TOK = 192
BLK = 640
COLS = 160
DCOLS = 80
SCALE = 0.25
AX = ("y", "zl", "x", "zh", "c")
DIMS = (4, 2, 4, 4, 2)
REL = (0, -1, 1, 2)
bf16 = jnp.bfloat16
f32 = jnp.float32

T_Y, T_D, T_S, T_F, T_J1, T_I1, T_J2, T_I2, T_J3, T_I3 = 0, 1, 2, 6, 40, 48, 56, 72, 88, 96
T_LEN = 104


def params(mib=48):
    return pltpu.CompilerParams(vmem_limit_bytes=mib << 20)


def coords():
    return [np.unravel_index(d, DIMS) for d in range(256)]


def device_table():
    rows = np.zeros((256, T_LEN), np.int32)
    for n, (y, zl, x, zh, c) in enumerate(coords()):
        r = rows[n]
        r[T_Y], r[T_D] = y, y * 2 + zl
        for k in range(4):
            r[T_S + k] = (zh - k) % 4
        for f in range(32):
            fx, fz, fc = f // 8, (f // 2) % 4, f % 2
            r[T_F + f] = (fc ^ c) * 16 + (fz ^ zh) * 4 + (fx ^ x)

        def tiles(own, v, us):
            kind = c if own else 1 - c
            if kind == 0:
                return [(2 * ((x + u) % 4), (y + v) % 4) for u in us]
            return [(2 * ((x + v) % 4) + 1, (y + u) % 4) for u in us]

        stage1 = tiles(True, 0, REL) + tiles(False, 0, REL)
        stage2 = tiles(True, -1, REL) + tiles(True, 1, REL) + tiles(False, -1, REL) + tiles(False, 1, REL)
        stage3 = tiles(True, 2, REL) + tiles(False, 2, REL)
        for at_j, at_i, stage in ((T_J1, T_I1, stage1), (T_J2, T_I2, stage2), (T_J3, T_I3, stage3)):
            for k, (j, i) in enumerate(stage):
                r[at_j + k], r[at_i + k] = j, i
    return rows


def index_of(y, zl, x, zh, c):
    return int(np.ravel_multi_index((y % 4, zl, x % 4, zh % 4, c), DIMS))


def send(value, target):
    pairs = [(n, index_of(*target(*(int(v) for v in at)))) for n, at in enumerate(coords())]
    return lax.ppermute(value, AX, pairs)


def z_round(value, k):
    return send(value, lambda y, zl, x, zh, c: (y, zl, x, 2 * (zh % 2) + c + k, zh // 2))


def middle(value, k):
    return send(value, lambda y, zl, x, zh, c: (y, zl, x + k, zh, c) if c == 0 else (y + k, zl, x, zh, c))


def outer(value, k):
    return send(value, lambda y, zl, x, zh, c: (y + k, zl, x, zh, c) if c == 0 else (y, zl, x + k, zh, c))


def sibling(value):
    return send(value, lambda y, zl, x, zh, c: (y, zl, x, zh, 1 - c))


def flip(value, axis, bit):
    at = AX.index(axis)

    def target(*place):
        place = list(place)
        place[at] ^= bit
        return place

    return send(value, target)


def nt(a, b):
    return lax.dot_general(a, b, (((1,), (1,)), ((), ())), preferred_element_type=f32)


def nn(a, b):
    return lax.dot_general(a, b, (((1,), (0,)), ((), ())), preferred_element_type=f32)


def tn(a, b):
    return lax.dot_general(a, b, (((0,), (0,)), ((), ())), preferred_element_type=f32)


def eye(n):
    rows = lax.broadcasted_iota(jnp.int32, (n, n), 0)
    cols = lax.broadcasted_iota(jnp.int32, (n, n), 1)
    return jnp.where(rows == cols, 1.0, 0.0).astype(bf16)


def base_body(tab, weight, codes, factor, offset, out):
    y = tab[T_Y]
    parts = []
    for k in range(10):
        b = y * 10 + k
        code = codes[pl.ds(b, 1), :].astype(f32)
        group = b // 8
        absmax = factor[pl.ds(group, 1), :] * (code + 1.0) / 256.0 + offset[pl.ds(group, 1), :]
        parts.append((weight[k * 64 : (k + 1) * 64, :].astype(f32) * absmax).astype(bf16))
    out[...] = nt(eye(COLS), jnp.concatenate(parts, 0)).astype(bf16)


def base_quarter(tab, weight, codes, factor, offset):
    whole = lambda i, tab: (0, 0)
    return pl.pallas_call(
        base_body,
        out_shape=jax.ShapeDtypeStruct((COLS, BLK), bf16),
        grid_spec=pltpu.PrefetchScalarGridSpec(
            num_scalar_prefetch=1,
            grid=(1,),
            in_specs=[
                pl.BlockSpec((BLK, COLS), lambda i, tab: (tab[T_Y], 0)),
                pl.BlockSpec((40, COLS), whole),
                pl.BlockSpec((5, COLS), whole),
                pl.BlockSpec((5, COLS), whole),
            ],
            out_specs=pl.BlockSpec((COLS, BLK), whole),
        ),
        compiler_params=params(),
        name="base_quarter",
    )(tab, weight, codes, factor, offset)


def order_body(tab, a, b, c, d, out, sems):
    copies = [
        pltpu.make_async_copy(src, out.at[pl.ds(tab[T_S + k] * COLS, COLS), :], sems.at[k])
        for k, src in enumerate((a, b, c, d))
    ]
    for copy in copies:
        copy.start()
    for copy in copies:
        copy.wait()


def ordered(tab, blocks):
    anywhere = pl.BlockSpec(memory_space=pl.ANY)
    return pl.pallas_call(
        order_body,
        out_shape=jax.ShapeDtypeStruct((BLK, BLK), bf16),
        grid_spec=pltpu.PrefetchScalarGridSpec(
            num_scalar_prefetch=1,
            grid=(1,),
            in_specs=[anywhere] * 4,
            out_specs=anywhere,
            scratch_shapes=[pltpu.SemaphoreType.DMA((4,))],
        ),
        compiler_params=params(),
        name="ordered",
    )(tab, *blocks)


def attend_body(tab, lens, queries, keys, values, out):
    d = tab[T_D]
    rows = lax.broadcasted_iota(jnp.int32, (TOK, TOK), 0)
    cols = lax.broadcasted_iota(jnp.int32, (TOK, TOK), 1)
    end = jnp.int32(0)
    row_doc = jnp.zeros((TOK, TOK), jnp.int32)
    col_doc = jnp.zeros((TOK, TOK), jnp.int32)
    for k in range(4):
        end = end + lens[d * 4 + k]
        row_doc = row_doc + jnp.where(rows >= end, 1, 0)
        col_doc = col_doc + jnp.where(cols >= end, 1, 0)
    allowed = (row_doc == col_doc) & (cols <= rows)
    for h in range(BLK // HEAD):
        at = slice(h * HEAD, (h + 1) * HEAD)
        scores = nt(queries[:, at], keys[:, at]) * (HEAD ** -0.5)
        scores = jnp.where(allowed, scores, -1e30)
        weights = jnp.exp(scores - jnp.max(scores, axis=-1, keepdims=True))
        total = jnp.sum(weights, axis=-1, keepdims=True)
        out[:, at] = (nn(weights.astype(bf16), values[:, at]) / total).astype(bf16)


def attend(tab, lens, queries, keys, values):
    spec = pl.BlockSpec((TOK, BLK), lambda i, *_: (0, i))
    return pl.pallas_call(
        attend_body,
        out_shape=jax.ShapeDtypeStruct(queries.shape, bf16),
        grid_spec=pltpu.PrefetchScalarGridSpec(
            num_scalar_prefetch=2, grid=(4,), in_specs=[spec] * 3, out_specs=spec
        ),
        compiler_params=params(),
        name="attend",
    )(tab, lens, queries, keys, values)


def low_body(tab, att, cot, gathered, out, grad, keep, give, down_t, up_t):
    unit = eye(256)
    for f in range(32):
        block = gathered[tab[T_F + f]]
        turned = nt(unit, jnp.concatenate([block, block], 0)).astype(bf16)
        down_t[f * DCOLS : (f + 1) * DCOLS, :] = turned[:DCOLS]
        up_t[f * COLS : (f + 1) * COLS, :] = turned[DCOLS : DCOLS + COLS]
    low = jnp.zeros((TOK, 128), f32)
    for i in range(4):
        at = slice(i * BLK, (i + 1) * BLK)
        low = low + nn(att[:, at], down_t[at, :])
    low_grad = jnp.zeros((TOK, 128), f32)
    for j in range(8):
        at = slice(j * BLK, (j + 1) * BLK)
        low_grad = low_grad + nn(cot[:, at], up_t[at, :])
    first = lax.broadcasted_iota(jnp.int32, (TOK, 128), 1) < 64
    low_grad = low_grad * SCALE
    none = jnp.zeros((TOK, 128), f32)
    low_a, low_b = (jnp.where(first, low, none).astype(bf16), jnp.where(first, none, low).astype(bf16))
    lg_a, lg_b = (
        jnp.where(first, low_grad, none).astype(bf16),
        jnp.where(first, none, low_grad).astype(bf16),
    )

    def put(f, lo, hi, value):
        place = tab[T_F + f]

        @pl.when(place < 16)
        def _():
            keep[place, lo:hi, :] = value

        @pl.when(place >= 16)
        def _():
            give[place - 16, lo:hi, :] = value

    half = DCOLS // 2
    for i in range(4):
        at = slice(i * BLK, (i + 1) * BLK)
        grad[i] = nt(lg_a, down_t[at, :])
        a, b = tn(att[:, at], lg_a), tn(att[:, at], lg_b)
        for k in range(8):
            s = k * DCOLS
            put(i * 8 + k, 0, half, a[s : s + half] + b[s + half : s + DCOLS])
    for j in range(8):
        at = slice(j * BLK, (j + 1) * BLK)
        out[j] = nt(low_a, up_t[at, :]) * SCALE
        a, b = tn(cot[:, at], low_a), tn(cot[:, at], low_b)
        for k in range(4):
            s = k * COLS
            put(j * 4 + k, half, half + DCOLS, (a[s : s + DCOLS] + b[s + DCOLS : s + COLS]) * SCALE)


def low_terms(tab, att, cot, gathered):
    return pl.pallas_call(
        low_body,
        out_shape=(
            jax.ShapeDtypeStruct((8, TOK, BLK), f32),
            jax.ShapeDtypeStruct((4, TOK, BLK), f32),
            jax.ShapeDtypeStruct((16, 120, 128), f32),
            jax.ShapeDtypeStruct((16, 120, 128), f32),
        ),
        grid_spec=pltpu.PrefetchScalarGridSpec(
            num_scalar_prefetch=1,
            grid=(1,),
            in_specs=[
                pl.BlockSpec(att.shape, lambda i, tab: (0, 0)),
                pl.BlockSpec(cot.shape, lambda i, tab: (0, 0)),
                pl.BlockSpec(gathered.shape, lambda i, tab: (0, 0, 0)),
            ],
            out_specs=[
                pl.BlockSpec((8, TOK, BLK), lambda i, tab: (0, 0, 0)),
                pl.BlockSpec((4, TOK, BLK), lambda i, tab: (0, 0, 0)),
                pl.BlockSpec((16, 120, 128), lambda i, tab: (0, 0, 0)),
                pl.BlockSpec((16, 120, 128), lambda i, tab: (0, 0, 0)),
            ],
            scratch_shapes=[
                pltpu.VMEM((32 * DCOLS, 128), bf16),
                pltpu.VMEM((32 * COLS, 128), bf16),
            ],
        ),
        compiler_params=params(56),
        name="low_terms",
    )(tab, att, cot, gathered)


def tiles_body(last, starts, at_j, at_i, tab, att, cot, out_in, grad_in, *refs):
    count = len(starts)
    tiles, (out, grad), rest = refs[:count], refs[count : count + 2], refs[count + 2 :]
    if last:
        out_acc, grad_acc, sems = rest
    else:
        out_acc, grad_acc, sems = out, grad, rest[0]
    step = pl.program_id(0)

    @pl.when(step == 0)
    def _():
        first = pltpu.make_async_copy(out_in, out_acc, sems.at[0])
        second = pltpu.make_async_copy(grad_in, grad_acc, sems.at[1])
        first.start()
        second.start()
        first.wait()
        second.wait()

    j, i = tab[at_j + step], tab[at_i + step]
    for k, (start, tile) in enumerate(zip(starts, tiles)):
        @pl.when((step >= start) & (step < start + tile_count(starts, k)))
        def _():
            w = tile[0]
            out_acc[j] = out_acc[j] + nt(att[...], w)
            grad_acc[i] = grad_acc[i] + nn(cot[...], w)

    if last:
        @pl.when(step == pl.num_programs(0) - 1)
        def _():
            for k in range(8):
                out[:, k * BLK : (k + 1) * BLK] = out_acc[k].astype(bf16)
            for k in range(4):
                grad[:, k * BLK : (k + 1) * BLK] = grad_acc[k].astype(bf16)


def tile_count(starts, k):
    return starts.counts[k]


class Starts(tuple):
    counts = ()


def add_tiles(tab, att, cot, sums, arrays, at_j, at_i, last=False):
    counts = [a.shape[0] for a in arrays]
    starts = Starts(int(v) for v in np.cumsum([0] + counts[:-1]))
    starts.counts = tuple(counts)
    anywhere = pl.BlockSpec(memory_space=pl.ANY)

    def tile_spec(start, n):
        return pl.BlockSpec((1, BLK, BLK), lambda s, tab: (jnp.clip(s - start, 0, n - 1), 0, 0))

    acc = [(8, TOK, BLK), (4, TOK, BLK)]
    if last:
        outs = [jax.ShapeDtypeStruct((TOK, 8 * BLK), bf16), jax.ShapeDtypeStruct((TOK, 4 * BLK), bf16)]
        scratch = [pltpu.VMEM(s, f32) for s in acc]
    else:
        outs = [jax.ShapeDtypeStruct(s, f32) for s in acc]
        scratch = []
    return pl.pallas_call(
        lambda *refs: tiles_body(last, starts, at_j, at_i, *refs),
        out_shape=outs,
        grid_spec=pltpu.PrefetchScalarGridSpec(
            num_scalar_prefetch=1,
            grid=(sum(counts),),
            in_specs=[
                pl.BlockSpec((TOK, BLK), lambda s, tab: (0, tab[at_i + s])),
                pl.BlockSpec((TOK, BLK), lambda s, tab: (0, tab[at_j + s])),
                anywhere,
                anywhere,
                *(tile_spec(start, n) for start, n in zip(starts, counts)),
            ],
            out_specs=[pl.BlockSpec(o.shape, lambda s, tab, n=len(o.shape): (0,) * n) for o in outs],
            scratch_shapes=[*scratch, pltpu.SemaphoreType.DMA((2,))],
        ),
        compiler_params=params(56),
        name="tiles",
    )(tab, att, cot, *sums, *arrays)


def per_device(
    table,
    queries,
    keys,
    values,
    lengths,
    weight,
    codes,
    factor,
    offset,
    down,
    up,
    cot,
):
    tab = table.reshape(-1)
    lens = lengths.reshape(-1)

    quarter = base_quarter(tab, weight, codes, factor, offset)
    own_tile = ordered(tab, [z_round(quarter, k) for k in range(4)])

    adapters = jnp.concatenate([down, up, jnp.zeros((64, 16), bf16)], 1)[None]
    for axis, bit in (("x", 1), ("x", 2), ("zh", 1), ("zh", 2), ("c", 1)):
        adapters = jnp.concatenate([adapters, flip(adapters, axis, bit)], 0)

    att = attend(tab, lens, queries, keys, values)

    row = jnp.stack([own_tile, middle(own_tile, 1), middle(own_tile, -1), middle(own_tile, 2)])
    from_less, from_more = outer(row, 1), outer(row, -1)
    far_a, far_b = outer(from_less[:2], 1), outer(from_more[2:], -1)

    out0, grad0, keep, give = low_terms(tab, att, cot, adapters)
    part = keep + flip(give, "c", 1)
    for axis, bit, n in (("zh", 2, 8), ("zh", 1, 4), ("x", 2, 2), ("x", 1, 1)):
        part = part[:n] + flip(part[n:], axis, bit)
    part = part[0]
    for axis, bit in (("y", 1), ("y", 2), ("zl", 1)):
        part = part + flip(part, axis, bit)
    half = DCOLS // 2
    down_grad = jnp.concatenate([part[:half, :64], part[:half, 64:]], 0).T
    up_grad = jnp.concatenate([part[half:, :64], part[half:, 64:]], 0).T

    sums = add_tiles(tab, att, cot, (out0, grad0), [row, sibling(row)], T_J1, T_I1)
    sums = add_tiles(
        tab,
        att,
        cot,
        sums,
        [from_less, from_more, sibling(from_less), sibling(from_more)],
        T_J2,
        T_I2,
    )
    out, grad = add_tiles(
        tab, att, cot, sums, [far_a, far_b, sibling(far_a), sibling(far_b)], T_J3, T_I3, last=True
    )
    return out, grad, down_grad, up_grad


def solution(mesh):
    fine = Mesh(np.asarray(mesh.devices).reshape(DIMS), AX)
    tokens, owners = ("y", "zl", "x", "zh", "c"), ("x", "zh", "c")
    table = device_table()
    mapped = jax.shard_map(
        per_device,
        mesh=fine,
        in_specs=(
            P(tokens, None),
            P(tokens, None),
            P(tokens, None),
            P(tokens, None),
            P(owners, None, None),
            P(None, owners),
            P(None, owners),
            P(None, owners),
            P(None, owners),
            P(None, owners),
            P(None, owners),
            P(tokens, None),
        ),
        out_specs=(
            P(tokens, None),
            P(tokens, None),
            P(None, owners),
            P(None, owners),
        ),
        check_vma=False,
    )
    return lambda *args: mapped(jnp.asarray(table), *args)
```

```python
import jax
import jax.numpy as jnp
import numpy as np
from jax import lax
from jax.experimental import pallas as pl
from jax.experimental.pallas import tpu as pltpu
from jax.sharding import Mesh
from jax.sharding import PartitionSpec as P

HEAD = 128
TOK = 192
BLK = 640
COLS = 160
DCOLS = 80
SCALE = 0.25
AX = ("y", "zl", "x", "zh", "c")
DIMS = (4, 2, 4, 4, 2)
REL = (0, -1, 1, 2)
bf16 = jnp.bfloat16
f32 = jnp.float32

T_Y, T_D, T_S, T_F, T_C, T_J1, T_I1, T_J2, T_I2, T_J3, T_I3, T_P = 0, 1, 2, 6, 38, 40, 48, 56, 72, 88, 96, 104
T_LEN = 136


def params(mib=48):
    return pltpu.CompilerParams(vmem_limit_bytes=mib << 20)


def coords():
    return [np.unravel_index(d, DIMS) for d in range(256)]


def device_table():
    rows = np.zeros((256, T_LEN), np.int32)
    for n, (y, zl, x, zh, c) in enumerate(coords()):
        r = rows[n]
        r[T_Y], r[T_D], r[T_C] = y, y * 2 + zl, c
        for k in range(4):
            r[T_S + k] = (zh - k) % 4
        for f in range(32):
            fx, fz, fc = f // 8, (f // 2) % 4, f % 2
            r[T_F + f] = (fc ^ c) * 16 + (fx ^ x) * 4 + (fz ^ zh)
            dz = fz ^ zh
            r[T_P + f] = (dz % 2) * 8 + (dz // 2) * 4 + (fx ^ x)

        def tiles(own, v, us):
            kind = c if own else 1 - c
            if kind == 0:
                return [(2 * ((x + u) % 4), (y + v) % 4) for u in us]
            return [(2 * ((x + v) % 4) + 1, (y + u) % 4) for u in us]

        stage1 = tiles(True, 0, REL) + tiles(False, 0, REL)
        stage2 = tiles(True, -1, REL) + tiles(True, 1, REL) + tiles(False, -1, REL) + tiles(False, 1, REL)
        stage3 = tiles(True, 2, REL) + tiles(False, 2, REL)
        for at_j, at_i, stage in ((T_J1, T_I1, stage1), (T_J2, T_I2, stage2), (T_J3, T_I3, stage3)):
            for k, (j, i) in enumerate(stage):
                r[at_j + k], r[at_i + k] = j, i
    return rows


def index_of(y, zl, x, zh, c):
    return int(np.ravel_multi_index((y % 4, zl, x % 4, zh % 4, c), DIMS))


def send(value, target):
    pairs = [(n, index_of(*target(*(int(v) for v in at)))) for n, at in enumerate(coords())]
    return lax.ppermute(value, AX, pairs)


def z_round(value, k):
    return send(value, lambda y, zl, x, zh, c: (y, zl, x, 2 * (zh % 2) + c + k, zh // 2))


def middle(value, k):
    return send(value, lambda y, zl, x, zh, c: (y, zl, x + k, zh, c) if c == 0 else (y + k, zl, x, zh, c))


def outer(value, k):
    return send(value, lambda y, zl, x, zh, c: (y + k, zl, x, zh, c) if c == 0 else (y, zl, x + k, zh, c))


def sibling(value):
    return send(value, lambda y, zl, x, zh, c: (y, zl, x, zh, 1 - c))


def flip(value, axis, bit):
    at = AX.index(axis)

    def target(*place):
        place = list(place)
        place[at] ^= bit
        return place

    return send(value, target)


def nt(a, b):
    return lax.dot_general(a, b, (((1,), (1,)), ((), ())), preferred_element_type=f32)


def nn(a, b):
    return lax.dot_general(a, b, (((1,), (0,)), ((), ())), preferred_element_type=f32)


def tn(a, b):
    return lax.dot_general(a, b, (((0,), (0,)), ((), ())), preferred_element_type=f32)


def eye(n):
    rows = lax.broadcasted_iota(jnp.int32, (n, n), 0)
    cols = lax.broadcasted_iota(jnp.int32, (n, n), 1)
    return jnp.where(rows == cols, 1.0, 0.0).astype(bf16)


def base_body(tab, weight_t, codes, factor, offset, out, weight, code_v, factor_v, offset_v, sems):
    y = tab[T_Y]
    copies = [
        pltpu.make_async_copy(weight_t.at[:, pl.ds(pl.multiple_of(y * BLK, 128), BLK)], weight, sems.at[0]),
        pltpu.make_async_copy(codes, code_v, sems.at[1]),
        pltpu.make_async_copy(factor, factor_v, sems.at[2]),
        pltpu.make_async_copy(offset, offset_v, sems.at[3]),
    ]
    for copy in copies:
        copy.start()
    for copy in copies:
        copy.wait()
    rows = []
    for k in range(10):
        b = y * 10 + k
        code = code_v[pl.ds(b, 1), :].astype(f32)
        group = b // 8
        rows.append(factor_v[pl.ds(group, 1), :] * (code + 1.0) / 256.0 + offset_v[pl.ds(group, 1), :])
    rest = jnp.concatenate([*rows, jnp.zeros((6, COLS), f32)], 0)
    spread = lax.broadcasted_iota(jnp.int32, (16, BLK), 1) // 64
    spread = spread == lax.broadcasted_iota(jnp.int32, (16, BLK), 0)
    spread = jnp.where(spread, 1.0, 0.0).astype(bf16)
    absmax = jnp.zeros((COLS, BLK), f32)
    for _ in range(3):
        piece = rest.astype(bf16)
        rest = rest - piece.astype(f32)
        absmax = absmax + tn(piece, spread)
    out[...] = (weight[...].astype(f32) * absmax).astype(bf16)


def base_quarter(tab, weight, codes, factor, offset):
    hbm = pl.BlockSpec(memory_space=pltpu.HBM)
    return pl.pallas_call(
        base_body,
        out_shape=jax.ShapeDtypeStruct((COLS, BLK), bf16),
        in_specs=[pl.BlockSpec(memory_space=pltpu.SMEM), hbm, hbm, hbm, hbm],
        out_specs=pl.BlockSpec(memory_space=pltpu.VMEM),
        scratch_shapes=[
            pltpu.VMEM((COLS, BLK), bf16),
            pltpu.VMEM(codes.shape, jnp.int32),
            pltpu.VMEM(factor.shape, f32),
            pltpu.VMEM(offset.shape, f32),
            pltpu.SemaphoreType.DMA((4,)),
        ],
        compiler_params=params(16),
        name="base_quarter",
    )(tab, weight.T, codes, factor, offset)


def order_body(tab, a, b, c, d, out, sems):
    copies = [
        pltpu.make_async_copy(src, out.at[pl.ds(tab[T_S + k] * COLS, COLS), :], sems.at[k])
        for k, src in enumerate((a, b, c, d))
    ]
    for copy in copies:
        copy.start()
    for copy in copies:
        copy.wait()


def ordered(tab, blocks):
    anywhere = pl.BlockSpec(memory_space=pl.ANY)
    return pl.pallas_call(
        order_body,
        out_shape=jax.ShapeDtypeStruct((BLK, BLK), bf16),
        grid_spec=pltpu.PrefetchScalarGridSpec(
            num_scalar_prefetch=1,
            grid=(1,),
            in_specs=[anywhere] * 4,
            out_specs=anywhere,
            scratch_shapes=[pltpu.SemaphoreType.DMA((4,))],
        ),
        compiler_params=params(),
        name="ordered",
    )(tab, *blocks)


def attend_body(tab, lens, queries, keys, values, out):
    d = tab[T_D]
    rows = lax.broadcasted_iota(jnp.int32, (TOK, TOK), 0)
    cols = lax.broadcasted_iota(jnp.int32, (TOK, TOK), 1)
    end = jnp.int32(0)
    row_doc = jnp.zeros((TOK, TOK), jnp.int32)
    col_doc = jnp.zeros((TOK, TOK), jnp.int32)
    for k in range(4):
        end = end + lens[d * 4 + k]
        row_doc = row_doc + jnp.where(rows >= end, 1, 0)
        col_doc = col_doc + jnp.where(cols >= end, 1, 0)
    allowed = (row_doc == col_doc) & (cols <= rows)
    for h in range(BLK // HEAD):
        at = slice(h * HEAD, (h + 1) * HEAD)
        scores = nt(queries[:, at], keys[:, at]) * (HEAD ** -0.5)
        scores = jnp.where(allowed, scores, -1e30)
        weights = jnp.exp(scores - jnp.max(scores, axis=-1, keepdims=True))
        total = jnp.sum(weights, axis=-1, keepdims=True)
        out[:, at] = (nn(weights.astype(bf16), values[:, at]) / total).astype(bf16)


def attend(tab, lens, queries, keys, values):
    spec = pl.BlockSpec((TOK, BLK), lambda i, *_: (0, i))
    return pl.pallas_call(
        attend_body,
        out_shape=jax.ShapeDtypeStruct(queries.shape, bf16),
        grid_spec=pltpu.PrefetchScalarGridSpec(
            num_scalar_prefetch=2, grid=(4,), in_specs=[spec] * 3, out_specs=spec
        ),
        compiler_params=params(),
        name="attend",
    )(tab, lens, queries, keys, values)


def low_body(tab, att, cot, gathered, low_out, lg_out, down_t, up_t, keep, give):
    unit = eye(256)
    for f in range(32):
        block = gathered[tab[T_F + f]]
        turned = nt(unit, jnp.concatenate([block, block], 0)).astype(bf16)
        down_t[f * DCOLS : (f + 1) * DCOLS, :] = turned[:DCOLS]
        up_t[f * COLS : (f + 1) * COLS, :] = turned[DCOLS : DCOLS + COLS]
    low = nn(att[...], down_t[...])
    low_grad = nn(cot[...], up_t[...]) * SCALE
    first = lax.broadcasted_iota(jnp.int32, (TOK, 128), 1) < 64
    none = jnp.zeros((TOK, 128), f32)
    low_a, low_b = (jnp.where(first, low, none).astype(bf16), jnp.where(first, none, low).astype(bf16))
    lg_a, lg_b = (
        jnp.where(first, low_grad, none).astype(bf16),
        jnp.where(first, none, low_grad).astype(bf16),
    )
    low_out[...] = low_a
    lg_out[...] = lg_a
    core = tab[T_C]

    def put(f, lo, hi, even, odd):
        place = tab[T_P + f]
        keep[place, lo:hi, :] = jnp.where(core == 0, even, odd)
        give[place, lo:hi, :] = jnp.where(core == 0, odd, even)

    half = DCOLS // 2
    both = jnp.concatenate([lg_a, lg_b], 1)
    for i in range(4):
        got = tn(att[:, i * BLK : (i + 1) * BLK], both)
        a, b = got[:, :128], got[:, 128:]
        pair = []
        for k in range(8):
            s = k * DCOLS
            pair.append(a[s : s + half] + b[s + half : s + DCOLS])
        for k in range(0, 8, 2):
            put(i * 8 + k, 0, half, pair[k], pair[k + 1])
    both = jnp.concatenate([low_a, low_b], 1)
    for j in range(8):
        got = tn(cot[:, j * BLK : (j + 1) * BLK], both) * SCALE
        a, b = got[:, :128], got[:, 128:]
        pair = []
        for k in range(4):
            s = k * COLS
            pair.append(a[s : s + DCOLS] + b[s + DCOLS : s + COLS])
        for k in range(0, 4, 2):
            put(j * 4 + k, half, half + DCOLS, pair[k], pair[k + 1])


def low_terms(tab, att, cot, gathered):
    vmem = pl.BlockSpec(memory_space=pltpu.VMEM)
    return pl.pallas_call(
        low_body,
        out_shape=(
            jax.ShapeDtypeStruct((TOK, 128), bf16),
            jax.ShapeDtypeStruct((TOK, 128), bf16),
            jax.ShapeDtypeStruct((32 * DCOLS, 128), bf16),
            jax.ShapeDtypeStruct((32 * COLS, 128), bf16),
            jax.ShapeDtypeStruct((16, 120, 128), f32),
            jax.ShapeDtypeStruct((16, 120, 128), f32),
        ),
        in_specs=[pl.BlockSpec(memory_space=pltpu.SMEM), vmem, vmem, vmem],
        out_specs=[vmem] * 6,
        compiler_params=params(24),
        name="low_terms",
    )(tab, att, cot, gathered)


SLOTS = 4


def tiles_body(stage, counts, at_j, at_i, tab, att, cot, *refs):
    n_head = 4 if stage == 1 else 2
    head, refs = refs[:n_head], refs[n_head:]
    tiles, refs = refs[: len(counts)], refs[len(counts) :]
    out_acc, grad_acc, *refs = refs
    if stage == 3:
        out, grad, *refs = refs
    buf, sems, *refs = refs
    places = [(a, k) for a, n in enumerate(counts) for k in range(n)]

    def fetch(t):
        a, k = places[t]
        return pltpu.make_async_copy(tiles[a].at[k], buf.at[t % SLOTS], sems.at[t % SLOTS])

    for t in range(SLOTS):
        fetch(t).start()
    if stage == 1:
        low_a, lg_a, down_t, up_t = head
        for j in range(8):
            out_acc[j] = nt(low_a[...], up_t[j * BLK : (j + 1) * BLK, :]) * SCALE
        for i in range(4):
            grad_acc[i] = nt(lg_a[...], down_t[i * BLK : (i + 1) * BLK, :])
    for t in range(len(places)):
        j, i = tab[at_j + t], tab[at_i + t]
        fetch(t).wait()
        tile = buf[t % SLOTS]
        out_acc[j] = out_acc[j] + nt(att[:, pl.ds(pl.multiple_of(i * BLK, 128), BLK)], tile)
        grad_acc[i] = grad_acc[i] + nn(cot[:, pl.ds(pl.multiple_of(j * BLK, 128), BLK)], tile)
        if t + SLOTS < len(places):
            fetch(t + SLOTS).start()
    if stage == 3:
        out_v, grad_v, out_sems = refs
        copies = []
        for acc, full, ref, base in ((out_acc, out_v, out, 0), (grad_acc, grad_v, grad, 8)):
            for k in range(acc.shape[0]):
                at = slice(k * BLK, (k + 1) * BLK)
                full[:, at] = acc[k].astype(bf16)
                copies.append(pltpu.make_async_copy(full.at[:, at], ref.at[:, at], out_sems.at[base + k]))
                copies[-1].start()
        for copy in copies:
            copy.wait()


def add_tiles(stage, tab, att, cot, head, arrays, at_j, at_i):
    counts = [a.shape[0] for a in arrays]
    vmem = pl.BlockSpec(memory_space=pltpu.VMEM)
    hbm = pl.BlockSpec(memory_space=pltpu.HBM)
    acc = [(8, TOK, BLK), (4, TOK, BLK)]
    outs, specs = [jax.ShapeDtypeStruct(s, f32) for s in acc], [vmem, vmem]
    scratch = [pltpu.VMEM((SLOTS, BLK, BLK), bf16), pltpu.SemaphoreType.DMA((SLOTS,))]
    if stage == 3:
        wide = [(TOK, 8 * BLK), (TOK, 4 * BLK)]
        outs += [jax.ShapeDtypeStruct(s, bf16) for s in wide]
        specs += [hbm, hbm]
        scratch += [pltpu.VMEM(s, bf16) for s in wide] + [pltpu.SemaphoreType.DMA((12,))]
    return pl.pallas_call(
        lambda *refs: tiles_body(stage, counts, at_j, at_i, *refs),
        out_shape=outs,
        in_specs=[pl.BlockSpec(memory_space=pltpu.SMEM), vmem, vmem, *([vmem] * len(head)), *([hbm] * len(arrays))],
        out_specs=specs,
        scratch_shapes=scratch,
        input_output_aliases={} if stage == 1 else {3: 0, 4: 1},
        compiler_params=params(24),
        name=f"tiles_{stage}",
    )(tab, att, cot, *head, *arrays)


def per_device(
    table,
    queries,
    keys,
    values,
    lengths,
    weight,
    codes,
    factor,
    offset,
    down,
    up,
    cot,
):
    tab = table.reshape(-1)
    lens = lengths.reshape(-1)

    quarter = base_quarter(tab, weight, codes, factor, offset)
    down, up, quarter = lax.optimization_barrier((down, up, quarter))
    own_tile = ordered(tab, [z_round(quarter, k) for k in range(4)])

    adapters = jnp.concatenate([down, up, jnp.zeros((64, 16), bf16)], 1)[None]
    for axis, bit in (("zh", 1), ("zh", 2)):
        adapters = jnp.concatenate([adapters, flip(adapters, axis, bit)], 0)
    att = attend(tab, lens, queries, keys, values)
    own_tile, adapters, att = lax.optimization_barrier((own_tile, adapters, att))

    mids = [middle(own_tile, k) for k in (1, -1, 2)]
    for axis, bit in (("x", 1), ("x", 2), ("c", 1)):
        adapters = jnp.concatenate([adapters, flip(adapters, axis, bit)], 0)
    row = jnp.stack([own_tile, *mids])
    row, adapters = lax.optimization_barrier((row, adapters))

    from_less, from_more = outer(row, 1), outer(row, -1)
    row_other = sibling(row)
    low_a, lg_a, down_t, up_t, keep, give = low_terms(tab, att, cot, adapters)
    part = keep + flip(give, "c", 1)
    for axis, bit, n in (("zh", 1, 8), ("zh", 2, 4)):
        part = part[:n] + flip(part[n:].astype(bf16), axis, bit).astype(f32)
    sums = add_tiles(1, tab, att, cot, (low_a, lg_a, down_t, up_t), [row, row_other], T_J1, T_I1)
    for axis, bit, n in (("x", 2, 2), ("x", 1, 1)):
        part = part[:n] + flip(part[n:], axis, bit)
    part = part[0]
    from_less, from_more, part, sums = lax.optimization_barrier((from_less, from_more, part, tuple(sums)))

    far_a, far_b = outer(from_less[:2], 1), outer(from_more[2:], -1)
    nears = [from_less, from_more, sibling(from_less), sibling(from_more)]
    part = part + flip(part, "y", 1)
    sums = add_tiles(2, tab, att, cot, sums, nears, T_J2, T_I2)
    far_a, far_b, part, sums = lax.optimization_barrier((far_a, far_b, part, tuple(sums)))

    fars = [far_a, far_b, sibling(far_a), sibling(far_b)]
    part = part + flip(part, "y", 2)
    part = part + flip(part, "zl", 1)
    _, _, out, grad = add_tiles(3, tab, att, cot, sums, fars, T_J3, T_I3)
    half = DCOLS // 2
    down_grad = jnp.concatenate([part[:half, :64], part[:half, 64:]], 0).T
    up_grad = jnp.concatenate([part[half:, :64], part[half:, 64:]], 0).T
    return out, grad, down_grad, up_grad


def solution(mesh):
    fine = Mesh(np.asarray(mesh.devices).reshape(DIMS), AX)
    tokens, owners = ("y", "zl", "x", "zh", "c"), ("x", "zh", "c")
    table = device_table()
    mapped = jax.shard_map(
        per_device,
        mesh=fine,
        in_specs=(
            P(tokens, None),
            P(tokens, None),
            P(tokens, None),
            P(tokens, None),
            P(owners, None, None),
            P(None, owners),
            P(None, owners),
            P(None, owners),
            P(None, owners),
            P(None, owners),
            P(None, owners),
            P(tokens, None),
        ),
        out_specs=(
            P(tokens, None),
            P(tokens, None),
            P(None, owners),
            P(None, owners),
        ),
        check_vma=False,
    )
    return lambda *args: mapped(jnp.asarray(table), *args)
```

```python
import jax
import jax.numpy as jnp
import numpy as np
from jax import lax
from jax.experimental import pallas as pl
from jax.experimental.pallas import tpu as pltpu
from jax.sharding import Mesh
from jax.sharding import PartitionSpec as P

HEAD = 128
TOK = 192
BLK = 640
COLS = 160
DCOLS = 80
SCALE = 0.25
AX = ("y", "zl", "x", "zh", "c")
DIMS = (4, 2, 4, 4, 2)
REL = (0, -1, 1, 2)
bf16 = jnp.bfloat16
f32 = jnp.float32

T_Y, T_D, T_S, T_F, T_C, T_P, T_TILES = 0, 1, 2, 6, 38, 40, 72
STAGE_AT = (72, 88, 104, 120, 128)
T_LEN = 136


def params(mib=48):
    return pltpu.CompilerParams(vmem_limit_bytes=mib << 20)


def in_hbm(value):
    return pltpu.with_memory_space_constraint(value, pltpu.HBM)


def coords():
    return [np.unravel_index(d, DIMS) for d in range(256)]


def device_table():
    rows = np.zeros((256, T_LEN), np.int32)
    for n, (y, zl, x, zh, c) in enumerate(coords()):
        r = rows[n]
        r[T_Y], r[T_D], r[T_C] = y, y * 2 + zl, c
        for k in range(4):
            r[T_S + k] = (zh - k) % 4
        for f in range(32):
            fx, fz, fc = f // 8, (f // 2) % 4, f % 2
            r[T_F + f] = (fc ^ c) * 16 + (fz ^ zh) * 4 + (fx ^ x)
            dz = fz ^ zh
            r[T_P + f] = (dz % 2) * 8 + (dz // 2) * 4 + (fx ^ x)

        def tiles(own, v, us):
            kind = c if own else 1 - c
            if kind == 0:
                return [(2 * ((x + u) % 4), (y + v) % 4) for u in us]
            return [(2 * ((x + v) % 4) + 1, (y + u) % 4) for u in us]

        both = lambda pairs: [
            t for own in (True, False) for u, v in pairs for t in tiles(own, v, (u,))
        ]
        stages = (
            both([(u, 0) for u in REL]),
            both([(u, v) for u in REL[:2] for v in (-1, 1)]),
            both([(u, v) for u in REL[2:] for v in (-1, 1)]),
            both([(0, 2), (1, 2)]),
            both([(-1, 2), (2, 2)]),
        )
        at = T_TILES
        for stage in stages:
            for k, (j, i) in enumerate(stage):
                r[at + k], r[at + len(stage) + k] = j, i
            at += 2 * len(stage)
    return rows


def index_of(y, zl, x, zh, c):
    return int(np.ravel_multi_index((y % 4, zl, x % 4, zh % 4, c), DIMS))


def send(value, target):
    pairs = [(n, index_of(*target(*(int(v) for v in at)))) for n, at in enumerate(coords())]
    return lax.ppermute(value, AX, pairs)


def z_round(value, k):
    return send(value, lambda y, zl, x, zh, c: (y, zl, x, 2 * (zh % 2) + c + k, zh // 2))


def middle(value, k):
    return send(value, lambda y, zl, x, zh, c: (y, zl, x + k, zh, c) if c == 0 else (y + k, zl, x, zh, c))


def outer(value, k):
    return send(value, lambda y, zl, x, zh, c: (y + k, zl, x, zh, c) if c == 0 else (y, zl, x + k, zh, c))


def sibling(value):
    return send(value, lambda y, zl, x, zh, c: (y, zl, x, zh, 1 - c))


def flip(value, axis, bit):
    at = AX.index(axis)

    def target(*place):
        place = list(place)
        place[at] ^= bit
        return place

    return send(value, target)


def nt(a, b):
    return lax.dot_general(a, b, (((1,), (1,)), ((), ())), preferred_element_type=f32)


def nn(a, b):
    return lax.dot_general(a, b, (((1,), (0,)), ((), ())), preferred_element_type=f32)


def tn(a, b):
    return lax.dot_general(a, b, (((0,), (0,)), ((), ())), preferred_element_type=f32)


def eye(n):
    rows = lax.broadcasted_iota(jnp.int32, (n, n), 0)
    cols = lax.broadcasted_iota(jnp.int32, (n, n), 1)
    return jnp.where(rows == cols, 1.0, 0.0).astype(bf16)


def base_body(tab, weight_t, codes, factor, offset, out, weight, code_v, factor_v, offset_v, sems):
    y = tab[T_Y]
    copies = [
        pltpu.make_async_copy(weight_t.at[:, pl.ds(pl.multiple_of(y * BLK, 128), BLK)], weight, sems.at[0]),
        pltpu.make_async_copy(codes, code_v, sems.at[1]),
        pltpu.make_async_copy(factor, factor_v, sems.at[2]),
        pltpu.make_async_copy(offset, offset_v, sems.at[3]),
    ]
    for copy in copies:
        copy.start()
    for copy in copies:
        copy.wait()
    rows = []
    for k in range(10):
        b = y * 10 + k
        code = code_v[pl.ds(b, 1), :].astype(f32)
        group = b // 8
        rows.append(factor_v[pl.ds(group, 1), :] * (code + 1.0) / 256.0 + offset_v[pl.ds(group, 1), :])
    rest = jnp.concatenate([*rows, jnp.zeros((6, COLS), f32)], 0)
    spread = lax.broadcasted_iota(jnp.int32, (16, BLK), 1) // 64
    spread = spread == lax.broadcasted_iota(jnp.int32, (16, BLK), 0)
    spread = jnp.where(spread, 1.0, 0.0).astype(bf16)
    absmax = jnp.zeros((COLS, BLK), f32)
    for _ in range(3):
        piece = rest.astype(bf16)
        rest = rest - piece.astype(f32)
        absmax = absmax + tn(piece, spread)
    out[...] = (weight[...].astype(f32) * absmax).astype(bf16)


def base_quarter(tab, weight, codes, factor, offset):
    hbm = pl.BlockSpec(memory_space=pltpu.HBM)
    return pl.pallas_call(
        base_body,
        out_shape=jax.ShapeDtypeStruct((COLS, BLK), bf16),
        in_specs=[pl.BlockSpec(memory_space=pltpu.SMEM), hbm, hbm, hbm, hbm],
        out_specs=pl.BlockSpec(memory_space=pltpu.VMEM),
        scratch_shapes=[
            pltpu.VMEM((COLS, BLK), bf16),
            pltpu.VMEM(codes.shape, jnp.int32),
            pltpu.VMEM(factor.shape, f32),
            pltpu.VMEM(offset.shape, f32),
            pltpu.SemaphoreType.DMA((4,)),
        ],
        compiler_params=params(16),
        name="base_quarter",
    )(tab, *(in_hbm(v) for v in (weight.T, codes, factor, offset)))


def order_body(tab, a, b, c, d, out, sems):
    copies = [
        pltpu.make_async_copy(src, out.at[pl.ds(tab[T_S + k] * COLS, COLS), :], sems.at[k])
        for k, src in enumerate((a, b, c, d))
    ]
    for copy in copies:
        copy.start()
    for copy in copies:
        copy.wait()


def ordered(tab, blocks):
    anywhere = pl.BlockSpec(memory_space=pl.ANY)
    return pl.pallas_call(
        order_body,
        out_shape=jax.ShapeDtypeStruct((BLK, BLK), bf16),
        grid_spec=pltpu.PrefetchScalarGridSpec(
            num_scalar_prefetch=1,
            grid=(1,),
            in_specs=[anywhere] * 4,
            out_specs=anywhere,
            scratch_shapes=[pltpu.SemaphoreType.DMA((4,))],
        ),
        compiler_params=params(),
        name="ordered",
    )(tab, *blocks)


def attend_body(tab, lens, queries, keys, values, out):
    d = tab[T_D]
    rows = lax.broadcasted_iota(jnp.int32, (TOK, TOK), 0)
    cols = lax.broadcasted_iota(jnp.int32, (TOK, TOK), 1)
    end = jnp.int32(0)
    row_doc = jnp.zeros((TOK, TOK), jnp.int32)
    col_doc = jnp.zeros((TOK, TOK), jnp.int32)
    for k in range(4):
        end = end + lens[d * 4 + k]
        row_doc = row_doc + jnp.where(rows >= end, 1, 0)
        col_doc = col_doc + jnp.where(cols >= end, 1, 0)
    allowed = (row_doc == col_doc) & (cols <= rows)
    for h in range(BLK // HEAD):
        at = slice(h * HEAD, (h + 1) * HEAD)
        scores = nt(queries[:, at], keys[:, at]) * (HEAD ** -0.5)
        scores = jnp.where(allowed, scores, -1e30)
        weights = jnp.exp(scores - jnp.max(scores, axis=-1, keepdims=True))
        total = jnp.sum(weights, axis=-1, keepdims=True)
        out[:, at] = (nn(weights.astype(bf16), values[:, at]) / total).astype(bf16)


def attend(tab, lens, queries, keys, values):
    spec = pl.BlockSpec((TOK, BLK), lambda i, *_: (0, i))
    return pl.pallas_call(
        attend_body,
        out_shape=jax.ShapeDtypeStruct(queries.shape, bf16),
        grid_spec=pltpu.PrefetchScalarGridSpec(
            num_scalar_prefetch=2, grid=(4,), in_specs=[spec] * 3, out_specs=spec
        ),
        compiler_params=params(12),
        name="attend",
    )(tab, lens, *(in_hbm(v) for v in (queries, keys, values)))


def low_body(tab, att, cot, gathered, low_out, lg_out, down_t, up_t, keep, give):
    unit = eye(256)
    for f in range(32):
        block = gathered[tab[T_F + f]]
        turned = nt(unit, jnp.concatenate([block, block], 0)).astype(bf16)
        down_t[f * DCOLS : (f + 1) * DCOLS, :] = turned[:DCOLS]
        up_t[f * COLS : (f + 1) * COLS, :] = turned[DCOLS : DCOLS + COLS]
    low = nn(att[...], down_t[...])
    low_grad = nn(cot[...], up_t[...]) * SCALE
    first = lax.broadcasted_iota(jnp.int32, (TOK, 128), 1) < 64
    none = jnp.zeros((TOK, 128), f32)
    low_a, low_b = (jnp.where(first, low, none).astype(bf16), jnp.where(first, none, low).astype(bf16))
    lg_a, lg_b = (
        jnp.where(first, low_grad, none).astype(bf16),
        jnp.where(first, none, low_grad).astype(bf16),
    )
    low_out[...] = low_a
    lg_out[...] = lg_a
    core = tab[T_C]

    def put(f, lo, hi, even, odd):
        place = tab[T_P + f]
        keep[place, lo:hi, :] = jnp.where(core == 0, even, odd)
        give[place, lo:hi, :] = jnp.where(core == 0, odd, even)

    half = DCOLS // 2
    both = jnp.concatenate([lg_a, lg_b], 1)
    for i in range(4):
        got = tn(att[:, i * BLK : (i + 1) * BLK], both)
        a, b = got[:, :128], got[:, 128:]
        pair = []
        for k in range(8):
            s = k * DCOLS
            pair.append(a[s : s + half] + b[s + half : s + DCOLS])
        for k in range(0, 8, 2):
            put(i * 8 + k, 0, half, pair[k], pair[k + 1])
    both = jnp.concatenate([low_a, low_b], 1)
    for j in range(8):
        got = tn(cot[:, j * BLK : (j + 1) * BLK], both) * SCALE
        a, b = got[:, :128], got[:, 128:]
        pair = []
        for k in range(4):
            s = k * COLS
            pair.append(a[s : s + DCOLS] + b[s + DCOLS : s + COLS])
        for k in range(0, 4, 2):
            put(j * 4 + k, half, half + DCOLS, pair[k], pair[k + 1])


def low_terms(tab, att, cot, gathered):
    vmem = pl.BlockSpec(memory_space=pltpu.VMEM)
    return pl.pallas_call(
        low_body,
        out_shape=(
            jax.ShapeDtypeStruct((TOK, 128), bf16),
            jax.ShapeDtypeStruct((TOK, 128), bf16),
            jax.ShapeDtypeStruct((32 * DCOLS, 128), bf16),
            jax.ShapeDtypeStruct((32 * COLS, 128), bf16),
            jax.ShapeDtypeStruct((16, 120, 128), f32),
            jax.ShapeDtypeStruct((16, 120, 128), f32),
        ),
        in_specs=[pl.BlockSpec(memory_space=pltpu.SMEM), vmem, vmem, vmem],
        out_specs=[vmem] * 6,
        compiler_params=params(16),
        name="low_terms",
    )(tab, att, cot, gathered)


SLOTS = 4


def tiles_body(stage, count, tab, att, cot, *refs):
    n_head = 4 if stage == 0 else 2
    head, refs = refs[:n_head], refs[n_head:]
    tiles, refs = refs[:count], refs[count:]
    out_acc, grad_acc, *refs = refs
    if stage == 4:
        out, grad, *refs = refs
    buf, sems, *refs = refs

    def fetch(t):
        return pltpu.make_async_copy(tiles[t], buf.at[t % SLOTS], sems.at[t % SLOTS])

    for t in range(SLOTS):
        fetch(t).start()
    if stage == 0:
        low_a, lg_a, down_t, up_t = head
        for j in range(8):
            out_acc[j] = nt(low_a[...], up_t[j * BLK : (j + 1) * BLK, :]) * SCALE
        for i in range(4):
            grad_acc[i] = nt(lg_a[...], down_t[i * BLK : (i + 1) * BLK, :])
    for t in range(count):
        j, i = tab[STAGE_AT[stage] + t], tab[STAGE_AT[stage] + count + t]
        fetch(t).wait()
        tile = buf[t % SLOTS]
        out_acc[j] = out_acc[j] + nt(att[:, pl.ds(pl.multiple_of(i * BLK, 128), BLK)], tile)
        grad_acc[i] = grad_acc[i] + nn(cot[:, pl.ds(pl.multiple_of(j * BLK, 128), BLK)], tile)
        if t + SLOTS < count:
            fetch(t + SLOTS).start()
    if stage == 4:
        out_v, grad_v, out_sems = refs
        copies = []
        for acc, full, ref, base in ((out_acc, out_v, out, 0), (grad_acc, grad_v, grad, 8)):
            for k in range(acc.shape[0]):
                at = slice(k * BLK, (k + 1) * BLK)
                full[:, at] = acc[k].astype(bf16)
                copies.append(pltpu.make_async_copy(full.at[:, at], ref.at[:, at], out_sems.at[base + k]))
                copies[-1].start()
        for copy in copies:
            copy.wait()


def add_tiles(stage, tab, att, cot, head, arrays):
    vmem = pl.BlockSpec(memory_space=pltpu.VMEM)
    hbm = pl.BlockSpec(memory_space=pltpu.HBM)
    acc = [(8, TOK, BLK), (4, TOK, BLK)]
    outs, specs = [jax.ShapeDtypeStruct(s, f32) for s in acc], [vmem, vmem]
    scratch = [pltpu.VMEM((SLOTS, BLK, BLK), bf16), pltpu.SemaphoreType.DMA((SLOTS,))]
    if stage == 4:
        wide = [(TOK, 8 * BLK), (TOK, 4 * BLK)]
        outs += [jax.ShapeDtypeStruct(s, bf16) for s in wide]
        specs += [hbm, hbm]
        scratch += [pltpu.VMEM(s, bf16) for s in wide] + [pltpu.SemaphoreType.DMA((12,))]
    return pl.pallas_call(
        lambda *refs: tiles_body(stage, len(arrays), *refs),
        out_shape=outs,
        in_specs=[pl.BlockSpec(memory_space=pltpu.SMEM), vmem, vmem, *([vmem] * len(head)), *([hbm] * len(arrays))],
        out_specs=specs,
        scratch_shapes=scratch,
        input_output_aliases={} if stage == 0 else {3: 0, 4: 1},
        compiler_params=params(16),
        name=f"tiles_{stage}",
    )(tab, att, cot, *head, *arrays)


def per_device(
    table,
    queries,
    keys,
    values,
    lengths,
    weight,
    codes,
    factor,
    offset,
    down,
    up,
    cot,
):
    tab = table.reshape(-1)
    lens = lengths.reshape(-1)

    tie = lax.optimization_barrier

    def doubled(adapters, axis, bit):
        return jnp.concatenate([adapters, flip(adapters, axis, bit)], 0)

    def near(tile):
        return outer(tile, 1), outer(tile, -1)

    def siblings(tiles):
        return [sibling(t) for t in tiles]

    quarter = base_quarter(tab, weight, codes, factor, offset)
    down, up, quarter, queries = tie((down, up, quarter, queries))
    rounds = [z_round(quarter, k) for k in range(4)]
    adapters = jnp.concatenate([down, up, jnp.zeros((64, 16), bf16)], 1)[None]
    adapters = doubled(adapters, "x", 1)
    adapters, queries = tie((adapters, queries))
    adapters = doubled(adapters, "x", 2)
    att = attend(tab, lens, queries, keys, values)
    rounds, att, adapters = tie((rounds, att, adapters))
    own = ordered(tab, rounds)

    less, more, far = middle(own, 1), middle(own, -1), middle(own, 2)
    own_n = near(own)
    own, adapters = tie((own, adapters))
    for bit in (1, 2):
        adapters = doubled(adapters, "zh", bit)
    less, more, adapters = tie((less, more, adapters))
    less_n, more_n = near(less), near(more)
    adapters = doubled(adapters, "c", 1)
    far, adapters = tie((far, adapters))
    far_n = near(far)
    row = [own, less, more, far]
    row_other = siblings(row)
    low_a, lg_a, down_t, up_t, keep, give = low_terms(tab, att, cot, adapters)
    part = keep + flip(give, "c", 1)

    def scattered(part, axis, bit, n, kind):
        return part[:n] + flip(part[n:].astype(kind), axis, bit).astype(f32)

    part, row, row_other, own_n = tie((part, row, row_other, own_n))
    own_far = outer(own_n[0], 1)
    part = scattered(part, "zh", 1, 8, bf16)
    sums = add_tiles(0, tab, att, cot, (low_a, lg_a, down_t, up_t), [*row, *row_other])

    sums, part, own_n, less_n = tie((tuple(sums), part, own_n, less_n))
    less_far = outer(less_n[0], 1)
    part = scattered(part, "zh", 2, 4, bf16)
    tiles = [*own_n, *less_n]
    tiles_other = siblings(tiles)
    sums = add_tiles(1, tab, att, cot, sums, [*tiles, *tiles_other])

    sums, part, more_n = tie((tuple(sums), part, more_n))
    more_far = outer(more_n[1], -1)
    part = scattered(part, "x", 2, 2, f32)
    far_n, part = tie((far_n, part))
    far_far = outer(far_n[1], -1)
    part = scattered(part, "x", 1, 1, f32)[0]
    tiles = [*more_n, *far_n]
    tiles_other = siblings(tiles)
    sums = add_tiles(2, tab, att, cot, sums, [*tiles, *tiles_other])

    sums, part, own_far, more_far = tie((tuple(sums), part, own_far, more_far))
    part = part + flip(part, "y", 1)
    tiles = [own_far, more_far]
    sums = add_tiles(3, tab, att, cot, sums, [*tiles, *siblings(tiles)])

    sums, part, less_far, far_far = tie((tuple(sums), part, less_far, far_far))
    part = part + flip(part, "y", 2)
    part = part + flip(part, "zl", 1)
    tiles = [less_far, far_far]
    _, _, out, grad = add_tiles(4, tab, att, cot, sums, [*tiles, *siblings(tiles)])
    half = DCOLS // 2
    down_grad = jnp.concatenate([part[:half, :64], part[:half, 64:]], 0).T
    up_grad = jnp.concatenate([part[half:, :64], part[half:, 64:]], 0).T
    return out, grad, down_grad, up_grad


def solution(mesh):
    fine = Mesh(np.asarray(mesh.devices).reshape(DIMS), AX)
    tokens, owners = ("y", "zl", "x", "zh", "c"), ("x", "zh", "c")
    table = device_table()
    mapped = jax.shard_map(
        per_device,
        mesh=fine,
        in_specs=(
            P(tokens, None),
            P(tokens, None),
            P(tokens, None),
            P(tokens, None),
            P(owners, None, None),
            P(None, owners),
            P(None, owners),
            P(None, owners),
            P(None, owners),
            P(None, owners),
            P(None, owners),
            P(tokens, None),
        ),
        out_specs=(
            P(tokens, None),
            P(tokens, None),
            P(None, owners),
            P(None, owners),
        ),
        check_vma=False,
    )
    return lambda *args: mapped(jnp.asarray(table), *args)
```

```python
import jax
import jax.numpy as jnp
import numpy as np
from jax import lax
from jax.experimental import pallas as pl
from jax.experimental.pallas import tpu as pltpu
from jax.sharding import Mesh
from jax.sharding import PartitionSpec as P

HEAD = 128
TOK = 192
BLK = 640
COLS = 160
DCOLS = 80
SCALE = 0.25
AX = ("y", "zl", "x", "zh", "c")
DIMS = (4, 2, 4, 4, 2)
REL = (0, -1, 1, 2)


def cost(us):
    return pl.CostEstimate(flops=int(us * 1.15e9) + 1, bytes_accessed=1, transcendentals=0)


bf16 = jnp.bfloat16
f32 = jnp.float32

T_Y, T_D, T_S, T_F, T_C, T_P, T_B, T_TILES = 0, 1, 2, 6, 38, 40, 72, 104
STAGE_AT = (104, 120, 136, 152)
T_LEN = 168
ROWS = COLS + 128


def params(mib=48):
    return pltpu.CompilerParams(vmem_limit_bytes=mib << 20)


def in_hbm(value):
    return pltpu.with_memory_space_constraint(value, pltpu.HBM)


def coords():
    return [np.unravel_index(d, DIMS) for d in range(256)]


def device_table():
    rows = np.zeros((256, T_LEN), np.int32)
    for n, (y, zl, x, zh, c) in enumerate(coords()):
        r = rows[n]
        r[T_Y], r[T_D], r[T_C] = y, y * 2 + zl, c
        for k in range(4):
            r[T_S + k] = (zh - k) % 4
        for f in range(32):
            fx, fz, fc = f // 8, (f // 2) % 4, f % 2
            r[T_F + f] = (zh - 2 * (fz % 2) - fc) % 4
            r[T_B + f] = [(x + k) % 4 for k in REL].index(fx) * 32
            r[T_P + f] = fx ^ x

        def tiles(own, v, us):
            kind = c if own else 1 - c
            if kind == 0:
                return [(2 * ((x + u) % 4), (y + v) % 4) for u in us]
            return [(2 * ((x + v) % 4) + 1, (y + u) % 4) for u in us]

        both = lambda pairs: [
            t for own in (True, False) for u, v in pairs for t in tiles(own, v, (u,))
        ]
        nears = [(u, v) for half in (REL[:2], REL[2:]) for v in (-1, 1) for u in half]
        stages = (
            both([(u, 0) for u in REL]),
            [t for u, v in nears for t in tiles(True, v, (u,))],
            [t for u, v in nears for t in tiles(False, v, (u,))],
            both([(u, 2) for u in REL]),
        )
        at = T_TILES
        for stage in stages:
            for k, (j, i) in enumerate(stage):
                r[at + k], r[at + len(stage) + k] = j, i
            at += 2 * len(stage)
    return rows


def index_of(y, zl, x, zh, c):
    return int(np.ravel_multi_index((y % 4, zl, x % 4, zh % 4, c), DIMS))


def send(value, target):
    pairs = [(n, index_of(*target(*(int(v) for v in at)))) for n, at in enumerate(coords())]
    return lax.ppermute(value, AX, pairs)


def z_round(value, k):
    return send(value, lambda y, zl, x, zh, c: (y, zl, x, 2 * (zh % 2) + c + k, zh // 2))


def middle(value, k):
    return send(value, lambda y, zl, x, zh, c: (y, zl, x + k, zh, c) if c == 0 else (y + k, zl, x, zh, c))


def outer(value, k):
    return send(value, lambda y, zl, x, zh, c: (y + k, zl, x, zh, c) if c == 0 else (y, zl, x + k, zh, c))


def sibling(value):
    return send(value, lambda y, zl, x, zh, c: (y, zl, x, zh, 1 - c))


def flip(value, axis, bit):
    at = AX.index(axis)

    def target(*place):
        place = list(place)
        place[at] ^= bit
        return place

    return send(value, target)


def nt(a, b):
    return lax.dot_general(a, b, (((1,), (1,)), ((), ())), preferred_element_type=f32)


def nn(a, b):
    return lax.dot_general(a, b, (((1,), (0,)), ((), ())), preferred_element_type=f32)


def tn(a, b):
    return lax.dot_general(a, b, (((0,), (0,)), ((), ())), preferred_element_type=f32)


def eye(n):
    rows = lax.broadcasted_iota(jnp.int32, (n, n), 0)
    cols = lax.broadcasted_iota(jnp.int32, (n, n), 1)
    return jnp.where(rows == cols, 1.0, 0.0).astype(bf16)


def base_body(tab, weight_t, codes, factor, offset, ad_0, ad_1, ad_2, ad_3, out, weight, code_v, factor_v, offset_v, sems):
    y = tab[T_Y]
    copies = [
        pltpu.make_async_copy(weight_t.at[:, pl.ds(pl.multiple_of(y * BLK, 128), BLK)], weight, sems.at[0]),
        pltpu.make_async_copy(codes, code_v, sems.at[1]),
        pltpu.make_async_copy(factor, factor_v, sems.at[2]),
        pltpu.make_async_copy(offset, offset_v, sems.at[3]),
    ]
    for copy in copies:
        copy.start()
    for copy in copies:
        copy.wait()
    rows = []
    for k in range(10):
        b = y * 10 + k
        code = code_v[pl.ds(b, 1), :].astype(f32)
        group = b // 8
        rows.append(factor_v[pl.ds(group, 1), :] * (code + 1.0) / 256.0 + offset_v[pl.ds(group, 1), :])
    rest = jnp.concatenate([*rows, jnp.zeros((6, COLS), f32)], 0)
    spread = lax.broadcasted_iota(jnp.int32, (16, BLK), 1) // 64
    spread = spread == lax.broadcasted_iota(jnp.int32, (16, BLK), 0)
    spread = jnp.where(spread, 1.0, 0.0).astype(bf16)
    absmax = jnp.zeros((COLS, BLK), f32)
    for _ in range(3):
        piece = rest.astype(bf16)
        rest = rest - piece.astype(f32)
        absmax = absmax + tn(piece, spread)
    out[:COLS, :] = (weight[...].astype(f32) * absmax).astype(bf16)
    for k, adapter in enumerate((ad_0, ad_1, ad_2, ad_3)):
        at = slice(COLS + k * 32, COLS + (k + 1) * 32)
        out[at, :256] = adapter[:32, :]
        out[at, 256:512] = adapter[32:, :]
        out[at, 512:] = jnp.zeros((32, 128), bf16)


def base_quarter(tab, weight, codes, factor, offset, adapters):
    hbm = pl.BlockSpec(memory_space=pltpu.HBM)
    vmem = pl.BlockSpec(memory_space=pltpu.VMEM)
    return pl.pallas_call(
        base_body,
        out_shape=jax.ShapeDtypeStruct((ROWS, BLK), bf16),
        in_specs=[pl.BlockSpec(memory_space=pltpu.SMEM), hbm, hbm, hbm, hbm, *([vmem] * 4)],
        out_specs=pl.BlockSpec(memory_space=pltpu.VMEM),
        scratch_shapes=[
            pltpu.VMEM((COLS, BLK), bf16),
            pltpu.VMEM(codes.shape, jnp.int32),
            pltpu.VMEM(factor.shape, f32),
            pltpu.VMEM(offset.shape, f32),
            pltpu.SemaphoreType.DMA((4,)),
        ],
        cost_estimate=cost(0),
        compiler_params=params(16),
        name="base_quarter",
    )(tab, *(in_hbm(v) for v in (weight.T, codes, factor, offset)), *adapters)


def order_body(tab, a, b, c, d, out, adapters, sems):
    copies = []
    for k, src in enumerate((a, b, c, d)):
        place = pl.multiple_of(tab[T_S + k] * COLS, 32)
        copies.append(pltpu.make_async_copy(src.at[:COLS, :], out.at[pl.ds(place, COLS), :], sems.at[k]))
        copies.append(pltpu.make_async_copy(src.at[COLS:, :], adapters.at[k], sems.at[4 + k]))
    for copy in copies:
        copy.start()
    for copy in copies:
        copy.wait()


def ordered(tab, blocks):
    anywhere = pl.BlockSpec(memory_space=pl.ANY)
    return pl.pallas_call(
        order_body,
        out_shape=(
            jax.ShapeDtypeStruct((BLK, BLK), bf16),
            jax.ShapeDtypeStruct((4, 128, BLK), bf16),
        ),
        in_specs=[pl.BlockSpec(memory_space=pltpu.SMEM), *([anywhere] * 4)],
        out_specs=[anywhere] * 2,
        scratch_shapes=[pltpu.SemaphoreType.DMA((8,))],
        cost_estimate=cost(0),
        compiler_params=params(8),
        name="ordered",
    )(tab, *blocks)


def attend_body(tab, lens, queries, keys, values, out):
    d = tab[T_D]
    rows = lax.broadcasted_iota(jnp.int32, (TOK, TOK), 0)
    cols = lax.broadcasted_iota(jnp.int32, (TOK, TOK), 1)
    end = jnp.int32(0)
    row_doc = jnp.zeros((TOK, TOK), jnp.int32)
    col_doc = jnp.zeros((TOK, TOK), jnp.int32)
    for k in range(4):
        end = end + lens[d * 4 + k]
        row_doc = row_doc + jnp.where(rows >= end, 1, 0)
        col_doc = col_doc + jnp.where(cols >= end, 1, 0)
    allowed = (row_doc == col_doc) & (cols <= rows)
    for h in range(BLK // HEAD):
        at = slice(h * HEAD, (h + 1) * HEAD)
        scores = nt(queries[:, at], keys[:, at]) * (HEAD ** -0.5)
        scores = jnp.where(allowed, scores, -1e30)
        weights = jnp.exp(scores - jnp.max(scores, axis=-1, keepdims=True))
        total = jnp.sum(weights, axis=-1, keepdims=True)
        out[:, at] = (nn(weights.astype(bf16), values[:, at]) / total).astype(bf16)


def attend(tab, lens, queries, keys, values):
    spec = pl.BlockSpec((TOK, BLK), lambda i, *_: (0, i))
    return pl.pallas_call(
        attend_body,
        out_shape=jax.ShapeDtypeStruct(queries.shape, bf16),
        grid_spec=pltpu.PrefetchScalarGridSpec(
            num_scalar_prefetch=2, grid=(4,), in_specs=[spec] * 3, out_specs=spec
        ),
        cost_estimate=cost(0),
        compiler_params=params(12),
        name="attend",
    )(tab, lens, *(in_hbm(v) for v in (queries, keys, values)))


def low_body(tab, att, cot, mine, other, low_out, lg_out, down_t, up_t, parts):
    unit = eye(256)
    for f in range(32):
        at = (tab[T_F + f], pl.ds(pl.multiple_of(tab[T_B + f], 32), 32))
        own_block = tab[T_C] == (f // 4) % 2
        halves = [
            jnp.where(own_block, mine[(*at, part)], other[(*at, part)])
            for part in (slice(0, 256), slice(256, 512))
        ]
        turned = nt(unit, jnp.concatenate(halves * 2, 0)).astype(bf16)
        down_t[f * DCOLS : (f + 1) * DCOLS, :] = turned[:DCOLS]
        up_t[f * COLS : (f + 1) * COLS, :] = turned[DCOLS : DCOLS + COLS]
    low = nn(att[...], down_t[...])
    low_grad = nn(cot[...], up_t[...]) * SCALE
    first = lax.broadcasted_iota(jnp.int32, (TOK, 128), 1) < 64
    none = jnp.zeros((TOK, 128), f32)
    low_a, low_b = (jnp.where(first, low, none).astype(bf16), jnp.where(first, none, low).astype(bf16))
    lg_a, lg_b = (
        jnp.where(first, low_grad, none).astype(bf16),
        jnp.where(first, none, low_grad).astype(bf16),
    )
    low_out[...] = low_a
    lg_out[...] = lg_a
    half = DCOLS // 2
    both = jnp.concatenate([lg_a, lg_b], 1)
    for i in range(4):
        got = tn(att[:, i * BLK : (i + 1) * BLK], both)
        a, b = got[:, :128], got[:, 128:]
        for k in range(8):
            f, s = i * 8 + k, k * DCOLS
            parts[f % 8, tab[T_P + f], :half, :] = (a[s : s + half] + b[s + half : s + DCOLS]).astype(bf16)
    both = jnp.concatenate([low_a, low_b], 1)
    for j in range(8):
        got = tn(cot[:, j * BLK : (j + 1) * BLK], both) * SCALE
        a, b = got[:, :128], got[:, 128:]
        for k in range(4):
            f, s = j * 4 + k, k * COLS
            value = a[s : s + DCOLS] + b[s + DCOLS : s + COLS]
            parts[f % 8, tab[T_P + f], half:, :] = value.astype(bf16)


def low_terms(tab, att, cot, mine, other):
    vmem = pl.BlockSpec(memory_space=pltpu.VMEM)
    return pl.pallas_call(
        low_body,
        out_shape=(
            jax.ShapeDtypeStruct((TOK, 128), bf16),
            jax.ShapeDtypeStruct((TOK, 128), bf16),
            jax.ShapeDtypeStruct((32 * DCOLS, 128), bf16),
            jax.ShapeDtypeStruct((32 * COLS, 128), bf16),
            jax.ShapeDtypeStruct((8, 4, 120, 128), bf16),
        ),
        in_specs=[pl.BlockSpec(memory_space=pltpu.SMEM), *([vmem] * 4)],
        out_specs=[vmem] * 5,
        cost_estimate=cost(4),
        compiler_params=params(16),
        name="low_terms",
    )(tab, att, cot, mine, other)


SLOTS = 4


def tiles_body(stage, counts, tab, att, cot, *refs):
    n_head = 4 if stage == 0 else 2
    head, refs = refs[:n_head], refs[n_head:]
    tiles, refs = refs[: len(counts)], refs[len(counts) :]
    places = [(a, k) for a, n in enumerate(counts) for k in range(n)]
    count = len(places)
    if stage == 3:
        out, grad, out_acc, grad_acc, out_old, grad_old, old_sems, *refs = refs
    elif stage == 2:
        out_new, grad_new, out_acc, grad_acc, new_sems, *refs = refs
    else:
        out_acc, grad_acc, *refs = refs
    buf, sems, *refs = refs

    def fetch(t):
        a, k = places[t]
        return pltpu.make_async_copy(tiles[a].at[k], buf.at[t % SLOTS], sems.at[t % SLOTS])

    for t in range(SLOTS):
        fetch(t).start()
    if stage == 2:
        out_acc[...] = head[0][...]
        grad_acc[...] = head[1][...]
    if stage == 3:
        olds = [
            pltpu.make_async_copy(head[k], ref, old_sems.at[k])
            for k, ref in enumerate((out_old, grad_old))
        ]
        for copy in olds:
            copy.start()
        out_acc[...] = jnp.zeros(out_acc.shape, f32)
        grad_acc[...] = jnp.zeros(grad_acc.shape, f32)
    if stage == 0:
        low_a, lg_a, down_t, up_t = head
        for j in range(8):
            out_acc[j] = nt(low_a[...], up_t[j * BLK : (j + 1) * BLK, :]) * SCALE
        for i in range(4):
            grad_acc[i] = nt(lg_a[...], down_t[i * BLK : (i + 1) * BLK, :])
    for t in range(count):
        j, i = tab[STAGE_AT[stage] + t], tab[STAGE_AT[stage] + count + t]
        fetch(t).wait()
        tile = buf[t % SLOTS]
        out_acc[j] = out_acc[j] + nt(att[:, pl.ds(pl.multiple_of(i * BLK, 128), BLK)], tile)
        grad_acc[i] = grad_acc[i] + nn(cot[:, pl.ds(pl.multiple_of(j * BLK, 128), BLK)], tile)
        if t + SLOTS < count:
            fetch(t + SLOTS).start()
    if stage == 2:
        news = [
            pltpu.make_async_copy(ref, (out_new, grad_new)[k], new_sems.at[k])
            for k, ref in enumerate((out_acc, grad_acc))
        ]
        for copy in news:
            copy.start()
        for copy in news:
            copy.wait()
    if stage == 3:
        out_v, grad_v, out_sems = refs
        for copy in olds:
            copy.wait()
        copies = []
        for acc, old, full, ref, base in (
            (out_acc, out_old, out_v, out, 0),
            (grad_acc, grad_old, grad_v, grad, 8),
        ):
            for k in range(acc.shape[0]):
                at = slice(k * BLK, (k + 1) * BLK)
                full[:, at] = (acc[k] + old[k]).astype(bf16)
                copies.append(pltpu.make_async_copy(full.at[:, at], ref.at[:, at], out_sems.at[base + k]))
                copies[-1].start()
        for copy in copies:
            copy.wait()


def add_tiles(stage, tab, att, cot, head, arrays):
    vmem = pl.BlockSpec(memory_space=pltpu.VMEM)
    hbm = pl.BlockSpec(memory_space=pltpu.HBM)
    acc = [(8, TOK, BLK), (4, TOK, BLK)]
    outs, specs = [jax.ShapeDtypeStruct(s, f32) for s in acc], [vmem, vmem]
    scratch = [pltpu.VMEM((SLOTS, BLK, BLK), bf16), pltpu.SemaphoreType.DMA((SLOTS,))]
    if stage == 3:
        wide = [(TOK, 8 * BLK), (TOK, 4 * BLK)]
        outs, specs = [jax.ShapeDtypeStruct(s, bf16) for s in wide], [hbm, hbm]
        scratch = [pltpu.VMEM(s, f32) for s in acc * 2] + [pltpu.SemaphoreType.DMA((2,))] + scratch
        scratch += [pltpu.VMEM(s, bf16) for s in wide] + [pltpu.SemaphoreType.DMA((12,))]
    if stage == 2:
        outs, specs = [pltpu.HBM(s, f32) for s in acc], [hbm, hbm]
        scratch = [pltpu.VMEM(s, f32) for s in acc] + [pltpu.SemaphoreType.DMA((2,))] + scratch
    if stage == 3:
        head = [in_hbm(h) for h in head]
    head_spec = hbm if stage == 3 else vmem
    return pl.pallas_call(
        lambda *refs: tiles_body(stage, [a.shape[0] for a in arrays], *refs),
        out_shape=outs,
        in_specs=[pl.BlockSpec(memory_space=pltpu.SMEM), vmem, vmem, *([head_spec] * len(head)), *([hbm] * len(arrays))],
        out_specs=specs,
        scratch_shapes=scratch,
        input_output_aliases={} if stage != 1 else {3: 0, 4: 1},
        cost_estimate=cost(0),
        compiler_params=params(28 if stage == 3 else 16),
        name=f"tiles_{stage}",
    )(tab, att, cot, *head, *arrays)


def per_device(
    table,
    queries,
    keys,
    values,
    lengths,
    weight,
    codes,
    factor,
    offset,
    down,
    up,
    cot,
):
    tab = table.reshape(-1)
    lens = lengths.reshape(-1)

    tie = lax.optimization_barrier

    def along_x(value, k):
        return send(value, lambda y, zl, x, zh, c: (y, zl, x + k, zh, c))

    adapter = jnp.concatenate([down, up, jnp.zeros((64, 16), bf16)], 1)
    adapters = [adapter, *(along_x(adapter, -k) for k in REL[1:])]
    message = base_quarter(tab, weight, codes, factor, offset, adapters)
    message, queries = tie((message, queries))
    rounds = [z_round(message, k) for k in range(4)]
    att = attend(tab, lens, queries, keys, values)
    rounds, att = tie((rounds, att))
    own, mine = ordered(tab, rounds)

    less, more, far = middle(own, 1), middle(own, -1), middle(own, 2)
    low = low_terms(tab, att, cot, mine, sibling(mine))
    less, more, far, low = tie((less, more, far, tuple(low)))
    low_a, lg_a, down_t, up_t, part = low
    row_a, row_b = jnp.stack([own, less]), jnp.stack([more, far])

    less_a, more_a = outer(row_a, 1), outer(row_a, -1)
    less_b, more_b = outer(row_b, 1), outer(row_b, -1)
    part, row_a = tie((part, row_a))
    part = lax.all_to_all(part, ("zh", "c"), 0, 0, tiled=True)
    part = jnp.sum(part.astype(f32), axis=0)
    tiles = [row_a, row_b]
    sums = add_tiles(0, tab, att, cot, (low_a, lg_a, down_t, up_t), [*tiles, *(sibling(t) for t in tiles)])

    less_a, more_a, less_b, more_b, part, sums = tie((less_a, more_a, less_b, more_b, part, tuple(sums)))
    a, b, c = (flip(part[k], "x", k) for k in (1, 2, 3))
    part = (part[0] + a) + (b + c)
    far_a, far_b = outer(less_a, 1), outer(more_b, -1)
    tiles = [less_a, more_a, less_b, more_b]
    sums = add_tiles(1, tab, att, cot, sums, tiles)
    sums = add_tiles(2, tab, att, cot, sums, [sibling(t) for t in tiles])
    far_a, far_b, part, sums = tie((far_a, far_b, part, tuple(sums)))
    a, b, c = (flip(part, "y", k) for k in (1, 2, 3))
    part = (part + a) + (b + c)
    tiles = [far_a, far_b]
    tiles_other = [sibling(t) for t in tiles]
    part = part + flip(part, "zl", 1)
    out, grad = add_tiles(3, tab, att, cot, sums, [*tiles, *tiles_other])
    half = DCOLS // 2
    down_grad = jnp.concatenate([part[:half, :64], part[:half, 64:]], 0).T
    up_grad = jnp.concatenate([part[half:, :64], part[half:, 64:]], 0).T
    return out, grad, down_grad, up_grad


def solution(mesh):
    fine = Mesh(np.asarray(mesh.devices).reshape(DIMS), AX)
    tokens, owners = ("y", "zl", "x", "zh", "c"), ("x", "zh", "c")
    table = device_table()
    mapped = jax.shard_map(
        per_device,
        mesh=fine,
        in_specs=(
            P(tokens, None),
            P(tokens, None),
            P(tokens, None),
            P(tokens, None),
            P(owners, None, None),
            P(None, owners),
            P(None, owners),
            P(None, owners),
            P(None, owners),
            P(None, owners),
            P(None, owners),
            P(tokens, None),
        ),
        out_specs=(
            P(tokens, None),
            P(tokens, None),
            P(None, owners),
            P(None, owners),
        ),
        check_vma=False,
    )
    return lambda *args: mapped(jnp.asarray(table), *args)
```

```python
import jax
import jax.numpy as jnp
import numpy as np
from jax import lax
from jax.experimental import pallas as pl
from jax.experimental.pallas import tpu as pltpu
from jax.sharding import Mesh
from jax.sharding import PartitionSpec as P

HEAD = 128
TOK = 192
BLK = 640
COLS = 160
DCOLS = 80
SCALE = 0.25
AX = ("y", "zl", "x", "zh", "c")
DIMS = (4, 2, 4, 4, 2)
REL = (0, -1, 1, 2)


def cost(us):
    return pl.CostEstimate(flops=int(us * 1.15e9) + 1, bytes_accessed=1, transcendentals=0)


bf16 = jnp.bfloat16
f32 = jnp.float32

T_Y, T_D, T_S, T_F, T_C, T_P, T_B, T_TILES = 0, 1, 2, 6, 38, 40, 72, 104
STAGE_AT = (104, 120, 136, 152)
T_LEN = 168


def params(mib=48):
    return pltpu.CompilerParams(vmem_limit_bytes=mib << 20)


def in_hbm(value):
    return pltpu.with_memory_space_constraint(value, pltpu.HBM)


def coords():
    return [np.unravel_index(d, DIMS) for d in range(256)]


def device_table():
    rows = np.zeros((256, T_LEN), np.int32)
    for n, (y, zl, x, zh, c) in enumerate(coords()):
        r = rows[n]
        r[T_Y], r[T_D], r[T_C] = y, y * 2 + zl, c
        for k in range(4):
            r[T_S + k] = (zh - k) % 4
        for f in range(32):
            fx, fz, fc = f // 8, (f // 2) % 4, f % 2
            r[T_F + f] = [(x + k) % 4 for k in REL].index(fx) * 4 + [(zh + k) % 4 for k in REL].index(fz)
            dz = fz ^ zh
            r[T_P + f] = (dz % 2) * 8 + (dz // 2) * 4 + (fx ^ x)

        def tiles(own, v, us):
            kind = c if own else 1 - c
            if kind == 0:
                return [(2 * ((x + u) % 4), (y + v) % 4) for u in us]
            return [(2 * ((x + v) % 4) + 1, (y + u) % 4) for u in us]

        both = lambda pairs: [
            t for own in (True, False) for u, v in pairs for t in tiles(own, v, (u,))
        ]
        nears = [(u, v) for v in (-1, 1) for u in REL]
        stages = (
            both([(u, 0) for u in REL]),
            [t for u, v in nears for t in tiles(True, v, (u,))],
            [t for u, v in nears for t in tiles(False, v, (u,))],
            both([(u, 2) for u in REL]),
        )
        at = T_TILES
        for stage in stages:
            for k, (j, i) in enumerate(stage):
                r[at + k], r[at + len(stage) + k] = j, i
            at += 2 * len(stage)
    return rows


def index_of(y, zl, x, zh, c):
    return int(np.ravel_multi_index((y % 4, zl, x % 4, zh % 4, c), DIMS))


def send(value, target):
    pairs = [(n, index_of(*target(*(int(v) for v in at)))) for n, at in enumerate(coords())]
    return lax.ppermute(value, AX, pairs)


def z_round(value, k):
    return send(value, lambda y, zl, x, zh, c: (y, zl, x, 2 * (zh % 2) + c + k, zh // 2))


def middle(value, k):
    return send(value, lambda y, zl, x, zh, c: (y, zl, x + k, zh, c) if c == 0 else (y + k, zl, x, zh, c))


def outer(value, k):
    return send(value, lambda y, zl, x, zh, c: (y + k, zl, x, zh, c) if c == 0 else (y, zl, x + k, zh, c))


def sibling(value):
    return send(value, lambda y, zl, x, zh, c: (y, zl, x, zh, 1 - c))


def flip(value, axis, bit):
    at = AX.index(axis)

    def target(*place):
        place = list(place)
        place[at] ^= bit
        return place

    return send(value, target)


def nt(a, b):
    return lax.dot_general(a, b, (((1,), (1,)), ((), ())), preferred_element_type=f32)


def nn(a, b):
    return lax.dot_general(a, b, (((1,), (0,)), ((), ())), preferred_element_type=f32)


def tn(a, b):
    return lax.dot_general(a, b, (((0,), (0,)), ((), ())), preferred_element_type=f32)


def eye(n):
    rows = lax.broadcasted_iota(jnp.int32, (n, n), 0)
    cols = lax.broadcasted_iota(jnp.int32, (n, n), 1)
    return jnp.where(rows == cols, 1.0, 0.0).astype(bf16)


def base_body(tab, weight_t, codes, factor, offset, out, weight, code_v, factor_v, offset_v, sems):
    y = tab[T_Y]
    copies = [
        pltpu.make_async_copy(weight_t.at[:, pl.ds(pl.multiple_of(y * BLK, 128), BLK)], weight, sems.at[0]),
        pltpu.make_async_copy(codes, code_v, sems.at[1]),
        pltpu.make_async_copy(factor, factor_v, sems.at[2]),
        pltpu.make_async_copy(offset, offset_v, sems.at[3]),
    ]
    for copy in copies:
        copy.start()
    for copy in copies:
        copy.wait()
    rows = []
    for k in range(10):
        b = y * 10 + k
        code = code_v[pl.ds(b, 1), :].astype(f32)
        group = b // 8
        rows.append(factor_v[pl.ds(group, 1), :] * (code + 1.0) / 256.0 + offset_v[pl.ds(group, 1), :])
    rest = jnp.concatenate([*rows, jnp.zeros((6, COLS), f32)], 0)
    spread = lax.broadcasted_iota(jnp.int32, (16, BLK), 1) // 64
    spread = spread == lax.broadcasted_iota(jnp.int32, (16, BLK), 0)
    spread = jnp.where(spread, 1.0, 0.0).astype(bf16)
    absmax = jnp.zeros((COLS, BLK), f32)
    for _ in range(3):
        piece = rest.astype(bf16)
        rest = rest - piece.astype(f32)
        absmax = absmax + tn(piece, spread)
    out[...] = (weight[...].astype(f32) * absmax).astype(bf16)


def base_quarter(tab, weight, codes, factor, offset):
    hbm = pl.BlockSpec(memory_space=pltpu.HBM)
    return pl.pallas_call(
        base_body,
        out_shape=jax.ShapeDtypeStruct((COLS, BLK), bf16),
        in_specs=[pl.BlockSpec(memory_space=pltpu.SMEM), hbm, hbm, hbm, hbm],
        out_specs=pl.BlockSpec(memory_space=pltpu.VMEM),
        scratch_shapes=[
            pltpu.VMEM((COLS, BLK), bf16),
            pltpu.VMEM(codes.shape, jnp.int32),
            pltpu.VMEM(factor.shape, f32),
            pltpu.VMEM(offset.shape, f32),
            pltpu.SemaphoreType.DMA((4,)),
        ],
        cost_estimate=cost(0),
        compiler_params=params(16),
        name="base_quarter",
    )(tab, *(in_hbm(v) for v in (weight.T, codes, factor, offset)))


def order_body(tab, a, b, c, d, out, sems):
    copies = []
    for k, src in enumerate((a, b, c, d)):
        place = pl.multiple_of(tab[T_S + k] * COLS, 32)
        copies.append(pltpu.make_async_copy(src, out.at[pl.ds(place, COLS), :], sems.at[k]))
    for copy in copies:
        copy.start()
    for copy in copies:
        copy.wait()


def ordered(tab, blocks):
    anywhere = pl.BlockSpec(memory_space=pl.ANY)
    return pl.pallas_call(
        order_body,
        out_shape=jax.ShapeDtypeStruct((BLK, BLK), bf16),
        in_specs=[pl.BlockSpec(memory_space=pltpu.SMEM), *([anywhere] * 4)],
        out_specs=anywhere,
        scratch_shapes=[pltpu.SemaphoreType.DMA((4,))],
        cost_estimate=cost(0),
        compiler_params=params(8),
        name="ordered",
    )(tab, *blocks)


def join_body(*refs):
    *parts, out, sems = refs
    copies = [pltpu.make_async_copy(src, out.at[k], sems.at[k]) for k, src in enumerate(parts)]
    for copy in copies:
        copy.start()
    for copy in copies:
        copy.wait()


def joined(parts):
    anywhere = pl.BlockSpec(memory_space=pl.ANY)
    return pl.pallas_call(
        join_body,
        out_shape=jax.ShapeDtypeStruct((len(parts), *parts[0].shape), parts[0].dtype),
        in_specs=[anywhere] * len(parts),
        out_specs=anywhere,
        scratch_shapes=[pltpu.SemaphoreType.DMA((len(parts),))],
        cost_estimate=cost(0),
        compiler_params=params(8),
        name="joined",
    )(*parts)


def attend_body(tab, lens, queries, keys, values, out):
    d = tab[T_D]
    rows = lax.broadcasted_iota(jnp.int32, (TOK, TOK), 0)
    cols = lax.broadcasted_iota(jnp.int32, (TOK, TOK), 1)
    end = jnp.int32(0)
    row_doc = jnp.zeros((TOK, TOK), jnp.int32)
    col_doc = jnp.zeros((TOK, TOK), jnp.int32)
    for k in range(4):
        end = end + lens[d * 4 + k]
        row_doc = row_doc + jnp.where(rows >= end, 1, 0)
        col_doc = col_doc + jnp.where(cols >= end, 1, 0)
    allowed = (row_doc == col_doc) & (cols <= rows)
    for h in range(BLK // HEAD):
        at = slice(h * HEAD, (h + 1) * HEAD)
        scores = nt(queries[:, at], keys[:, at]) * (HEAD ** -0.5)
        scores = jnp.where(allowed, scores, -1e30)
        weights = jnp.exp(scores - jnp.max(scores, axis=-1, keepdims=True))
        total = jnp.sum(weights, axis=-1, keepdims=True)
        out[:, at] = (nn(weights.astype(bf16), values[:, at]) / total).astype(bf16)


def attend(tab, lens, queries, keys, values):
    spec = pl.BlockSpec((TOK, BLK), lambda i, *_: (0, i))
    return pl.pallas_call(
        attend_body,
        out_shape=jax.ShapeDtypeStruct(queries.shape, bf16),
        grid_spec=pltpu.PrefetchScalarGridSpec(
            num_scalar_prefetch=2, grid=(4,), in_specs=[spec] * 3, out_specs=spec
        ),
        cost_estimate=cost(0),
        compiler_params=params(12),
        name="attend",
    )(tab, lens, *(in_hbm(v) for v in (queries, keys, values)))


def low_body(tab, att, cot, mine, other, low_out, lg_out, down_t, up_t, keep, give):
    unit = eye(256)
    for f in range(32):
        at = tab[T_F + f]
        block = jnp.where(tab[T_C] == f % 2, mine[at], other[at])
        turned = nt(unit, jnp.concatenate([block, block], 0)).astype(bf16)
        down_t[f * DCOLS : (f + 1) * DCOLS, :] = turned[:DCOLS]
        up_t[f * COLS : (f + 1) * COLS, :] = turned[DCOLS : DCOLS + COLS]
    low = nn(att[...], down_t[...])
    low_grad = nn(cot[...], up_t[...]) * SCALE
    first = lax.broadcasted_iota(jnp.int32, (TOK, 128), 1) < 64
    none = jnp.zeros((TOK, 128), f32)
    low_a, low_b = (jnp.where(first, low, none).astype(bf16), jnp.where(first, none, low).astype(bf16))
    lg_a, lg_b = (
        jnp.where(first, low_grad, none).astype(bf16),
        jnp.where(first, none, low_grad).astype(bf16),
    )
    low_out[...] = low_a
    lg_out[...] = lg_a
    core = tab[T_C]

    def put(f, lo, hi, even, odd):
        place = tab[T_P + f]
        keep[place, lo:hi, :] = jnp.where(core == 0, even, odd)
        give[place, lo:hi, :] = jnp.where(core == 0, odd, even).astype(bf16)

    half = DCOLS // 2
    both = jnp.concatenate([lg_a, lg_b], 1)
    for i in range(4):
        got = tn(att[:, i * BLK : (i + 1) * BLK], both)
        a, b = got[:, :128], got[:, 128:]
        pair = []
        for k in range(8):
            s = k * DCOLS
            pair.append(a[s : s + half] + b[s + half : s + DCOLS])
        for k in range(0, 8, 2):
            put(i * 8 + k, 0, half, pair[k], pair[k + 1])
    both = jnp.concatenate([low_a, low_b], 1)
    for j in range(8):
        got = tn(cot[:, j * BLK : (j + 1) * BLK], both) * SCALE
        a, b = got[:, :128], got[:, 128:]
        pair = []
        for k in range(4):
            s = k * COLS
            pair.append(a[s : s + DCOLS] + b[s + DCOLS : s + COLS])
        for k in range(0, 4, 2):
            put(j * 4 + k, half, half + DCOLS, pair[k], pair[k + 1])


def low_terms(tab, att, cot, mine, other):
    vmem = pl.BlockSpec(memory_space=pltpu.VMEM)
    return pl.pallas_call(
        low_body,
        out_shape=(
            jax.ShapeDtypeStruct((TOK, 128), bf16),
            jax.ShapeDtypeStruct((TOK, 128), bf16),
            jax.ShapeDtypeStruct((32 * DCOLS, 128), bf16),
            jax.ShapeDtypeStruct((32 * COLS, 128), bf16),
            jax.ShapeDtypeStruct((16, 120, 128), f32),
            jax.ShapeDtypeStruct((16, 120, 128), bf16),
        ),
        in_specs=[pl.BlockSpec(memory_space=pltpu.SMEM), *([vmem] * 4)],
        out_specs=[vmem] * 6,
        cost_estimate=cost(4),
        compiler_params=params(16),
        name="low_terms",
    )(tab, att, cot, mine, other)


SLOTS = 4


def tiles_body(stage, counts, tab, att, cot, *refs):
    n_head = 4 if stage == 0 else 2
    head, refs = refs[:n_head], refs[n_head:]
    tiles, refs = refs[: len(counts)], refs[len(counts) :]
    places = [(a, k) for a, n in enumerate(counts) for k in range(n)]
    count = len(places)
    if stage == 3:
        out, grad, out_acc, grad_acc, out_old, grad_old, old_sems, *refs = refs
    elif stage == 2:
        out_new, grad_new, out_acc, grad_acc, new_sems, *refs = refs
    else:
        out_acc, grad_acc, *refs = refs
    buf, sems, *refs = refs

    def fetch(t):
        a, k = places[t]
        return pltpu.make_async_copy(tiles[a].at[k], buf.at[t % SLOTS], sems.at[t % SLOTS])

    for t in range(SLOTS):
        fetch(t).start()
    if stage == 2:
        out_acc[...] = head[0][...]
        grad_acc[...] = head[1][...]
    if stage == 3:
        olds = [
            pltpu.make_async_copy(head[k], ref, old_sems.at[k])
            for k, ref in enumerate((out_old, grad_old))
        ]
        for copy in olds:
            copy.start()
        out_acc[...] = jnp.zeros(out_acc.shape, f32)
        grad_acc[...] = jnp.zeros(grad_acc.shape, f32)
    if stage == 0:
        low_a, lg_a, down_t, up_t = head
        for j in range(8):
            out_acc[j] = nt(low_a[...], up_t[j * BLK : (j + 1) * BLK, :]) * SCALE
        for i in range(4):
            grad_acc[i] = nt(lg_a[...], down_t[i * BLK : (i + 1) * BLK, :])
    for t in range(count):
        j, i = tab[STAGE_AT[stage] + t], tab[STAGE_AT[stage] + count + t]
        fetch(t).wait()
        tile = buf[t % SLOTS]
        out_acc[j] = out_acc[j] + nt(att[:, pl.ds(pl.multiple_of(i * BLK, 128), BLK)], tile)
        grad_acc[i] = grad_acc[i] + nn(cot[:, pl.ds(pl.multiple_of(j * BLK, 128), BLK)], tile)
        if t + SLOTS < count:
            fetch(t + SLOTS).start()
    if stage == 2:
        news = [
            pltpu.make_async_copy(ref, (out_new, grad_new)[k], new_sems.at[k])
            for k, ref in enumerate((out_acc, grad_acc))
        ]
        for copy in news:
            copy.start()
        for copy in news:
            copy.wait()
    if stage == 3:
        out_v, grad_v, out_sems = refs
        for copy in olds:
            copy.wait()
        copies = []
        for acc, old, full, ref, base in (
            (out_acc, out_old, out_v, out, 0),
            (grad_acc, grad_old, grad_v, grad, 8),
        ):
            for k in range(acc.shape[0]):
                at = slice(k * BLK, (k + 1) * BLK)
                full[:, at] = (acc[k] + old[k]).astype(bf16)
                copies.append(pltpu.make_async_copy(full.at[:, at], ref.at[:, at], out_sems.at[base + k]))
                copies[-1].start()
        for copy in copies:
            copy.wait()


def add_tiles(stage, tab, att, cot, head, arrays):
    vmem = pl.BlockSpec(memory_space=pltpu.VMEM)
    hbm = pl.BlockSpec(memory_space=pltpu.HBM)
    acc = [(8, TOK, BLK), (4, TOK, BLK)]
    outs, specs = [jax.ShapeDtypeStruct(s, f32) for s in acc], [vmem, vmem]
    scratch = [pltpu.VMEM((SLOTS, BLK, BLK), bf16), pltpu.SemaphoreType.DMA((SLOTS,))]
    if stage == 3:
        wide = [(TOK, 8 * BLK), (TOK, 4 * BLK)]
        outs, specs = [jax.ShapeDtypeStruct(s, bf16) for s in wide], [hbm, hbm]
        scratch = [pltpu.VMEM(s, f32) for s in acc * 2] + [pltpu.SemaphoreType.DMA((2,))] + scratch
        scratch += [pltpu.VMEM(s, bf16) for s in wide] + [pltpu.SemaphoreType.DMA((12,))]
    if stage == 2:
        outs, specs = [pltpu.HBM(s, f32) for s in acc], [hbm, hbm]
        scratch = [pltpu.VMEM(s, f32) for s in acc] + [pltpu.SemaphoreType.DMA((2,))] + scratch
    if stage == 3:
        head = [in_hbm(h) for h in head]
    head_spec = hbm if stage == 3 else vmem
    return pl.pallas_call(
        lambda *refs: tiles_body(stage, [a.shape[0] for a in arrays], *refs),
        out_shape=outs,
        in_specs=[pl.BlockSpec(memory_space=pltpu.SMEM), vmem, vmem, *([head_spec] * len(head)), *([hbm] * len(arrays))],
        out_specs=specs,
        scratch_shapes=scratch,
        input_output_aliases={} if stage != 1 else {3: 0, 4: 1},
        cost_estimate=cost(0),
        compiler_params=params(28 if stage == 3 else 16),
        name=f"tiles_{stage}",
    )(tab, att, cot, *head, *arrays)


def per_device(
    table,
    queries,
    keys,
    values,
    lengths,
    weight,
    codes,
    factor,
    offset,
    down,
    up,
    cot,
):
    tab = table.reshape(-1)
    lens = lengths.reshape(-1)

    tie = lax.optimization_barrier

    def along(value, axis, k):
        at = AX.index(axis)
        return send(value, lambda *to: tuple(v + (k if n == at else 0) for n, v in enumerate(to)))

    def scattered(part, axis, bit, n, kind):
        return part[:n] + flip(part[n:].astype(kind), axis, bit).astype(f32)

    adapters = jnp.concatenate([down, up, jnp.zeros((64, 16), bf16)], 1)
    adapters = jnp.stack([adapters, *(along(adapters, "zh", -k) for k in REL[1:])])
    quarter = base_quarter(tab, weight, codes, factor, offset)
    quarter, adapters, queries = tie((quarter, adapters, queries))
    rounds = [z_round(quarter, k) for k in range(4)]
    adapters = [adapters, *(along(adapters, "x", -k) for k in REL[1:])]
    att = attend(tab, lens, queries, keys, values)
    rounds, att, adapters = tie((rounds, att, adapters))
    own = ordered(tab, rounds)
    mine = jnp.concatenate(adapters, 0)

    less, more, far = middle(own, 1), middle(own, -1), middle(own, 2)
    low = low_terms(tab, att, cot, mine, sibling(mine))
    less, more, far, low = tie((less, more, far, tuple(low)))
    low_a, lg_a, down_t, up_t, keep, give = low
    row = joined([own, less, more, far])

    all_less, all_more = outer(row, 1), outer(row, -1)
    give, row = tie((give, row))
    part = keep + flip(give, "c", 1).astype(f32)
    part = scattered(part, "zh", 1, 8, bf16)
    part = scattered(part, "zh", 2, 4, bf16)
    sums = add_tiles(0, tab, att, cot, (low_a, lg_a, down_t, up_t), [row, sibling(row)])
    part, sums = tie((part, tuple(sums)))
    a, b, c = (flip(part[k], "x", k) for k in (1, 2, 3))
    part = (part[0] + a) + (b + c)
    all_less, all_more, part, sums = tie((all_less, all_more, part, sums))

    far_a, far_b = outer(all_less[:2], 1), outer(all_more[2:], -1)
    tiles = [all_less, all_more]
    sums = add_tiles(1, tab, att, cot, sums, tiles)
    sums = add_tiles(2, tab, att, cot, sums, [sibling(t) for t in tiles])
    part, sums = tie((part, tuple(sums)))
    a, b, c = (flip(part, "y", k) for k in (1, 2, 3))
    part = (part + a) + (b + c)
    far_a, far_b, part, sums = tie((far_a, far_b, part, sums))
    tiles = [far_a, far_b]
    tiles_other = [sibling(t) for t in tiles]
    part = part + flip(part, "zl", 1)
    out, grad = add_tiles(3, tab, att, cot, sums, [*tiles, *tiles_other])
    half = DCOLS // 2
    down_grad = jnp.concatenate([part[:half, :64], part[:half, 64:]], 0).T
    up_grad = jnp.concatenate([part[half:, :64], part[half:, 64:]], 0).T
    return out, grad, down_grad, up_grad


def solution(mesh):
    fine = Mesh(np.asarray(mesh.devices).reshape(DIMS), AX)
    tokens, owners = ("y", "zl", "x", "zh", "c"), ("x", "zh", "c")
    table = device_table()
    mapped = jax.shard_map(
        per_device,
        mesh=fine,
        in_specs=(
            P(tokens, None),
            P(tokens, None),
            P(tokens, None),
            P(tokens, None),
            P(owners, None, None),
            P(None, owners),
            P(None, owners),
            P(None, owners),
            P(None, owners),
            P(None, owners),
            P(None, owners),
            P(tokens, None),
        ),
        out_specs=(
            P(tokens, None),
            P(tokens, None),
            P(None, owners),
            P(None, owners),
        ),
        check_vma=False,
    )
    return lambda *args: mapped(jnp.asarray(table), *args)
```

```python
import jax
import jax.numpy as jnp
import numpy as np
from jax import lax
from jax.experimental import pallas as pl
from jax.experimental.pallas import tpu as pltpu
from jax.sharding import Mesh
from jax.sharding import PartitionSpec as P

HEAD = 128
TOK = 192
BLK = 640
COLS = 160
DCOLS = 80
SCALE = 0.25
AX = ("y", "zl", "x", "zh", "c")
DIMS = (4, 2, 4, 4, 2)
REL = (0, -1, 1, 2)


def cost(us):
    return pl.CostEstimate(flops=int(us * 1.15e9) + 1, bytes_accessed=1, transcendentals=0)


bf16 = jnp.bfloat16
f32 = jnp.float32

T_Y, T_D, T_S, T_F, T_C, T_P, T_B, T_TILES = 0, 1, 2, 6, 38, 40, 72, 104
STAGE_AT = (104, 120, 136, 152)
T_LEN = 168


def params(mib=48):
    return pltpu.CompilerParams(vmem_limit_bytes=mib << 20)


def in_hbm(value):
    return pltpu.with_memory_space_constraint(value, pltpu.HBM)


def coords():
    return [np.unravel_index(d, DIMS) for d in range(256)]


def device_table():
    rows = np.zeros((256, T_LEN), np.int32)
    for n, (y, zl, x, zh, c) in enumerate(coords()):
        r = rows[n]
        r[T_Y], r[T_D], r[T_C] = y, y * 2 + zl, c
        for k in range(4):
            r[T_S + k] = (zh - k) % 4
        for f in range(32):
            fx, fz, fc = f // 8, (f // 2) % 4, f % 2
            r[T_F + f] = [(x + k) % 4 for k in REL].index(fx) * 4 + [(zh + k) % 4 for k in REL].index(fz)
            dz = fz ^ zh
            r[T_P + f] = (dz % 2) * 8 + (dz // 2) * 4 + (fx ^ x)

        def tiles(own, v, us):
            kind = c if own else 1 - c
            if kind == 0:
                return [(2 * ((x + u) % 4), (y + v) % 4) for u in us]
            return [(2 * ((x + v) % 4) + 1, (y + u) % 4) for u in us]

        both = lambda pairs: [
            t for own in (True, False) for u, v in pairs for t in tiles(own, v, (u,))
        ]
        nears = [(u, v) for v in (-1, 1) for u in REL]
        stages = (
            both([(u, 0) for u in REL]),
            [t for u, v in nears for t in tiles(True, v, (u,))],
            [t for u, v in nears for t in tiles(False, v, (u,))],
            both([(u, 2) for u in REL]),
        )
        at = T_TILES
        for stage in stages:
            for k, (j, i) in enumerate(stage):
                r[at + k], r[at + len(stage) + k] = j, i
            at += 2 * len(stage)
    return rows


def index_of(y, zl, x, zh, c):
    return int(np.ravel_multi_index((y % 4, zl, x % 4, zh % 4, c), DIMS))


def send(value, target):
    pairs = [(n, index_of(*target(*(int(v) for v in at)))) for n, at in enumerate(coords())]
    return lax.ppermute(value, AX, pairs)


def z_round(value, k):
    return send(value, lambda y, zl, x, zh, c: (y, zl, x, 2 * (zh % 2) + c + k, zh // 2))


def middle(value, k):
    return send(value, lambda y, zl, x, zh, c: (y, zl, x + k, zh, c) if c == 0 else (y + k, zl, x, zh, c))


def outer(value, k):
    return send(value, lambda y, zl, x, zh, c: (y + k, zl, x, zh, c) if c == 0 else (y, zl, x + k, zh, c))


def sibling(value):
    return send(value, lambda y, zl, x, zh, c: (y, zl, x, zh, 1 - c))


def flip(value, axis, bit):
    at = AX.index(axis)

    def target(*place):
        place = list(place)
        place[at] ^= bit
        return place

    return send(value, target)


def nt(a, b):
    return lax.dot_general(a, b, (((1,), (1,)), ((), ())), preferred_element_type=f32)


def nn(a, b):
    return lax.dot_general(a, b, (((1,), (0,)), ((), ())), preferred_element_type=f32)


def tn(a, b):
    return lax.dot_general(a, b, (((0,), (0,)), ((), ())), preferred_element_type=f32)


def eye(n):
    rows = lax.broadcasted_iota(jnp.int32, (n, n), 0)
    cols = lax.broadcasted_iota(jnp.int32, (n, n), 1)
    return jnp.where(rows == cols, 1.0, 0.0).astype(bf16)


def base_body(tab, weight_t, codes, factor, offset, out, weight, code_v, factor_v, offset_v, sems):
    y = tab[T_Y]
    copies = [
        pltpu.make_async_copy(weight_t.at[:, pl.ds(pl.multiple_of(y * BLK, 128), BLK)], weight, sems.at[0]),
        pltpu.make_async_copy(codes, code_v, sems.at[1]),
        pltpu.make_async_copy(factor, factor_v, sems.at[2]),
        pltpu.make_async_copy(offset, offset_v, sems.at[3]),
    ]
    for copy in copies:
        copy.start()
    for copy in copies:
        copy.wait()
    rows = []
    for k in range(10):
        b = y * 10 + k
        code = code_v[pl.ds(b, 1), :].astype(f32)
        group = b // 8
        rows.append(factor_v[pl.ds(group, 1), :] * (code + 1.0) / 256.0 + offset_v[pl.ds(group, 1), :])
    rest = jnp.concatenate([*rows, jnp.zeros((6, COLS), f32)], 0)
    spread = lax.broadcasted_iota(jnp.int32, (16, BLK), 1) // 64
    spread = spread == lax.broadcasted_iota(jnp.int32, (16, BLK), 0)
    spread = jnp.where(spread, 1.0, 0.0).astype(bf16)
    absmax = jnp.zeros((COLS, BLK), f32)
    for _ in range(3):
        piece = rest.astype(bf16)
        rest = rest - piece.astype(f32)
        absmax = absmax + tn(piece, spread)
    out[...] = (weight[...].astype(f32) * absmax).astype(bf16)


def base_quarter(tab, weight, codes, factor, offset):
    hbm = pl.BlockSpec(memory_space=pltpu.HBM)
    return pl.pallas_call(
        base_body,
        out_shape=jax.ShapeDtypeStruct((COLS, BLK), bf16),
        in_specs=[pl.BlockSpec(memory_space=pltpu.SMEM), hbm, hbm, hbm, hbm],
        out_specs=pl.BlockSpec(memory_space=pltpu.VMEM),
        scratch_shapes=[
            pltpu.VMEM((COLS, BLK), bf16),
            pltpu.VMEM(codes.shape, jnp.int32),
            pltpu.VMEM(factor.shape, f32),
            pltpu.VMEM(offset.shape, f32),
            pltpu.SemaphoreType.DMA((4,)),
        ],
        cost_estimate=cost(0),
        compiler_params=params(16),
        name="base_quarter",
    )(tab, *(in_hbm(v) for v in (weight.T, codes, factor, offset)))


def order_body(tab, a, b, c, d, out, sems):
    copies = []
    for k, src in enumerate((a, b, c, d)):
        place = pl.multiple_of(tab[T_S + k] * COLS, 32)
        copies.append(pltpu.make_async_copy(src, out.at[pl.ds(place, COLS), :], sems.at[k]))
    for copy in copies:
        copy.start()
    for copy in copies:
        copy.wait()


def ordered(tab, blocks):
    anywhere = pl.BlockSpec(memory_space=pl.ANY)
    return pl.pallas_call(
        order_body,
        out_shape=jax.ShapeDtypeStruct((BLK, BLK), bf16),
        in_specs=[pl.BlockSpec(memory_space=pltpu.SMEM), *([anywhere] * 4)],
        out_specs=anywhere,
        scratch_shapes=[pltpu.SemaphoreType.DMA((4,))],
        cost_estimate=cost(0),
        compiler_params=params(8),
        name="ordered",
    )(tab, *blocks)


def join_body(*refs):
    *parts, out, sems = refs
    copies = [pltpu.make_async_copy(src, out.at[k], sems.at[k]) for k, src in enumerate(parts)]
    for copy in copies:
        copy.start()
    for copy in copies:
        copy.wait()


def joined(parts):
    anywhere = pl.BlockSpec(memory_space=pl.ANY)
    return pl.pallas_call(
        join_body,
        out_shape=jax.ShapeDtypeStruct((len(parts), *parts[0].shape), parts[0].dtype),
        in_specs=[anywhere] * len(parts),
        out_specs=anywhere,
        scratch_shapes=[pltpu.SemaphoreType.DMA((len(parts),))],
        cost_estimate=cost(0),
        compiler_params=params(8),
        name="joined",
    )(*parts)


def attend_body(tab, lens, queries, keys, values, out):
    d = tab[T_D]
    rows = lax.broadcasted_iota(jnp.int32, (TOK, TOK), 0)
    cols = lax.broadcasted_iota(jnp.int32, (TOK, TOK), 1)
    end = jnp.int32(0)
    row_doc = jnp.zeros((TOK, TOK), jnp.int32)
    col_doc = jnp.zeros((TOK, TOK), jnp.int32)
    for k in range(4):
        end = end + lens[d * 4 + k]
        row_doc = row_doc + jnp.where(rows >= end, 1, 0)
        col_doc = col_doc + jnp.where(cols >= end, 1, 0)
    allowed = (row_doc == col_doc) & (cols <= rows)
    for h in range(BLK // HEAD):
        at = slice(h * HEAD, (h + 1) * HEAD)
        scores = nt(queries[:, at], keys[:, at]) * (HEAD ** -0.5)
        scores = jnp.where(allowed, scores, -1e30)
        weights = jnp.exp(scores - jnp.max(scores, axis=-1, keepdims=True))
        total = jnp.sum(weights, axis=-1, keepdims=True)
        out[:, at] = (nn(weights.astype(bf16), values[:, at]) / total).astype(bf16)


def attend(tab, lens, queries, keys, values):
    spec = pl.BlockSpec((TOK, BLK), lambda i, *_: (0, i))
    return pl.pallas_call(
        attend_body,
        out_shape=jax.ShapeDtypeStruct(queries.shape, bf16),
        grid_spec=pltpu.PrefetchScalarGridSpec(
            num_scalar_prefetch=2, grid=(4,), in_specs=[spec] * 3, out_specs=spec
        ),
        cost_estimate=cost(0),
        compiler_params=params(12),
        name="attend",
    )(tab, lens, *(in_hbm(v) for v in (queries, keys, values)))


def low_body(tab, att, cot, mine, other, low_out, lg_out, down_t, up_t, keep, give):
    unit = eye(256)
    for f in range(32):
        at = tab[T_F + f]
        block = jnp.where(tab[T_C] == f % 2, mine[at], other[at])
        turned = nt(unit, jnp.concatenate([block, block], 0)).astype(bf16)
        down_t[f * DCOLS : (f + 1) * DCOLS, :] = turned[:DCOLS]
        up_t[f * COLS : (f + 1) * COLS, :] = turned[DCOLS : DCOLS + COLS]
    low = nn(att[...], down_t[...])
    low_grad = nn(cot[...], up_t[...]) * SCALE
    first = lax.broadcasted_iota(jnp.int32, (TOK, 128), 1) < 64
    none = jnp.zeros((TOK, 128), f32)
    low_a, low_b = (jnp.where(first, low, none).astype(bf16), jnp.where(first, none, low).astype(bf16))
    lg_a, lg_b = (
        jnp.where(first, low_grad, none).astype(bf16),
        jnp.where(first, none, low_grad).astype(bf16),
    )
    low_out[...] = low_a
    lg_out[...] = lg_a
    core = tab[T_C]

    def put(f, lo, hi, even, odd):
        place = tab[T_P + f]
        keep[place, lo:hi, :] = jnp.where(core == 0, even, odd)
        give[place, lo:hi, :] = jnp.where(core == 0, odd, even).astype(bf16)

    half = DCOLS // 2
    both = jnp.concatenate([lg_a, lg_b], 1)
    for i in range(4):
        got = tn(att[:, i * BLK : (i + 1) * BLK], both)
        a, b = got[:, :128], got[:, 128:]
        pair = []
        for k in range(8):
            s = k * DCOLS
            pair.append(a[s : s + half] + b[s + half : s + DCOLS])
        for k in range(0, 8, 2):
            put(i * 8 + k, 0, half, pair[k], pair[k + 1])
    both = jnp.concatenate([low_a, low_b], 1)
    for j in range(8):
        got = tn(cot[:, j * BLK : (j + 1) * BLK], both) * SCALE
        a, b = got[:, :128], got[:, 128:]
        pair = []
        for k in range(4):
            s = k * COLS
            pair.append(a[s : s + DCOLS] + b[s + DCOLS : s + COLS])
        for k in range(0, 4, 2):
            put(j * 4 + k, half, half + DCOLS, pair[k], pair[k + 1])


def low_terms(tab, att, cot, mine, other):
    vmem = pl.BlockSpec(memory_space=pltpu.VMEM)
    return pl.pallas_call(
        low_body,
        out_shape=(
            jax.ShapeDtypeStruct((TOK, 128), bf16),
            jax.ShapeDtypeStruct((TOK, 128), bf16),
            jax.ShapeDtypeStruct((32 * DCOLS, 128), bf16),
            jax.ShapeDtypeStruct((32 * COLS, 128), bf16),
            jax.ShapeDtypeStruct((16, 120, 128), f32),
            jax.ShapeDtypeStruct((16, 120, 128), bf16),
        ),
        in_specs=[pl.BlockSpec(memory_space=pltpu.SMEM), *([vmem] * 4)],
        out_specs=[vmem] * 6,
        cost_estimate=cost(4),
        compiler_params=params(16),
        name="low_terms",
    )(tab, att, cot, mine, other)


SLOTS = 4


def tiles_body(stage, counts, tab, att, cot, *refs):
    n_head = 4 if stage == 0 else 2
    head, refs = refs[:n_head], refs[n_head:]
    tiles, refs = refs[: len(counts)], refs[len(counts) :]
    places = [(a, k) for a, n in enumerate(counts) for k in range(n)]
    count = len(places)
    if stage == 3:
        out, grad, out_acc, grad_acc, out_old, grad_old, old_sems, *refs = refs
    elif stage == 2:
        out_new, grad_new, out_acc, grad_acc, new_sems, *refs = refs
    else:
        out_acc, grad_acc, *refs = refs
    buf, sems, *refs = refs

    def fetch(t):
        a, k = places[t]
        return pltpu.make_async_copy(tiles[a].at[k], buf.at[t % SLOTS], sems.at[t % SLOTS])

    for t in range(SLOTS):
        fetch(t).start()
    if stage == 2:
        out_acc[...] = head[0][...]
        grad_acc[...] = head[1][...]
    if stage == 3:
        olds = [
            pltpu.make_async_copy(head[k], ref, old_sems.at[k])
            for k, ref in enumerate((out_old, grad_old))
        ]
        for copy in olds:
            copy.start()
        out_acc[...] = jnp.zeros(out_acc.shape, f32)
        grad_acc[...] = jnp.zeros(grad_acc.shape, f32)
    if stage == 0:
        low_a, lg_a, down_t, up_t = head
        for j in range(8):
            out_acc[j] = nt(low_a[...], up_t[j * BLK : (j + 1) * BLK, :]) * SCALE
        for i in range(4):
            grad_acc[i] = nt(lg_a[...], down_t[i * BLK : (i + 1) * BLK, :])
    for t in range(count):
        j, i = tab[STAGE_AT[stage] + t], tab[STAGE_AT[stage] + count + t]
        fetch(t).wait()
        tile = buf[t % SLOTS]
        out_acc[j] = out_acc[j] + nt(att[:, pl.ds(pl.multiple_of(i * BLK, 128), BLK)], tile)
        grad_acc[i] = grad_acc[i] + nn(cot[:, pl.ds(pl.multiple_of(j * BLK, 128), BLK)], tile)
        if t + SLOTS < count:
            fetch(t + SLOTS).start()
    if stage == 2:
        news = [
            pltpu.make_async_copy(ref, (out_new, grad_new)[k], new_sems.at[k])
            for k, ref in enumerate((out_acc, grad_acc))
        ]
        for copy in news:
            copy.start()
        for copy in news:
            copy.wait()
    if stage == 3:
        out_v, grad_v, out_sems = refs
        for copy in olds:
            copy.wait()
        copies = []
        for acc, old, full, ref, base in (
            (out_acc, out_old, out_v, out, 0),
            (grad_acc, grad_old, grad_v, grad, 8),
        ):
            for k in range(acc.shape[0]):
                at = slice(k * BLK, (k + 1) * BLK)
                full[:, at] = (acc[k] + old[k]).astype(bf16)
                copies.append(pltpu.make_async_copy(full.at[:, at], ref.at[:, at], out_sems.at[base + k]))
                copies[-1].start()
        for copy in copies:
            copy.wait()


def add_tiles(stage, tab, att, cot, head, arrays):
    vmem = pl.BlockSpec(memory_space=pltpu.VMEM)
    hbm = pl.BlockSpec(memory_space=pltpu.HBM)
    acc = [(8, TOK, BLK), (4, TOK, BLK)]
    outs, specs = [jax.ShapeDtypeStruct(s, f32) for s in acc], [vmem, vmem]
    scratch = [pltpu.VMEM((SLOTS, BLK, BLK), bf16), pltpu.SemaphoreType.DMA((SLOTS,))]
    if stage == 3:
        wide = [(TOK, 8 * BLK), (TOK, 4 * BLK)]
        outs, specs = [jax.ShapeDtypeStruct(s, bf16) for s in wide], [hbm, hbm]
        scratch = [pltpu.VMEM(s, f32) for s in acc * 2] + [pltpu.SemaphoreType.DMA((2,))] + scratch
        scratch += [pltpu.VMEM(s, bf16) for s in wide] + [pltpu.SemaphoreType.DMA((12,))]
    if stage == 2:
        outs, specs = [pltpu.HBM(s, f32) for s in acc], [hbm, hbm]
        scratch = [pltpu.VMEM(s, f32) for s in acc] + [pltpu.SemaphoreType.DMA((2,))] + scratch
    if stage == 3:
        head = [in_hbm(h) for h in head]
    head_spec = hbm if stage == 3 else vmem
    return pl.pallas_call(
        lambda *refs: tiles_body(stage, [a.shape[0] for a in arrays], *refs),
        out_shape=outs,
        in_specs=[pl.BlockSpec(memory_space=pltpu.SMEM), vmem, vmem, *([head_spec] * len(head)), *([hbm] * len(arrays))],
        out_specs=specs,
        scratch_shapes=scratch,
        input_output_aliases={} if stage != 1 else {3: 0, 4: 1},
        cost_estimate=cost(8 if stage == 0 else 0),
        compiler_params=params(28 if stage == 3 else 16),
        name=f"tiles_{stage}",
    )(tab, att, cot, *head, *arrays)


def per_device(
    table,
    queries,
    keys,
    values,
    lengths,
    weight,
    codes,
    factor,
    offset,
    down,
    up,
    cot,
):
    tab = table.reshape(-1)
    lens = lengths.reshape(-1)

    tie = lax.optimization_barrier

    def along(value, axis, k):
        at = AX.index(axis)
        return send(value, lambda *to: tuple(v + (k if n == at else 0) for n, v in enumerate(to)))

    def scattered(part, axis, bit, n, kind):
        return part[:n] + flip(part[n:].astype(kind), axis, bit).astype(f32)

    adapters = jnp.concatenate([down, up, jnp.zeros((64, 16), bf16)], 1)
    adapters = jnp.stack([adapters, *(along(adapters, "zh", -k) for k in REL[1:])])
    quarter = base_quarter(tab, weight, codes, factor, offset)
    quarter, queries = tie((quarter, queries))
    rounds = [z_round(quarter, k) for k in range(4)]
    rounds[0], queries = tie((rounds[0], queries))
    att = attend(tab, lens, queries, keys, values)
    adapters, att = tie((adapters, att))
    adapters = [adapters, *(along(adapters, "x", -k) for k in REL[1:])]
    rounds, att, adapters = tie((rounds, att, adapters))
    own = ordered(tab, rounds)
    own, adapters = tie((own, adapters))
    mine = joined(adapters).reshape(16, 64, 256)

    less, more, far = middle(own, 1), middle(own, -1), middle(own, 2)
    low_a, lg_a, down_t, up_t, keep, give = low_terms(tab, att, cot, mine, sibling(mine))
    part = keep + flip(give, "c", 1).astype(f32)
    less, more, far, part = tie((less, more, far, part))
    row = joined([own, less, more, far])

    all_less, all_more = outer(row, 1), outer(row, -1)
    part, row = tie((part, row))
    kept, got = part[:8], flip(part[8:].astype(bf16), "zh", 1)
    sums = add_tiles(0, tab, att, cot, (low_a, lg_a, down_t, up_t), [row, sibling(row)])
    got, sums = tie((got, tuple(sums)))
    part = scattered(kept + got.astype(f32), "zh", 2, 4, bf16)
    part = part + flip(part, "zl", 1)
    a, b, c = (flip(part[k], "x", k) for k in (1, 2, 3))
    part = (part[0] + a) + (b + c)
    all_less, all_more, part, sums = tie((all_less, all_more, part, sums))

    far_a, far_b = outer(all_less[:2], 1), outer(all_more[2:], -1)
    a, b, c = (flip(part, "y", k) for k in (1, 2, 3))
    tiles = [all_less, all_more]
    sums = add_tiles(1, tab, att, cot, sums, tiles)
    sums = add_tiles(2, tab, att, cot, sums, [sibling(t) for t in tiles])
    a, b, c, sums = tie((a, b, c, tuple(sums)))
    part = (part + a) + (b + c)
    far_a, far_b, part, sums = tie((far_a, far_b, part, sums))
    tiles = [far_a, far_b]
    out, grad = add_tiles(3, tab, att, cot, sums, [*tiles, *(sibling(t) for t in tiles)])
    half = DCOLS // 2
    down_grad = jnp.concatenate([part[:half, :64], part[:half, 64:]], 0).T
    up_grad = jnp.concatenate([part[half:, :64], part[half:, 64:]], 0).T
    return out, grad, down_grad, up_grad


def solution(mesh):
    fine = Mesh(np.asarray(mesh.devices).reshape(DIMS), AX)
    tokens, owners = ("y", "zl", "x", "zh", "c"), ("x", "zh", "c")
    table = device_table()
    mapped = jax.shard_map(
        per_device,
        mesh=fine,
        in_specs=(
            P(tokens, None),
            P(tokens, None),
            P(tokens, None),
            P(tokens, None),
            P(owners, None, None),
            P(None, owners),
            P(None, owners),
            P(None, owners),
            P(None, owners),
            P(None, owners),
            P(None, owners),
            P(tokens, None),
        ),
        out_specs=(
            P(tokens, None),
            P(tokens, None),
            P(None, owners),
            P(None, owners),
        ),
        check_vma=False,
    )
    return lambda *args: mapped(jnp.asarray(table), *args)
```

```python
import jax
import jax.numpy as jnp
import numpy as np
from jax import lax
from jax.experimental import pallas as pl
from jax.experimental.pallas import tpu as pltpu
from jax.sharding import Mesh
from jax.sharding import PartitionSpec as P

HEAD = 128
TOK = 192
BLK = 640
COLS = 160
DCOLS = 80
SCALE = 0.25
AX = ("y", "zl", "x", "zh", "c")
DIMS = (4, 2, 4, 4, 2)
REL = (0, -1, 1, 2)


def cost(us):
    return pl.CostEstimate(flops=int(us * 1.15e9) + 1, bytes_accessed=1, transcendentals=0)


bf16 = jnp.bfloat16
f32 = jnp.float32

T_Y, T_D, T_S, T_F, T_C, T_P, T_B, T_TILES = 0, 1, 2, 6, 38, 40, 72, 104
STAGE_AT = (104, 120, 136, 152)
T_LEN = 168


def params(mib=48):
    return pltpu.CompilerParams(vmem_limit_bytes=mib << 20)


def in_hbm(value):
    return pltpu.with_memory_space_constraint(value, pltpu.HBM)


def coords():
    return [np.unravel_index(d, DIMS) for d in range(256)]


def device_table():
    rows = np.zeros((256, T_LEN), np.int32)
    for n, (y, zl, x, zh, c) in enumerate(coords()):
        r = rows[n]
        r[T_Y], r[T_D], r[T_C] = y, y * 2 + zl, c
        for k in range(4):
            r[T_S + k] = (zh - k) % 4
        for f in range(32):
            fx, fz, fc = f // 8, (f // 2) % 4, f % 2
            r[T_F + f] = [(x + k) % 4 for k in REL].index(fx) * 4 + [(zh + k) % 4 for k in REL].index(fz)
            dz = fz ^ zh
            r[T_P + f] = (dz % 2) * 8 + (dz // 2) * 4 + (fx ^ x)

        def tiles(own, v, us):
            kind = c if own else 1 - c
            if kind == 0:
                return [(2 * ((x + u) % 4), (y + v) % 4) for u in us]
            return [(2 * ((x + v) % 4) + 1, (y + u) % 4) for u in us]

        both = lambda pairs: [
            t for own in (True, False) for u, v in pairs for t in tiles(own, v, (u,))
        ]
        nears = [(u, v) for v in (-1, 1) for u in REL]
        stages = (
            both([(u, 0) for u in REL]),
            [t for u, v in nears for t in tiles(True, v, (u,))],
            [t for u, v in nears for t in tiles(False, v, (u,))],
            both([(u, 2) for u in REL]),
        )
        at = T_TILES
        for stage in stages:
            for k, (j, i) in enumerate(stage):
                r[at + k], r[at + len(stage) + k] = j, i
            at += 2 * len(stage)
    return rows


def index_of(y, zl, x, zh, c):
    return int(np.ravel_multi_index((y % 4, zl, x % 4, zh % 4, c), DIMS))


def send(value, target):
    pairs = [(n, index_of(*target(*(int(v) for v in at)))) for n, at in enumerate(coords())]
    return lax.ppermute(value, AX, pairs)


def z_round(value, k):
    return send(value, lambda y, zl, x, zh, c: (y, zl, x, 2 * (zh % 2) + c + k, zh // 2))


def middle(value, k):
    return send(value, lambda y, zl, x, zh, c: (y, zl, x + k, zh, c) if c == 0 else (y + k, zl, x, zh, c))


def outer(value, k):
    return send(value, lambda y, zl, x, zh, c: (y + k, zl, x, zh, c) if c == 0 else (y, zl, x + k, zh, c))


def sibling(value):
    return send(value, lambda y, zl, x, zh, c: (y, zl, x, zh, 1 - c))


def flip(value, axis, bit):
    at = AX.index(axis)

    def target(*place):
        place = list(place)
        place[at] ^= bit
        return place

    return send(value, target)


def nt(a, b):
    return lax.dot_general(a, b, (((1,), (1,)), ((), ())), preferred_element_type=f32)


def nn(a, b):
    return lax.dot_general(a, b, (((1,), (0,)), ((), ())), preferred_element_type=f32)


def tn(a, b):
    return lax.dot_general(a, b, (((0,), (0,)), ((), ())), preferred_element_type=f32)


def eye(n):
    rows = lax.broadcasted_iota(jnp.int32, (n, n), 0)
    cols = lax.broadcasted_iota(jnp.int32, (n, n), 1)
    return jnp.where(rows == cols, 1.0, 0.0).astype(bf16)


def base_body(tab, weight_t, codes, factor, offset, out, weight, code_v, factor_v, offset_v, sems):
    y = tab[T_Y]
    copies = [
        pltpu.make_async_copy(weight_t.at[:, pl.ds(pl.multiple_of(y * BLK, 128), BLK)], weight, sems.at[0]),
        pltpu.make_async_copy(codes, code_v, sems.at[1]),
        pltpu.make_async_copy(factor, factor_v, sems.at[2]),
        pltpu.make_async_copy(offset, offset_v, sems.at[3]),
    ]
    for copy in copies:
        copy.start()
    for copy in copies:
        copy.wait()
    rows = []
    for k in range(10):
        b = y * 10 + k
        code = code_v[pl.ds(b, 1), :].astype(f32)
        group = b // 8
        rows.append(factor_v[pl.ds(group, 1), :] * (code + 1.0) / 256.0 + offset_v[pl.ds(group, 1), :])
    rest = jnp.concatenate([*rows, jnp.zeros((6, COLS), f32)], 0)
    spread = lax.broadcasted_iota(jnp.int32, (16, BLK), 1) // 64
    spread = spread == lax.broadcasted_iota(jnp.int32, (16, BLK), 0)
    spread = jnp.where(spread, 1.0, 0.0).astype(bf16)
    absmax = jnp.zeros((COLS, BLK), f32)
    for _ in range(3):
        piece = rest.astype(bf16)
        rest = rest - piece.astype(f32)
        absmax = absmax + tn(piece, spread)
    out[...] = (weight[...].astype(f32) * absmax).astype(bf16)


def base_quarter(tab, weight, codes, factor, offset):
    hbm = pl.BlockSpec(memory_space=pltpu.HBM)
    return pl.pallas_call(
        base_body,
        out_shape=jax.ShapeDtypeStruct((COLS, BLK), bf16),
        in_specs=[pl.BlockSpec(memory_space=pltpu.SMEM), hbm, hbm, hbm, hbm],
        out_specs=pl.BlockSpec(memory_space=pltpu.VMEM),
        scratch_shapes=[
            pltpu.VMEM((COLS, BLK), bf16),
            pltpu.VMEM(codes.shape, jnp.int32),
            pltpu.VMEM(factor.shape, f32),
            pltpu.VMEM(offset.shape, f32),
            pltpu.SemaphoreType.DMA((4,)),
        ],
        cost_estimate=cost(0),
        compiler_params=params(16),
        name="base_quarter",
    )(tab, *(in_hbm(v) for v in (weight.T, codes, factor, offset)))


def order_body(tab, a, b, c, d, out, sems):
    copies = []
    for k, src in enumerate((a, b, c, d)):
        place = pl.multiple_of(tab[T_S + k] * COLS, 32)
        copies.append(pltpu.make_async_copy(src, out.at[pl.ds(place, COLS), :], sems.at[k]))
    for copy in copies:
        copy.start()
    for copy in copies:
        copy.wait()


def ordered(tab, blocks):
    anywhere = pl.BlockSpec(memory_space=pl.ANY)
    return pl.pallas_call(
        order_body,
        out_shape=jax.ShapeDtypeStruct((BLK, BLK), bf16),
        in_specs=[pl.BlockSpec(memory_space=pltpu.SMEM), *([anywhere] * 4)],
        out_specs=anywhere,
        scratch_shapes=[pltpu.SemaphoreType.DMA((4,))],
        cost_estimate=cost(0),
        compiler_params=params(8),
        name="ordered",
    )(tab, *blocks)


def join_body(*refs):
    *parts, out, sems = refs
    copies = [pltpu.make_async_copy(src, out.at[k], sems.at[k]) for k, src in enumerate(parts)]
    for copy in copies:
        copy.start()
    for copy in copies:
        copy.wait()


def joined(parts):
    anywhere = pl.BlockSpec(memory_space=pl.ANY)
    return pl.pallas_call(
        join_body,
        out_shape=jax.ShapeDtypeStruct((len(parts), *parts[0].shape), parts[0].dtype),
        in_specs=[anywhere] * len(parts),
        out_specs=anywhere,
        scratch_shapes=[pltpu.SemaphoreType.DMA((len(parts),))],
        cost_estimate=cost(0),
        compiler_params=params(8),
        name="joined",
    )(*parts)


def attend_body(tab, lens, queries, keys, values, out):
    d = tab[T_D]
    rows = lax.broadcasted_iota(jnp.int32, (TOK, TOK), 0)
    cols = lax.broadcasted_iota(jnp.int32, (TOK, TOK), 1)
    end = jnp.int32(0)
    row_doc = jnp.zeros((TOK, TOK), jnp.int32)
    col_doc = jnp.zeros((TOK, TOK), jnp.int32)
    for k in range(4):
        end = end + lens[d * 4 + k]
        row_doc = row_doc + jnp.where(rows >= end, 1, 0)
        col_doc = col_doc + jnp.where(cols >= end, 1, 0)
    allowed = (row_doc == col_doc) & (cols <= rows)
    for h in range(BLK // HEAD):
        at = slice(h * HEAD, (h + 1) * HEAD)
        scores = nt(queries[:, at], keys[:, at]) * (HEAD ** -0.5)
        scores = jnp.where(allowed, scores, -1e30)
        weights = jnp.exp(scores - jnp.max(scores, axis=-1, keepdims=True))
        total = jnp.sum(weights, axis=-1, keepdims=True)
        out[:, at] = (nn(weights.astype(bf16), values[:, at]) / total).astype(bf16)


def attend(tab, lens, queries, keys, values):
    spec = pl.BlockSpec((TOK, BLK), lambda i, *_: (0, i))
    return pl.pallas_call(
        attend_body,
        out_shape=jax.ShapeDtypeStruct(queries.shape, bf16),
        grid_spec=pltpu.PrefetchScalarGridSpec(
            num_scalar_prefetch=2, grid=(4,), in_specs=[spec] * 3, out_specs=spec
        ),
        cost_estimate=cost(0),
        compiler_params=params(12),
        name="attend",
    )(tab, lens, *(in_hbm(v) for v in (queries, keys, values)))


def low_body(tab, att, cot, mine, other, low_out, lg_out, down_t, up_t, keep, give):
    unit = eye(256)
    for f in range(32):
        at = tab[T_F + f]
        block = jnp.where(tab[T_C] == f % 2, mine[at], other[at])
        turned = nt(unit, jnp.concatenate([block, block], 0)).astype(bf16)
        down_t[f * DCOLS : (f + 1) * DCOLS, :] = turned[:DCOLS]
        up_t[f * COLS : (f + 1) * COLS, :] = turned[DCOLS : DCOLS + COLS]
    low = nn(att[...], down_t[...])
    low_grad = nn(cot[...], up_t[...]) * SCALE
    first = lax.broadcasted_iota(jnp.int32, (TOK, 128), 1) < 64
    none = jnp.zeros((TOK, 128), f32)
    low_a, low_b = (jnp.where(first, low, none).astype(bf16), jnp.where(first, none, low).astype(bf16))
    lg_a, lg_b = (
        jnp.where(first, low_grad, none).astype(bf16),
        jnp.where(first, none, low_grad).astype(bf16),
    )
    low_out[...] = low_a
    lg_out[...] = lg_a
    core = tab[T_C]

    def put(f, lo, hi, even, odd):
        place = tab[T_P + f]
        keep[place, lo:hi, :] = jnp.where(core == 0, even, odd)
        give[place, lo:hi, :] = jnp.where(core == 0, odd, even).astype(bf16)

    half = DCOLS // 2
    both = jnp.concatenate([lg_a, lg_b], 1)
    for i in range(4):
        got = tn(att[:, i * BLK : (i + 1) * BLK], both)
        a, b = got[:, :128], got[:, 128:]
        pair = []
        for k in range(8):
            s = k * DCOLS
            pair.append(a[s : s + half] + b[s + half : s + DCOLS])
        for k in range(0, 8, 2):
            put(i * 8 + k, 0, half, pair[k], pair[k + 1])
    both = jnp.concatenate([low_a, low_b], 1)
    for j in range(8):
        got = tn(cot[:, j * BLK : (j + 1) * BLK], both) * SCALE
        a, b = got[:, :128], got[:, 128:]
        pair = []
        for k in range(4):
            s = k * COLS
            pair.append(a[s : s + DCOLS] + b[s + DCOLS : s + COLS])
        for k in range(0, 4, 2):
            put(j * 4 + k, half, half + DCOLS, pair[k], pair[k + 1])


def low_terms(tab, att, cot, mine, other):
    vmem = pl.BlockSpec(memory_space=pltpu.VMEM)
    return pl.pallas_call(
        low_body,
        out_shape=(
            jax.ShapeDtypeStruct((TOK, 128), bf16),
            jax.ShapeDtypeStruct((TOK, 128), bf16),
            jax.ShapeDtypeStruct((32 * DCOLS, 128), bf16),
            jax.ShapeDtypeStruct((32 * COLS, 128), bf16),
            jax.ShapeDtypeStruct((16, 120, 128), f32),
            jax.ShapeDtypeStruct((16, 120, 128), bf16),
        ),
        in_specs=[pl.BlockSpec(memory_space=pltpu.SMEM), *([vmem] * 4)],
        out_specs=[vmem] * 6,
        cost_estimate=cost(4),
        compiler_params=params(16),
        name="low_terms",
    )(tab, att, cot, mine, other)


SLOTS = 4


def tiles_body(stage, counts, tab, att, cot, *refs):
    n_head = 4 if stage == 0 else 2
    head, refs = refs[:n_head], refs[n_head:]
    tiles, refs = refs[: len(counts)], refs[len(counts) :]
    places = [(a, k) for a, n in enumerate(counts) for k in range(n)]
    count = len(places)
    if stage == 3:
        out, grad, out_acc, grad_acc, out_old, grad_old, old_sems, *refs = refs
    elif stage == 2:
        out_new, grad_new, out_acc, grad_acc, new_sems, *refs = refs
    else:
        out_acc, grad_acc, *refs = refs
    buf, sems, *refs = refs

    def fetch(t):
        a, k = places[t]
        return pltpu.make_async_copy(tiles[a].at[k], buf.at[t % SLOTS], sems.at[t % SLOTS])

    for t in range(SLOTS):
        fetch(t).start()
    if stage == 2:
        out_acc[...] = head[0][...]
        grad_acc[...] = head[1][...]
    if stage == 3:
        olds = [
            pltpu.make_async_copy(head[k], ref, old_sems.at[k])
            for k, ref in enumerate((out_old, grad_old))
        ]
        for copy in olds:
            copy.start()
        out_acc[...] = jnp.zeros(out_acc.shape, f32)
        grad_acc[...] = jnp.zeros(grad_acc.shape, f32)
    if stage == 0:
        low_a, lg_a, down_t, up_t = head
        for j in range(8):
            out_acc[j] = nt(low_a[...], up_t[j * BLK : (j + 1) * BLK, :]) * SCALE
        for i in range(4):
            grad_acc[i] = nt(lg_a[...], down_t[i * BLK : (i + 1) * BLK, :])
    for t in range(count):
        j, i = tab[STAGE_AT[stage] + t], tab[STAGE_AT[stage] + count + t]
        fetch(t).wait()
        tile = buf[t % SLOTS]
        out_acc[j] = out_acc[j] + nt(att[:, pl.ds(pl.multiple_of(i * BLK, 128), BLK)], tile)
        grad_acc[i] = grad_acc[i] + nn(cot[:, pl.ds(pl.multiple_of(j * BLK, 128), BLK)], tile)
        if t + SLOTS < count:
            fetch(t + SLOTS).start()
    if stage == 2:
        news = [
            pltpu.make_async_copy(ref, (out_new, grad_new)[k], new_sems.at[k])
            for k, ref in enumerate((out_acc, grad_acc))
        ]
        for copy in news:
            copy.start()
        for copy in news:
            copy.wait()
    if stage == 3:
        out_v, grad_v, out_sems = refs
        for copy in olds:
            copy.wait()
        copies = []
        for acc, old, full, ref, base in (
            (out_acc, out_old, out_v, out, 0),
            (grad_acc, grad_old, grad_v, grad, 8),
        ):
            for k in range(acc.shape[0]):
                at = slice(k * BLK, (k + 1) * BLK)
                full[:, at] = (acc[k] + old[k]).astype(bf16)
                copies.append(pltpu.make_async_copy(full.at[:, at], ref.at[:, at], out_sems.at[base + k]))
                copies[-1].start()
        for copy in copies:
            copy.wait()


def add_tiles(stage, tab, att, cot, head, arrays):
    vmem = pl.BlockSpec(memory_space=pltpu.VMEM)
    hbm = pl.BlockSpec(memory_space=pltpu.HBM)
    acc = [(8, TOK, BLK), (4, TOK, BLK)]
    outs, specs = [jax.ShapeDtypeStruct(s, f32) for s in acc], [vmem, vmem]
    scratch = [pltpu.VMEM((SLOTS, BLK, BLK), bf16), pltpu.SemaphoreType.DMA((SLOTS,))]
    if stage == 3:
        wide = [(TOK, 8 * BLK), (TOK, 4 * BLK)]
        outs, specs = [jax.ShapeDtypeStruct(s, bf16) for s in wide], [hbm, hbm]
        scratch = [pltpu.VMEM(s, f32) for s in acc * 2] + [pltpu.SemaphoreType.DMA((2,))] + scratch
        scratch += [pltpu.VMEM(s, bf16) for s in wide] + [pltpu.SemaphoreType.DMA((12,))]
    if stage == 2:
        outs, specs = [pltpu.HBM(s, f32) for s in acc], [hbm, hbm]
        scratch = [pltpu.VMEM(s, f32) for s in acc] + [pltpu.SemaphoreType.DMA((2,))] + scratch
    if stage == 3:
        head = [in_hbm(h) for h in head]
    head_spec = hbm if stage == 3 else vmem
    return pl.pallas_call(
        lambda *refs: tiles_body(stage, [a.shape[0] for a in arrays], *refs),
        out_shape=outs,
        in_specs=[pl.BlockSpec(memory_space=pltpu.SMEM), vmem, vmem, *([head_spec] * len(head)), *([hbm] * len(arrays))],
        out_specs=specs,
        scratch_shapes=scratch,
        input_output_aliases={} if stage != 1 else {3: 0, 4: 1},
        cost_estimate=cost(8 if stage == 0 else 0),
        compiler_params=params(28 if stage == 3 else 16),
        name=f"tiles_{stage}",
    )(tab, att, cot, *head, *arrays)


def per_device(
    table,
    queries,
    keys,
    values,
    lengths,
    weight,
    codes,
    factor,
    offset,
    down,
    up,
    cot,
):
    tab = table.reshape(-1)
    lens = lengths.reshape(-1)

    tie = lax.optimization_barrier

    def along(value, axis, k):
        at = AX.index(axis)
        return send(value, lambda *to: tuple(v + (k if n == at else 0) for n, v in enumerate(to)))

    def scattered(part, axis, bit, n, kind):
        return part[:n] + flip(part[n:].astype(kind), axis, bit).astype(f32)

    adapters = jnp.concatenate([down, up, jnp.zeros((64, 16), bf16)], 1)
    adapters = jnp.stack([adapters, *(along(adapters, "zh", -k) for k in REL[1:])])
    quarter = base_quarter(tab, weight, codes, factor, offset)
    quarter, queries = tie((quarter, queries))
    rounds = [z_round(quarter, k) for k in range(4)]
    rounds[0], queries, adapters = tie((rounds[0], queries, adapters))
    att = attend(tab, lens, queries, keys, values)
    adapters = [adapters, *(along(adapters, "x", -k) for k in REL[1:])]
    rounds, att, adapters = tie((rounds, att, adapters))
    own = ordered(tab, rounds)
    own, adapters = tie((own, adapters))
    mine = joined(adapters).reshape(16, 64, 256)

    less, more, far = middle(own, 1), middle(own, -1), middle(own, 2)
    low_a, lg_a, down_t, up_t, keep, give = low_terms(tab, att, cot, mine, sibling(mine))
    part = keep + flip(give, "c", 1).astype(f32)
    less, more, far, part = tie((less, more, far, part))
    row = joined([own, less, more, far])

    all_less, all_more = outer(row, 1), outer(row, -1)
    part, row = tie((part, row))
    kept, got = part[:8], flip(part[8:].astype(bf16), "zh", 1)
    sums = add_tiles(0, tab, att, cot, (low_a, lg_a, down_t, up_t), [row, sibling(row)])
    got, sums = tie((got, tuple(sums)))
    part = scattered(kept + got.astype(f32), "zh", 2, 4, bf16)
    part = part + flip(part, "zl", 1)
    all_less, all_more, part, sums = tie((all_less, all_more, part, sums))

    far_a, far_b = outer(all_less[:2], 1), outer(all_more[2:], -1)
    tiles = [all_less, all_more]
    sums = add_tiles(1, tab, att, cot, sums, tiles)
    part, sums = tie((part, tuple(sums)))
    a, b, c = (flip(part[k], "x", k) for k in (1, 2, 3))
    sums = add_tiles(2, tab, att, cot, sums, [sibling(t) for t in tiles])
    a, b, c, sums = tie((a, b, c, tuple(sums)))
    part = (part[0] + a) + (b + c)
    far_a, far_b, part, sums = tie((far_a, far_b, part, sums))
    tiles = [far_a, far_b]
    tiles_other = [sibling(t) for t in tiles]
    a, b, c = (flip(part, "y", k) for k in (1, 2, 3))
    part = (part + a) + (b + c)
    out, grad = add_tiles(3, tab, att, cot, sums, [*tiles, *tiles_other])
    half = DCOLS // 2
    down_grad = jnp.concatenate([part[:half, :64], part[:half, 64:]], 0).T
    up_grad = jnp.concatenate([part[half:, :64], part[half:, 64:]], 0).T
    return out, grad, down_grad, up_grad


def solution(mesh):
    fine = Mesh(np.asarray(mesh.devices).reshape(DIMS), AX)
    tokens, owners = ("y", "zl", "x", "zh", "c"), ("x", "zh", "c")
    table = device_table()
    mapped = jax.shard_map(
        per_device,
        mesh=fine,
        in_specs=(
            P(tokens, None),
            P(tokens, None),
            P(tokens, None),
            P(tokens, None),
            P(owners, None, None),
            P(None, owners),
            P(None, owners),
            P(None, owners),
            P(None, owners),
            P(None, owners),
            P(None, owners),
            P(tokens, None),
        ),
        out_specs=(
            P(tokens, None),
            P(tokens, None),
            P(None, owners),
            P(None, owners),
        ),
        check_vma=False,
    )
    return lambda *args: mapped(jnp.asarray(table), *args)
```

```python
import jax
import jax.numpy as jnp
import numpy as np
from jax import lax
from jax.experimental import pallas as pl
from jax.experimental.pallas import tpu as pltpu
from jax.sharding import Mesh
from jax.sharding import PartitionSpec as P

HEAD = 128
TOK = 192
BLK = 640
COLS = 160
DCOLS = 80
SCALE = 0.25
AX = ("y", "zl", "x", "zh", "c")
DIMS = (4, 2, 4, 4, 2)
REL = (0, -1, 1, 2)


def cost(us):
    return pl.CostEstimate(flops=int(us * 1.15e9) + 1, bytes_accessed=1, transcendentals=0)


bf16 = jnp.bfloat16
f32 = jnp.float32

T_Y, T_D, T_S, T_F, T_C, T_P, T_B, T_TILES = 0, 1, 2, 6, 38, 40, 72, 104
STAGE_AT = (104, 120, 136, 152)
T_LEN = 168


def params(mib=48):
    return pltpu.CompilerParams(vmem_limit_bytes=mib << 20)


def in_hbm(value):
    return pltpu.with_memory_space_constraint(value, pltpu.HBM)


def coords():
    return [np.unravel_index(d, DIMS) for d in range(256)]


def device_table():
    rows = np.zeros((256, T_LEN), np.int32)
    for n, (y, zl, x, zh, c) in enumerate(coords()):
        r = rows[n]
        r[T_Y], r[T_D], r[T_C] = y, y * 2 + zl, c
        for k in range(4):
            r[T_S + k] = (zh - k) % 4
        for f in range(32):
            fx, fz, fc = f // 8, (f // 2) % 4, f % 2
            r[T_F + f] = [(x + k) % 4 for k in REL].index(fx) * 4 + [(zh + k) % 4 for k in REL].index(fz)
            dz = fz ^ zh
            r[T_P + f] = (dz % 2) * 8 + (dz // 2) * 4 + (fx ^ x)

        def tiles(own, v, us):
            kind = c if own else 1 - c
            if kind == 0:
                return [(2 * ((x + u) % 4), (y + v) % 4) for u in us]
            return [(2 * ((x + v) % 4) + 1, (y + u) % 4) for u in us]

        both = lambda pairs: [
            t for own in (True, False) for u, v in pairs for t in tiles(own, v, (u,))
        ]
        nears = [(u, v) for v in (-1, 1) for u in REL]
        stages = (
            both([(u, 0) for u in REL]),
            [t for u, v in nears for t in tiles(True, v, (u,))],
            [t for u, v in nears for t in tiles(False, v, (u,))],
            both([(u, 2) for u in REL]),
        )
        at = T_TILES
        for stage in stages:
            for k, (j, i) in enumerate(stage):
                r[at + k], r[at + len(stage) + k] = j, i
            at += 2 * len(stage)
    return rows


def index_of(y, zl, x, zh, c):
    return int(np.ravel_multi_index((y % 4, zl, x % 4, zh % 4, c), DIMS))


def send(value, target):
    pairs = [(n, index_of(*target(*(int(v) for v in at)))) for n, at in enumerate(coords())]
    return lax.ppermute(value, AX, pairs)


def z_round(value, k):
    return send(value, lambda y, zl, x, zh, c: (y, zl, x, 2 * (zh % 2) + c + k, zh // 2))


def middle(value, k):
    return send(value, lambda y, zl, x, zh, c: (y, zl, x + k, zh, c) if c == 0 else (y + k, zl, x, zh, c))


def outer(value, k):
    return send(value, lambda y, zl, x, zh, c: (y + k, zl, x, zh, c) if c == 0 else (y, zl, x + k, zh, c))


def sibling(value):
    return send(value, lambda y, zl, x, zh, c: (y, zl, x, zh, 1 - c))


def flip(value, axis, bit):
    at = AX.index(axis)

    def target(*place):
        place = list(place)
        place[at] ^= bit
        return place

    return send(value, target)


def nt(a, b):
    return lax.dot_general(a, b, (((1,), (1,)), ((), ())), preferred_element_type=f32)


def nn(a, b):
    return lax.dot_general(a, b, (((1,), (0,)), ((), ())), preferred_element_type=f32)


def tn(a, b):
    return lax.dot_general(a, b, (((0,), (0,)), ((), ())), preferred_element_type=f32)


def eye(n):
    rows = lax.broadcasted_iota(jnp.int32, (n, n), 0)
    cols = lax.broadcasted_iota(jnp.int32, (n, n), 1)
    return jnp.where(rows == cols, 1.0, 0.0).astype(bf16)


def base_body(tab, weight_t, codes, factor, offset, out, weight, code_v, factor_v, offset_v, sems):
    y = tab[T_Y]
    copies = [
        pltpu.make_async_copy(weight_t.at[:, pl.ds(pl.multiple_of(y * BLK, 128), BLK)], weight, sems.at[0]),
        pltpu.make_async_copy(codes, code_v, sems.at[1]),
        pltpu.make_async_copy(factor, factor_v, sems.at[2]),
        pltpu.make_async_copy(offset, offset_v, sems.at[3]),
    ]
    for copy in copies:
        copy.start()
    for copy in copies:
        copy.wait()
    rows = []
    for k in range(10):
        b = y * 10 + k
        code = code_v[pl.ds(b, 1), :].astype(f32)
        group = b // 8
        rows.append(factor_v[pl.ds(group, 1), :] * (code + 1.0) / 256.0 + offset_v[pl.ds(group, 1), :])
    rest = jnp.concatenate([*rows, jnp.zeros((6, COLS), f32)], 0)
    spread = lax.broadcasted_iota(jnp.int32, (16, BLK), 1) // 64
    spread = spread == lax.broadcasted_iota(jnp.int32, (16, BLK), 0)
    spread = jnp.where(spread, 1.0, 0.0).astype(bf16)
    absmax = jnp.zeros((COLS, BLK), f32)
    for _ in range(3):
        piece = rest.astype(bf16)
        rest = rest - piece.astype(f32)
        absmax = absmax + tn(piece, spread)
    out[...] = (weight[...].astype(f32) * absmax).astype(bf16)


def base_quarter(tab, weight, codes, factor, offset):
    hbm = pl.BlockSpec(memory_space=pltpu.HBM)
    return pl.pallas_call(
        base_body,
        out_shape=jax.ShapeDtypeStruct((COLS, BLK), bf16),
        in_specs=[pl.BlockSpec(memory_space=pltpu.SMEM), hbm, hbm, hbm, hbm],
        out_specs=pl.BlockSpec(memory_space=pltpu.VMEM),
        scratch_shapes=[
            pltpu.VMEM((COLS, BLK), bf16),
            pltpu.VMEM(codes.shape, jnp.int32),
            pltpu.VMEM(factor.shape, f32),
            pltpu.VMEM(offset.shape, f32),
            pltpu.SemaphoreType.DMA((4,)),
        ],
        cost_estimate=cost(0),
        compiler_params=params(16),
        name="base_quarter",
    )(tab, *(in_hbm(v) for v in (weight.T, codes, factor, offset)))


def order_body(tab, a, b, c, d, out, sems):
    copies = []
    for k, src in enumerate((a, b, c, d)):
        place = pl.multiple_of(tab[T_S + k] * COLS, 32)
        copies.append(pltpu.make_async_copy(src, out.at[pl.ds(place, COLS), :], sems.at[k]))
    for copy in copies:
        copy.start()
    for copy in copies:
        copy.wait()


def ordered(tab, blocks):
    anywhere = pl.BlockSpec(memory_space=pl.ANY)
    return pl.pallas_call(
        order_body,
        out_shape=jax.ShapeDtypeStruct((BLK, BLK), bf16),
        in_specs=[pl.BlockSpec(memory_space=pltpu.SMEM), *([anywhere] * 4)],
        out_specs=anywhere,
        scratch_shapes=[pltpu.SemaphoreType.DMA((4,))],
        cost_estimate=cost(0),
        compiler_params=params(8),
        name="ordered",
    )(tab, *blocks)


def join_body(*refs):
    *parts, out, sems = refs
    copies = [pltpu.make_async_copy(src, out.at[k], sems.at[k]) for k, src in enumerate(parts)]
    for copy in copies:
        copy.start()
    for copy in copies:
        copy.wait()


def joined(parts):
    anywhere = pl.BlockSpec(memory_space=pl.ANY)
    return pl.pallas_call(
        join_body,
        out_shape=jax.ShapeDtypeStruct((len(parts), *parts[0].shape), parts[0].dtype),
        in_specs=[anywhere] * len(parts),
        out_specs=anywhere,
        scratch_shapes=[pltpu.SemaphoreType.DMA((len(parts),))],
        cost_estimate=cost(0),
        compiler_params=params(8),
        name="joined",
    )(*parts)


def attend_body(tab, lens, queries, keys, values, out):
    d = tab[T_D]
    rows = lax.broadcasted_iota(jnp.int32, (TOK, TOK), 0)
    cols = lax.broadcasted_iota(jnp.int32, (TOK, TOK), 1)
    end = jnp.int32(0)
    row_doc = jnp.zeros((TOK, TOK), jnp.int32)
    col_doc = jnp.zeros((TOK, TOK), jnp.int32)
    for k in range(4):
        end = end + lens[d * 4 + k]
        row_doc = row_doc + jnp.where(rows >= end, 1, 0)
        col_doc = col_doc + jnp.where(cols >= end, 1, 0)
    allowed = (row_doc == col_doc) & (cols <= rows)
    for h in range(BLK // HEAD):
        at = slice(h * HEAD, (h + 1) * HEAD)
        scores = nt(queries[:, at], keys[:, at]) * (HEAD ** -0.5)
        scores = jnp.where(allowed, scores, -1e30)
        weights = jnp.exp(scores - jnp.max(scores, axis=-1, keepdims=True))
        total = jnp.sum(weights, axis=-1, keepdims=True)
        out[:, at] = (nn(weights.astype(bf16), values[:, at]) / total).astype(bf16)


def attend(tab, lens, queries, keys, values):
    spec = pl.BlockSpec((TOK, BLK), lambda i, *_: (0, i))
    return pl.pallas_call(
        attend_body,
        out_shape=jax.ShapeDtypeStruct(queries.shape, bf16),
        grid_spec=pltpu.PrefetchScalarGridSpec(
            num_scalar_prefetch=2, grid=(4,), in_specs=[spec] * 3, out_specs=spec
        ),
        cost_estimate=cost(0),
        compiler_params=params(12),
        name="attend",
    )(tab, lens, *(in_hbm(v) for v in (queries, keys, values)))


def low_body(tab, att, cot, mine, other, low_out, lg_out, down_t, up_t, keep, give):
    unit = eye(256)
    for f in range(32):
        at = tab[T_F + f]
        block = jnp.where(tab[T_C] == f % 2, mine[at], other[at])
        turned = nt(unit, jnp.concatenate([block, block], 0)).astype(bf16)
        down_t[f * DCOLS : (f + 1) * DCOLS, :] = turned[:DCOLS]
        up_t[f * COLS : (f + 1) * COLS, :] = turned[DCOLS : DCOLS + COLS]
    low = nn(att[...], down_t[...])
    low_grad = nn(cot[...], up_t[...]) * SCALE
    first = lax.broadcasted_iota(jnp.int32, (TOK, 128), 1) < 64
    none = jnp.zeros((TOK, 128), f32)
    low_a, low_b = (jnp.where(first, low, none).astype(bf16), jnp.where(first, none, low).astype(bf16))
    lg_a, lg_b = (
        jnp.where(first, low_grad, none).astype(bf16),
        jnp.where(first, none, low_grad).astype(bf16),
    )
    low_out[...] = low_a
    lg_out[...] = lg_a
    core = tab[T_C]

    def put(f, lo, hi, even, odd):
        place = tab[T_P + f]
        keep[place, lo:hi, :] = jnp.where(core == 0, even, odd)
        give[place, lo:hi, :] = jnp.where(core == 0, odd, even).astype(bf16)

    half = DCOLS // 2
    both = jnp.concatenate([lg_a, lg_b], 1)
    for i in range(4):
        got = tn(att[:, i * BLK : (i + 1) * BLK], both)
        a, b = got[:, :128], got[:, 128:]
        pair = []
        for k in range(8):
            s = k * DCOLS
            pair.append(a[s : s + half] + b[s + half : s + DCOLS])
        for k in range(0, 8, 2):
            put(i * 8 + k, 0, half, pair[k], pair[k + 1])
    both = jnp.concatenate([low_a, low_b], 1)
    for j in range(8):
        got = tn(cot[:, j * BLK : (j + 1) * BLK], both) * SCALE
        a, b = got[:, :128], got[:, 128:]
        pair = []
        for k in range(4):
            s = k * COLS
            pair.append(a[s : s + DCOLS] + b[s + DCOLS : s + COLS])
        for k in range(0, 4, 2):
            put(j * 4 + k, half, half + DCOLS, pair[k], pair[k + 1])


def low_terms(tab, att, cot, mine, other):
    vmem = pl.BlockSpec(memory_space=pltpu.VMEM)
    return pl.pallas_call(
        low_body,
        out_shape=(
            jax.ShapeDtypeStruct((TOK, 128), bf16),
            jax.ShapeDtypeStruct((TOK, 128), bf16),
            jax.ShapeDtypeStruct((32 * DCOLS, 128), bf16),
            jax.ShapeDtypeStruct((32 * COLS, 128), bf16),
            jax.ShapeDtypeStruct((16, 120, 128), f32),
            jax.ShapeDtypeStruct((16, 120, 128), bf16),
        ),
        in_specs=[pl.BlockSpec(memory_space=pltpu.SMEM), *([vmem] * 4)],
        out_specs=[vmem] * 6,
        cost_estimate=cost(0),
        compiler_params=params(16),
        name="low_terms",
    )(tab, att, cot, mine, other)


SLOTS = 4


def tiles_body(stage, counts, tab, att, cot, *refs):
    n_head = 4 if stage == 0 else 2
    head, refs = refs[:n_head], refs[n_head:]
    tiles, refs = refs[: len(counts)], refs[len(counts) :]
    places = [(a, k) for a, n in enumerate(counts) for k in range(n)]
    count = len(places)
    if stage == 3:
        out, grad, out_acc, grad_acc, out_old, grad_old, old_sems, *refs = refs
    elif stage == 2:
        out_new, grad_new, out_acc, grad_acc, new_sems, *refs = refs
    else:
        out_acc, grad_acc, *refs = refs
    buf, sems, *refs = refs

    def fetch(t):
        a, k = places[t]
        return pltpu.make_async_copy(tiles[a].at[k], buf.at[t % SLOTS], sems.at[t % SLOTS])

    for t in range(SLOTS):
        fetch(t).start()
    if stage == 2:
        out_acc[...] = head[0][...]
        grad_acc[...] = head[1][...]
    if stage == 3:
        olds = [
            pltpu.make_async_copy(head[k], ref, old_sems.at[k])
            for k, ref in enumerate((out_old, grad_old))
        ]
        for copy in olds:
            copy.start()
        out_acc[...] = jnp.zeros(out_acc.shape, f32)
        grad_acc[...] = jnp.zeros(grad_acc.shape, f32)
    if stage == 0:
        low_a, lg_a, down_t, up_t = head
        for j in range(8):
            out_acc[j] = nt(low_a[...], up_t[j * BLK : (j + 1) * BLK, :]) * SCALE
        for i in range(4):
            grad_acc[i] = nt(lg_a[...], down_t[i * BLK : (i + 1) * BLK, :])
    for t in range(count):
        j, i = tab[STAGE_AT[stage] + t], tab[STAGE_AT[stage] + count + t]
        fetch(t).wait()
        tile = buf[t % SLOTS]
        out_acc[j] = out_acc[j] + nt(att[:, pl.ds(pl.multiple_of(i * BLK, 128), BLK)], tile)
        grad_acc[i] = grad_acc[i] + nn(cot[:, pl.ds(pl.multiple_of(j * BLK, 128), BLK)], tile)
        if t + SLOTS < count:
            fetch(t + SLOTS).start()
    if stage == 2:
        news = [
            pltpu.make_async_copy(ref, (out_new, grad_new)[k], new_sems.at[k])
            for k, ref in enumerate((out_acc, grad_acc))
        ]
        for copy in news:
            copy.start()
        for copy in news:
            copy.wait()
    if stage == 3:
        out_v, grad_v, out_sems = refs
        for copy in olds:
            copy.wait()
        copies = []
        for acc, old, full, ref, base in (
            (out_acc, out_old, out_v, out, 0),
            (grad_acc, grad_old, grad_v, grad, 8),
        ):
            for k in range(acc.shape[0]):
                at = slice(k * BLK, (k + 1) * BLK)
                full[:, at] = (acc[k] + old[k]).astype(bf16)
                copies.append(pltpu.make_async_copy(full.at[:, at], ref.at[:, at], out_sems.at[base + k]))
                copies[-1].start()
        for copy in copies:
            copy.wait()


def add_tiles(stage, tab, att, cot, head, arrays):
    vmem = pl.BlockSpec(memory_space=pltpu.VMEM)
    hbm = pl.BlockSpec(memory_space=pltpu.HBM)
    acc = [(8, TOK, BLK), (4, TOK, BLK)]
    outs, specs = [jax.ShapeDtypeStruct(s, f32) for s in acc], [vmem, vmem]
    scratch = [pltpu.VMEM((SLOTS, BLK, BLK), bf16), pltpu.SemaphoreType.DMA((SLOTS,))]
    if stage == 3:
        wide = [(TOK, 8 * BLK), (TOK, 4 * BLK)]
        outs, specs = [jax.ShapeDtypeStruct(s, bf16) for s in wide], [hbm, hbm]
        scratch = [pltpu.VMEM(s, f32) for s in acc * 2] + [pltpu.SemaphoreType.DMA((2,))] + scratch
        scratch += [pltpu.VMEM(s, bf16) for s in wide] + [pltpu.SemaphoreType.DMA((12,))]
    if stage == 2:
        outs, specs = [pltpu.HBM(s, f32) for s in acc], [hbm, hbm]
        scratch = [pltpu.VMEM(s, f32) for s in acc] + [pltpu.SemaphoreType.DMA((2,))] + scratch
    if stage == 3:
        head = [in_hbm(h) for h in head]
    head_spec = hbm if stage == 3 else vmem
    return pl.pallas_call(
        lambda *refs: tiles_body(stage, [a.shape[0] for a in arrays], *refs),
        out_shape=outs,
        in_specs=[pl.BlockSpec(memory_space=pltpu.SMEM), vmem, vmem, *([head_spec] * len(head)), *([hbm] * len(arrays))],
        out_specs=specs,
        scratch_shapes=scratch,
        input_output_aliases={} if stage != 1 else {3: 0, 4: 1},
        cost_estimate=cost(8 if stage == 0 else 0),
        compiler_params=params(28 if stage == 3 else 16),
        name=f"tiles_{stage}",
    )(tab, att, cot, *head, *arrays)


def per_device(
    table,
    queries,
    keys,
    values,
    lengths,
    weight,
    codes,
    factor,
    offset,
    down,
    up,
    cot,
):
    tab = table.reshape(-1)
    lens = lengths.reshape(-1)

    tie = lax.optimization_barrier

    def along(value, axis, k):
        at = AX.index(axis)
        return send(value, lambda *to: tuple(v + (k if n == at else 0) for n, v in enumerate(to)))

    def scattered(part, axis, bit, n, kind):
        return part[:n] + flip(part[n:].astype(kind), axis, bit).astype(f32)

    adapters = jnp.concatenate([down, up, jnp.zeros((64, 16), bf16)], 1)
    adapters = jnp.stack([adapters, *(along(adapters, "zh", -k) for k in REL[1:])])
    quarter = base_quarter(tab, weight, codes, factor, offset)
    quarter, queries = tie((quarter, queries))
    rounds = [z_round(quarter, k) for k in range(4)]
    rounds[0], adapters = tie((rounds[0], adapters))
    adapters = [adapters, *(along(adapters, "x", -k) for k in REL[1:])]
    rounds, adapters = tie((rounds, adapters))
    own = ordered(tab, rounds)

    less, more, far = middle(own, 1), middle(own, -1), middle(own, 2)
    own, queries = tie((own, queries))
    att = attend(tab, lens, queries, keys, values)
    mine = joined(adapters).reshape(16, 64, 256)
    low = low_terms(tab, att, cot, mine, sibling(mine))
    less, more, far, low = tie((less, more, far, tuple(low)))
    low_a, lg_a, down_t, up_t, keep, give = low
    row = joined([own, less, more, far])

    all_less, all_more = outer(row, 1), outer(row, -1)
    give, row = tie((give, row))
    part = keep + flip(give, "c", 1).astype(f32)
    kept, got = part[:8], flip(part[8:].astype(bf16), "zh", 1)
    sums = add_tiles(0, tab, att, cot, (low_a, lg_a, down_t, up_t), [row, sibling(row)])
    got, sums = tie((got, tuple(sums)))
    part = scattered(kept + got.astype(f32), "zh", 2, 4, bf16)
    part = part + flip(part, "zl", 1)
    all_less, all_more, part, sums = tie((all_less, all_more, part, sums))

    far_a, far_b = outer(all_less[:2], 1), outer(all_more[2:], -1)
    tiles = [all_less, all_more]
    sums = add_tiles(1, tab, att, cot, sums, tiles)
    part, sums = tie((part, tuple(sums)))
    a, b, c = (flip(part[k], "x", k) for k in (1, 2, 3))
    sums = add_tiles(2, tab, att, cot, sums, [sibling(t) for t in tiles])
    a, b, c, sums = tie((a, b, c, tuple(sums)))
    part = (part[0] + a) + (b + c)
    far_a, far_b, part, sums = tie((far_a, far_b, part, sums))
    tiles = [far_a, far_b]
    tiles_other = [sibling(t) for t in tiles]
    a, b, c = (flip(part, "y", k) for k in (1, 2, 3))
    part = (part + a) + (b + c)
    out, grad = add_tiles(3, tab, att, cot, sums, [*tiles, *tiles_other])
    half = DCOLS // 2
    down_grad = jnp.concatenate([part[:half, :64], part[:half, 64:]], 0).T
    up_grad = jnp.concatenate([part[half:, :64], part[half:, 64:]], 0).T
    return out, grad, down_grad, up_grad


def solution(mesh):
    fine = Mesh(np.asarray(mesh.devices).reshape(DIMS), AX)
    tokens, owners = ("y", "zl", "x", "zh", "c"), ("x", "zh", "c")
    table = device_table()
    mapped = jax.shard_map(
        per_device,
        mesh=fine,
        in_specs=(
            P(tokens, None),
            P(tokens, None),
            P(tokens, None),
            P(tokens, None),
            P(owners, None, None),
            P(None, owners),
            P(None, owners),
            P(None, owners),
            P(None, owners),
            P(None, owners),
            P(None, owners),
            P(tokens, None),
        ),
        out_specs=(
            P(tokens, None),
            P(tokens, None),
            P(None, owners),
            P(None, owners),
        ),
        check_vma=False,
    )
    return lambda *args: mapped(jnp.asarray(table), *args)
```

```python
import jax
import jax.numpy as jnp
import numpy as np
from jax import lax
from jax.experimental import pallas as pl
from jax.experimental.pallas import tpu as pltpu
from jax.sharding import Mesh
from jax.sharding import PartitionSpec as P

HEAD = 128
TOK = 192
BLK = 640
COLS = 160
DCOLS = 80
SCALE = 0.25
AX = ("y", "zl", "x", "zh", "c")
DIMS = (4, 2, 4, 4, 2)
REL = (0, -1, 1, 2)


def cost(us):
    return pl.CostEstimate(flops=int(us * 1.15e9) + 1, bytes_accessed=1, transcendentals=0)


bf16 = jnp.bfloat16
f32 = jnp.float32

T_Y, T_D, T_S, T_F, T_C, T_P, T_B, T_TILES = 0, 1, 2, 6, 38, 40, 72, 104
STAGE_AT = (104, 120, 136, 152)
T_LEN = 168


def params(mib=48):
    return pltpu.CompilerParams(vmem_limit_bytes=mib << 20)


def in_hbm(value):
    return pltpu.with_memory_space_constraint(value, pltpu.HBM)


def coords():
    return [np.unravel_index(d, DIMS) for d in range(256)]


def device_table():
    rows = np.zeros((256, T_LEN), np.int32)
    for n, (y, zl, x, zh, c) in enumerate(coords()):
        r = rows[n]
        r[T_Y], r[T_D], r[T_C] = y, y * 2 + zl, c
        for k in range(4):
            r[T_S + k] = (zh - k) % 4
        for f in range(32):
            fx, fz, fc = f // 8, (f // 2) % 4, f % 2
            r[T_F + f] = [(x + k) % 4 for k in REL].index(fx) * 4 + [(zh + k) % 4 for k in REL].index(fz)
            dz = fz ^ zh
            r[T_P + f] = (dz % 2) * 8 + (dz // 2) * 4 + (fx ^ x)

        def tiles(own, v, us):
            kind = c if own else 1 - c
            if kind == 0:
                return [(2 * ((x + u) % 4), (y + v) % 4) for u in us]
            return [(2 * ((x + v) % 4) + 1, (y + u) % 4) for u in us]

        both = lambda pairs: [
            t for own in (True, False) for u, v in pairs for t in tiles(own, v, (u,))
        ]
        nears = [(u, v) for v in (-1, 1) for u in REL]
        stages = (
            both([(u, 0) for u in REL]),
            [t for u, v in nears for t in tiles(True, v, (u,))],
            [t for u, v in nears for t in tiles(False, v, (u,))],
            both([(u, 2) for u in REL]),
        )
        at = T_TILES
        for stage in stages:
            for k, (j, i) in enumerate(stage):
                r[at + k], r[at + len(stage) + k] = j, i
            at += 2 * len(stage)
    return rows


def index_of(y, zl, x, zh, c):
    return int(np.ravel_multi_index((y % 4, zl, x % 4, zh % 4, c), DIMS))


def send(value, target):
    pairs = [(n, index_of(*target(*(int(v) for v in at)))) for n, at in enumerate(coords())]
    return lax.ppermute(value, AX, pairs)


def z_round(value, k):
    return send(value, lambda y, zl, x, zh, c: (y, zl, x, 2 * (zh % 2) + c + k, zh // 2))


def middle(value, k):
    return send(value, lambda y, zl, x, zh, c: (y, zl, x + k, zh, c) if c == 0 else (y + k, zl, x, zh, c))


def outer(value, k):
    return send(value, lambda y, zl, x, zh, c: (y + k, zl, x, zh, c) if c == 0 else (y, zl, x + k, zh, c))


def sibling(value):
    return send(value, lambda y, zl, x, zh, c: (y, zl, x, zh, 1 - c))


def flip(value, axis, bit):
    at = AX.index(axis)

    def target(*place):
        place = list(place)
        place[at] ^= bit
        return place

    return send(value, target)


def nt(a, b):
    return lax.dot_general(a, b, (((1,), (1,)), ((), ())), preferred_element_type=f32)


def nn(a, b):
    return lax.dot_general(a, b, (((1,), (0,)), ((), ())), preferred_element_type=f32)


def tn(a, b):
    return lax.dot_general(a, b, (((0,), (0,)), ((), ())), preferred_element_type=f32)


def eye(n):
    rows = lax.broadcasted_iota(jnp.int32, (n, n), 0)
    cols = lax.broadcasted_iota(jnp.int32, (n, n), 1)
    return jnp.where(rows == cols, 1.0, 0.0).astype(bf16)


def base_body(tab, weight_t, codes, factor, offset, out, weight, code_v, factor_v, offset_v, sems):
    y = tab[T_Y]
    copies = [
        pltpu.make_async_copy(weight_t.at[:, pl.ds(pl.multiple_of(y * BLK, 128), BLK)], weight, sems.at[0]),
        pltpu.make_async_copy(codes, code_v, sems.at[1]),
        pltpu.make_async_copy(factor, factor_v, sems.at[2]),
        pltpu.make_async_copy(offset, offset_v, sems.at[3]),
    ]
    for copy in copies:
        copy.start()
    for copy in copies:
        copy.wait()
    rows = []
    for k in range(10):
        b = y * 10 + k
        code = code_v[pl.ds(b, 1), :].astype(f32)
        group = b // 8
        rows.append(factor_v[pl.ds(group, 1), :] * (code + 1.0) / 256.0 + offset_v[pl.ds(group, 1), :])
    rest = jnp.concatenate([*rows, jnp.zeros((6, COLS), f32)], 0)
    spread = lax.broadcasted_iota(jnp.int32, (16, BLK), 1) // 64
    spread = spread == lax.broadcasted_iota(jnp.int32, (16, BLK), 0)
    spread = jnp.where(spread, 1.0, 0.0).astype(bf16)
    absmax = jnp.zeros((COLS, BLK), f32)
    for _ in range(3):
        piece = rest.astype(bf16)
        rest = rest - piece.astype(f32)
        absmax = absmax + tn(piece, spread)
    out[...] = (weight[...].astype(f32) * absmax).astype(bf16)


def base_quarter(tab, weight, codes, factor, offset):
    hbm = pl.BlockSpec(memory_space=pltpu.HBM)
    return pl.pallas_call(
        base_body,
        out_shape=jax.ShapeDtypeStruct((COLS, BLK), bf16),
        in_specs=[pl.BlockSpec(memory_space=pltpu.SMEM), hbm, hbm, hbm, hbm],
        out_specs=pl.BlockSpec(memory_space=pltpu.VMEM),
        scratch_shapes=[
            pltpu.VMEM((COLS, BLK), bf16),
            pltpu.VMEM(codes.shape, jnp.int32),
            pltpu.VMEM(factor.shape, f32),
            pltpu.VMEM(offset.shape, f32),
            pltpu.SemaphoreType.DMA((4,)),
        ],
        cost_estimate=cost(0),
        compiler_params=params(16),
        name="base_quarter",
    )(tab, *(in_hbm(v) for v in (weight.T, codes, factor, offset)))


def order_body(tab, a, b, c, d, out, sems):
    copies = []
    for k, src in enumerate((a, b, c, d)):
        place = pl.multiple_of(tab[T_S + k] * COLS, 32)
        copies.append(pltpu.make_async_copy(src, out.at[pl.ds(place, COLS), :], sems.at[k]))
    for copy in copies:
        copy.start()
    for copy in copies:
        copy.wait()


def ordered(tab, blocks):
    anywhere = pl.BlockSpec(memory_space=pl.ANY)
    return pl.pallas_call(
        order_body,
        out_shape=jax.ShapeDtypeStruct((BLK, BLK), bf16),
        in_specs=[pl.BlockSpec(memory_space=pltpu.SMEM), *([anywhere] * 4)],
        out_specs=anywhere,
        scratch_shapes=[pltpu.SemaphoreType.DMA((4,))],
        cost_estimate=cost(0),
        compiler_params=params(8),
        name="ordered",
    )(tab, *blocks)


def join_body(*refs):
    *parts, out, sems = refs
    copies = [pltpu.make_async_copy(src, out.at[k], sems.at[k]) for k, src in enumerate(parts)]
    for copy in copies:
        copy.start()
    for copy in copies:
        copy.wait()


def joined(parts):
    anywhere = pl.BlockSpec(memory_space=pl.ANY)
    return pl.pallas_call(
        join_body,
        out_shape=jax.ShapeDtypeStruct((len(parts), *parts[0].shape), parts[0].dtype),
        in_specs=[anywhere] * len(parts),
        out_specs=anywhere,
        scratch_shapes=[pltpu.SemaphoreType.DMA((len(parts),))],
        cost_estimate=cost(0),
        compiler_params=params(8),
        name="joined",
    )(*parts)


def attend_body(tab, lens, queries, keys, values, out):
    d = tab[T_D]
    rows = lax.broadcasted_iota(jnp.int32, (TOK, TOK), 0)
    cols = lax.broadcasted_iota(jnp.int32, (TOK, TOK), 1)
    end = jnp.int32(0)
    row_doc = jnp.zeros((TOK, TOK), jnp.int32)
    col_doc = jnp.zeros((TOK, TOK), jnp.int32)
    for k in range(4):
        end = end + lens[d * 4 + k]
        row_doc = row_doc + jnp.where(rows >= end, 1, 0)
        col_doc = col_doc + jnp.where(cols >= end, 1, 0)
    allowed = (row_doc == col_doc) & (cols <= rows)
    for h in range(BLK // HEAD):
        at = slice(h * HEAD, (h + 1) * HEAD)
        scores = nt(queries[:, at], keys[:, at]) * (HEAD ** -0.5)
        scores = jnp.where(allowed, scores, -1e30)
        weights = jnp.exp(scores - jnp.max(scores, axis=-1, keepdims=True))
        total = jnp.sum(weights, axis=-1, keepdims=True)
        out[:, at] = (nn(weights.astype(bf16), values[:, at]) / total).astype(bf16)


def attend(tab, lens, queries, keys, values):
    spec = pl.BlockSpec((TOK, BLK), lambda i, *_: (0, i))
    return pl.pallas_call(
        attend_body,
        out_shape=jax.ShapeDtypeStruct(queries.shape, bf16),
        grid_spec=pltpu.PrefetchScalarGridSpec(
            num_scalar_prefetch=2, grid=(4,), in_specs=[spec] * 3, out_specs=spec
        ),
        cost_estimate=cost(0),
        compiler_params=params(12),
        name="attend",
    )(tab, lens, *(in_hbm(v) for v in (queries, keys, values)))


def low_body(tab, att, cot, mine, other, low_out, lg_out, down_t, up_t, keep, give):
    unit = eye(256)
    for f in range(32):
        at = tab[T_F + f]
        block = jnp.where(tab[T_C] == f % 2, mine[at], other[at])
        turned = nt(unit, jnp.concatenate([block, block], 0)).astype(bf16)
        down_t[f * DCOLS : (f + 1) * DCOLS, :] = turned[:DCOLS]
        up_t[f * COLS : (f + 1) * COLS, :] = turned[DCOLS : DCOLS + COLS]
    low = nn(att[...], down_t[...])
    low_grad = nn(cot[...], up_t[...]) * SCALE
    first = lax.broadcasted_iota(jnp.int32, (TOK, 128), 1) < 64
    none = jnp.zeros((TOK, 128), f32)
    low_a, low_b = (jnp.where(first, low, none).astype(bf16), jnp.where(first, none, low).astype(bf16))
    lg_a, lg_b = (
        jnp.where(first, low_grad, none).astype(bf16),
        jnp.where(first, none, low_grad).astype(bf16),
    )
    low_out[...] = low_a
    lg_out[...] = lg_a
    core = tab[T_C]

    def put(f, lo, hi, even, odd):
        place = tab[T_P + f]
        keep[place, lo:hi, :] = jnp.where(core == 0, even, odd)
        give[place, lo:hi, :] = jnp.where(core == 0, odd, even).astype(bf16)

    half = DCOLS // 2
    both = jnp.concatenate([lg_a, lg_b], 1)
    for i in range(4):
        got = tn(att[:, i * BLK : (i + 1) * BLK], both)
        a, b = got[:, :128], got[:, 128:]
        pair = []
        for k in range(8):
            s = k * DCOLS
            pair.append(a[s : s + half] + b[s + half : s + DCOLS])
        for k in range(0, 8, 2):
            put(i * 8 + k, 0, half, pair[k], pair[k + 1])
    both = jnp.concatenate([low_a, low_b], 1)
    for j in range(8):
        got = tn(cot[:, j * BLK : (j + 1) * BLK], both) * SCALE
        a, b = got[:, :128], got[:, 128:]
        pair = []
        for k in range(4):
            s = k * COLS
            pair.append(a[s : s + DCOLS] + b[s + DCOLS : s + COLS])
        for k in range(0, 4, 2):
            put(j * 4 + k, half, half + DCOLS, pair[k], pair[k + 1])


def low_terms(tab, att, cot, mine, other):
    vmem = pl.BlockSpec(memory_space=pltpu.VMEM)
    return pl.pallas_call(
        low_body,
        out_shape=(
            jax.ShapeDtypeStruct((TOK, 128), bf16),
            jax.ShapeDtypeStruct((TOK, 128), bf16),
            jax.ShapeDtypeStruct((32 * DCOLS, 128), bf16),
            jax.ShapeDtypeStruct((32 * COLS, 128), bf16),
            jax.ShapeDtypeStruct((16, 120, 128), f32),
            jax.ShapeDtypeStruct((16, 120, 128), bf16),
        ),
        in_specs=[pl.BlockSpec(memory_space=pltpu.SMEM), *([vmem] * 4)],
        out_specs=[vmem] * 6,
        cost_estimate=cost(0),
        compiler_params=params(16),
        name="low_terms",
    )(tab, att, cot, mine, other)


SLOTS = 4


def tiles_body(stage, counts, tab, att, cot, *refs):
    n_head = 4 if stage == 0 else 2
    head, refs = refs[:n_head], refs[n_head:]
    tiles, refs = refs[: len(counts)], refs[len(counts) :]
    places = [(a, k) for a, n in enumerate(counts) for k in range(n)]
    count = len(places)
    if stage == 3:
        out, grad, out_acc, grad_acc, out_old, grad_old, old_sems, *refs = refs
    elif stage == 2:
        out_new, grad_new, out_acc, grad_acc, new_sems, *refs = refs
    else:
        out_acc, grad_acc, *refs = refs
    buf, sems, *refs = refs

    def fetch(t):
        a, k = places[t]
        return pltpu.make_async_copy(tiles[a].at[k], buf.at[t % SLOTS], sems.at[t % SLOTS])

    for t in range(SLOTS):
        fetch(t).start()
    if stage == 2:
        out_acc[...] = head[0][...]
        grad_acc[...] = head[1][...]
    if stage == 3:
        olds = [
            pltpu.make_async_copy(head[k], ref, old_sems.at[k])
            for k, ref in enumerate((out_old, grad_old))
        ]
        for copy in olds:
            copy.start()
        out_acc[...] = jnp.zeros(out_acc.shape, f32)
        grad_acc[...] = jnp.zeros(grad_acc.shape, f32)
    if stage == 0:
        low_a, lg_a, down_t, up_t = head
        for j in range(8):
            out_acc[j] = nt(low_a[...], up_t[j * BLK : (j + 1) * BLK, :]) * SCALE
        for i in range(4):
            grad_acc[i] = nt(lg_a[...], down_t[i * BLK : (i + 1) * BLK, :])
    for t in range(count):
        j, i = tab[STAGE_AT[stage] + t], tab[STAGE_AT[stage] + count + t]
        fetch(t).wait()
        tile = buf[t % SLOTS]
        out_acc[j] = out_acc[j] + nt(att[:, pl.ds(pl.multiple_of(i * BLK, 128), BLK)], tile)
        grad_acc[i] = grad_acc[i] + nn(cot[:, pl.ds(pl.multiple_of(j * BLK, 128), BLK)], tile)
        if t + SLOTS < count:
            fetch(t + SLOTS).start()
    if stage == 2:
        news = [
            pltpu.make_async_copy(ref, (out_new, grad_new)[k], new_sems.at[k])
            for k, ref in enumerate((out_acc, grad_acc))
        ]
        for copy in news:
            copy.start()
        for copy in news:
            copy.wait()
    if stage == 3:
        out_v, grad_v, out_sems = refs
        for copy in olds:
            copy.wait()
        copies = []
        for acc, old, full, ref, base in (
            (out_acc, out_old, out_v, out, 0),
            (grad_acc, grad_old, grad_v, grad, 8),
        ):
            for k in range(acc.shape[0]):
                at = slice(k * BLK, (k + 1) * BLK)
                full[:, at] = (acc[k] + old[k]).astype(bf16)
                copies.append(pltpu.make_async_copy(full.at[:, at], ref.at[:, at], out_sems.at[base + k]))
                copies[-1].start()
        for copy in copies:
            copy.wait()


def add_tiles(stage, tab, att, cot, head, arrays):
    vmem = pl.BlockSpec(memory_space=pltpu.VMEM)
    hbm = pl.BlockSpec(memory_space=pltpu.HBM)
    acc = [(8, TOK, BLK), (4, TOK, BLK)]
    outs, specs = [jax.ShapeDtypeStruct(s, f32) for s in acc], [vmem, vmem]
    scratch = [pltpu.VMEM((SLOTS, BLK, BLK), bf16), pltpu.SemaphoreType.DMA((SLOTS,))]
    if stage == 3:
        wide = [(TOK, 8 * BLK), (TOK, 4 * BLK)]
        outs, specs = [jax.ShapeDtypeStruct(s, bf16) for s in wide], [hbm, hbm]
        scratch = [pltpu.VMEM(s, f32) for s in acc * 2] + [pltpu.SemaphoreType.DMA((2,))] + scratch
        scratch += [pltpu.VMEM(s, bf16) for s in wide] + [pltpu.SemaphoreType.DMA((12,))]
    if stage == 2:
        outs, specs = [pltpu.HBM(s, f32) for s in acc], [hbm, hbm]
        scratch = [pltpu.VMEM(s, f32) for s in acc] + [pltpu.SemaphoreType.DMA((2,))] + scratch
    if stage == 3:
        head = [in_hbm(h) for h in head]
    head_spec = hbm if stage == 3 else vmem
    return pl.pallas_call(
        lambda *refs: tiles_body(stage, [a.shape[0] for a in arrays], *refs),
        out_shape=outs,
        in_specs=[pl.BlockSpec(memory_space=pltpu.SMEM), vmem, vmem, *([head_spec] * len(head)), *([hbm] * len(arrays))],
        out_specs=specs,
        scratch_shapes=scratch,
        input_output_aliases={} if stage != 1 else {3: 0, 4: 1},
        cost_estimate=cost(8 if stage == 0 else 0),
        compiler_params=params(28 if stage == 3 else 16),
        name=f"tiles_{stage}",
    )(tab, att, cot, *head, *arrays)


def per_device(
    table,
    queries,
    keys,
    values,
    lengths,
    weight,
    codes,
    factor,
    offset,
    down,
    up,
    cot,
):
    tab = table.reshape(-1)
    lens = lengths.reshape(-1)

    tie = lax.optimization_barrier

    def along(value, axis, k):
        at = AX.index(axis)
        return send(value, lambda *to: tuple(v + (k if n == at else 0) for n, v in enumerate(to)))

    def scattered(part, axis, bit, n, kind):
        return part[:n] + flip(part[n:].astype(kind), axis, bit).astype(f32)

    quarter = base_quarter(tab, weight, codes, factor, offset)
    quarter, down, up = tie((quarter, down, up))
    adapters = jnp.concatenate([down, up, jnp.zeros((64, 16), bf16)], 1)
    adapters = jnp.stack([adapters, *(along(adapters, "zh", -k) for k in REL[1:])])
    quarter, queries = tie((quarter, queries))
    rounds = [z_round(quarter, k) for k in range(4)]
    rounds[0], adapters = tie((rounds[0], adapters))
    adapters = [adapters, *(along(adapters, "x", -k) for k in REL[1:])]
    rounds, adapters = tie((rounds, adapters))
    own = ordered(tab, rounds)

    less, more, far = middle(own, 1), middle(own, -1), middle(own, 2)
    own, queries = tie((own, queries))
    att = attend(tab, lens, queries, keys, values)
    mine = joined(adapters).reshape(16, 64, 256)
    low = low_terms(tab, att, cot, mine, sibling(mine))
    less, more, far, low = tie((less, more, far, tuple(low)))
    low_a, lg_a, down_t, up_t, keep, give = low
    row = joined([own, less, more, far])

    all_less, all_more = outer(row, 1), outer(row, -1)
    give, row = tie((give, row))
    part = keep + flip(give, "c", 1).astype(f32)
    kept, got = part[:8], flip(part[8:].astype(bf16), "zh", 1)
    sums = add_tiles(0, tab, att, cot, (low_a, lg_a, down_t, up_t), [row, sibling(row)])
    got, sums = tie((got, tuple(sums)))
    part = scattered(kept + got.astype(f32), "zh", 2, 4, bf16)
    part = part + flip(part, "zl", 1)
    all_less, all_more, part, sums = tie((all_less, all_more, part, sums))

    far_a, far_b = outer(all_less[:2], 1), outer(all_more[2:], -1)
    tiles = [all_less, all_more]
    sums = add_tiles(1, tab, att, cot, sums, tiles)
    part, sums = tie((part, tuple(sums)))
    a, b, c = (flip(part[k], "x", k) for k in (1, 2, 3))
    sums = add_tiles(2, tab, att, cot, sums, [sibling(t) for t in tiles])
    a, b, c, sums = tie((a, b, c, tuple(sums)))
    part = (part[0] + a) + (b + c)
    far_a, far_b, part, sums = tie((far_a, far_b, part, sums))
    tiles = [far_a, far_b]
    tiles_other = [sibling(t) for t in tiles]
    a, b, c = (flip(part, "y", k) for k in (1, 2, 3))
    part = (part + a) + (b + c)
    out, grad = add_tiles(3, tab, att, cot, sums, [*tiles, *tiles_other])
    half = DCOLS // 2
    down_grad = jnp.concatenate([part[:half, :64], part[:half, 64:]], 0).T
    up_grad = jnp.concatenate([part[half:, :64], part[half:, 64:]], 0).T
    return out, grad, down_grad, up_grad


def solution(mesh):
    fine = Mesh(np.asarray(mesh.devices).reshape(DIMS), AX)
    tokens, owners = ("y", "zl", "x", "zh", "c"), ("x", "zh", "c")
    table = device_table()
    mapped = jax.shard_map(
        per_device,
        mesh=fine,
        in_specs=(
            P(tokens, None),
            P(tokens, None),
            P(tokens, None),
            P(tokens, None),
            P(owners, None, None),
            P(None, owners),
            P(None, owners),
            P(None, owners),
            P(None, owners),
            P(None, owners),
            P(None, owners),
            P(tokens, None),
        ),
        out_specs=(
            P(tokens, None),
            P(tokens, None),
            P(None, owners),
            P(None, owners),
        ),
        check_vma=False,
    )
    return lambda *args: mapped(jnp.asarray(table), *args)
```
